128 devices in a mesh: pool: 2 (over x_lo), seq: 16 (over x_hi, y, core), head: 4 (over z).
Axes of the slice: x: 4 (x_hi: 2, x_lo: 2; x = x_hi * 2 + x_lo), y: 4, z: 4, core: 2. Of those that a mesh axis runs over, the one named last changes fastest.
Arguments:
- prompt: bfloat16 [8, 2048, 8192], P('pool', 'seq'), may hold values from -6 to 6
- key_value_weight: bfloat16 [8192, 2, 1024], P('seq', None, 'head'), may hold values from -0.0625 to 0.0625
- adapter_down_weight: bfloat16 [8192, 256], P('seq'), may hold values from -0.0625 to 0.0625
- adapter_up_weight: bfloat16 [8, 2, 16, 1024], P(None, None, None, 'head'), may hold values from -0.75 to 0.75
- request_adapter_index: int32 [8], P('pool'), may hold values from 0 to 7
- destination: int32 [8], replicated, may hold values from 0 to 15, as said below
- rotated_query: bfloat16 [1536, 8192], P(('pool', 'seq'), 'head'), may hold values from -150 to 150
- key_value_cache: bfloat16 [1536, 128, 2, 1024], P(('pool', 'seq'), None, None, 'head'), may hold values from -6 to 6
- current_key_value: bfloat16 [1536, 2, 1024], P(('pool', 'seq'), None, 'head'), may hold values from -6 to 6
- cached_length: int32 [1536], P(('pool', 'seq')), may hold values from 1 to 128
- row_adapter_index: int32 [1536], P('pool'), may hold values from 0 to 7
- output_weight: bfloat16 [8192, 8192], P('head', 'seq'), may hold values from -0.0625 to 0.0625
- output_down_weight: bfloat16 [8192, 8, 16], P('head'), may hold values from -0.0625 to 0.0625
- output_up_weight: bfloat16 [8, 16, 8192], P(None, None, 'seq'), may hold values from -3.59375 to 3.59375
Outputs:
- handed: bfloat16 [32, 2, 2048, 2, 1024], P(('pool', 'seq'), None, None, None, 'head')
- decoded: bfloat16 [1536, 8192], P(('pool', 'head'), 'seq')
The draws below stay inside these ranges and needn't reach their ends.
Inputs may be any that keep to these rules, and one draw needn't show every extreme that they name: `destination`: among one pool's 4 requests no decode owner is named more than 2 times, and some owner exactly 2 times; in each pool owners 0 and 15 both receive requests.
All inputs are finite; a program needn't handle non-finite values.
Results may differ from the reference program's by a relative error of at most 0.0085.
Values may be sent and summed in bfloat16 or wider, within the bound.
No kernel may reach another device: no remote copies, remote signals or barrier semaphores. Data moves between devices by JAX's collectives and lax.ppermute only.
A program may use at most 128 MiB of HBM per device.

```python
import jax
import jax.numpy as jnp
from jax import lax

MODEL_DIM = 8192
QUERY_HEADS = 64
KEY_HEADS = 8
HEAD_DIM = 128
ADAPTER_RANK = 16
ADAPTER_COUNT = 8
PROMPT = 2048
CAP = 2
REQ_POOL = 4
ROWS_DEV = 48
CONTEXT_SLOTS = 128
REQS = 8
DECODE_ROWS = 1536
DECODERS = 16
OWNERS = 32
N_POOL = 2
N_SEQ = 16


def cache_front(key):
    leading_part = jax.random.normal(jax.random.fold_in(key, 11), (DECODE_ROWS, 2, 2, KEY_HEADS * HEAD_DIM), jnp.float32)
    leading_part = jnp.clip(leading_part, -6.0, 6.0)
    return leading_part


def draw_key_value_cache(key, part):
    leading_part = cache_front(key)
    remaining_part = jax.random.normal(jax.random.fold_in(key, 12), (DECODE_ROWS, CONTEXT_SLOTS - 2, 2, KEY_HEADS * HEAD_DIM), jnp.float32)
    remaining_part = jnp.clip(remaining_part, -6.0, 6.0)
    whole = jnp.concatenate([leading_part, remaining_part], axis=1)
    return jnp.clip(whole, -6.0, 6.0).astype(jnp.bfloat16)


def draw_rotated_query(key, part):
    query_matrix = jax.random.normal(jax.random.fold_in(key, 21), (DECODE_ROWS, QUERY_HEADS * HEAD_DIM), jnp.float32)
    query_matrix = jnp.clip(query_matrix, -5.0, 5.0)
    return query_matrix.astype(jnp.bfloat16)


def draw_destination(key, part):
    halves = []
    for pool_index in range(N_POOL):
        sub_key = jax.random.fold_in(key, 100 + pool_index)
        ranks = jax.random.permutation(jax.random.fold_in(sub_key, 1), N_SEQ).astype(jnp.int32)
        coin = jax.random.randint(jax.random.fold_in(sub_key, 4), (), 0, 2).astype(jnp.int32)
        first_owner = coin * (N_SEQ - 1)
        second_owner = N_SEQ - 1 - first_owner
        ranks = ranks.at[first_owner].set(-2)
        ranks = ranks.at[second_owner].set(-1)
        owners = jnp.argsort(ranks, stable=True).astype(jnp.int32)
        counts = jax.random.randint(jax.random.fold_in(sub_key, 2), (N_SEQ,), 1, CAP + 1)
        counts = counts.at[0].set(CAP)
        listed = jnp.repeat(owners, counts, total_repeat_length=REQ_POOL)
        shuffle = jax.random.permutation(jax.random.fold_in(sub_key, 3), REQ_POOL)
        halves.append(listed[shuffle])
    return jnp.concatenate(halves).astype(jnp.int32)


def place_ends(values, key, smallest, top_value):
    index_at = [jax.random.randint(jax.random.fold_in(key, axis), (), 0, length) for axis, length in enumerate(values.shape)]
    widest = values.shape.index(max(values.shape))
    beside = index_at[:widest] + [(index_at[widest] + 1) % values.shape[widest]] + index_at[widest + 1:]
    return values.at[tuple(index_at)].set(smallest).at[tuple(beside)].set(top_value)


def level_of(rng, dims, pieces, low, largest):
    level = 1.0
    for dim, blocks in pieces:
        heights = jax.random.uniform(jax.random.fold_in(jax.random.fold_in(rng, 6), dim), (blocks,), jnp.float32, low / len(pieces), largest / len(pieces))
        level = level * jnp.repeat(jnp.exp(heights), dims[dim] // blocks).reshape((-1,) + (1,) * (len(dims) - 1 - dim))
    return level


def noise(stream_key, dims, scale, reach, cuts=(), kind=jnp.bfloat16):
    values = jax.random.normal(stream_key, dims, jnp.float32) * scale
    if len(cuts) > 0:
        values = level_of(stream_key, dims, cuts, -0.22, 0.18) * values
    return jnp.clip(values, min=-reach, max=reach).astype(kind)


def setup_inputs(seed: int = 0) -> dict:
    key_of = jax.random.split(jax.random.key(seed), 15)
    prompt = noise(key_of[0], (REQS, PROMPT, MODEL_DIM), 1.0, 6.0, ((0, 2), (1, 16)))
    key_value_weight = noise(key_of[1], (MODEL_DIM, 2, KEY_HEADS * HEAD_DIM), MODEL_DIM ** -0.5, 0.0625, ((0, 16), (2, 4)))
    adapter_down_weight = noise(key_of[2], (MODEL_DIM, ADAPTER_COUNT * 2 * ADAPTER_RANK), MODEL_DIM ** -0.5, 0.0625, ((0, 16),))
    adapter_up_weight = noise(key_of[3], (ADAPTER_COUNT, 2, ADAPTER_RANK, KEY_HEADS * HEAD_DIM), 0.125, 0.75, ((3, 4),))
    request_adapter_index = place_ends(jax.random.randint(key_of[4], (REQS,), 0, ADAPTER_COUNT), jax.random.fold_in(key_of[4], 1), 0, ADAPTER_COUNT - 1).astype(jnp.int32)
    destination = draw_destination(jax.random.fold_in(key_of[14], 71), 0)
    rotated_query = draw_rotated_query(jax.random.fold_in(key_of[14], 71), 0)
    key_value_cache = draw_key_value_cache(jax.random.fold_in(key_of[14], 71), 0)
    current_key_value = noise(key_of[8], (DECODE_ROWS, 2, KEY_HEADS * HEAD_DIM), 1.0, 6.0, ((0, 32), (2, 4)))
    cached_length = place_ends(jax.random.randint(key_of[9], (DECODE_ROWS,), 1, CONTEXT_SLOTS + 1), jax.random.fold_in(key_of[9], 1), 1, CONTEXT_SLOTS).astype(jnp.int32)
    row_adapter_index = place_ends(jax.random.randint(key_of[10], (DECODE_ROWS,), 0, ADAPTER_COUNT), jax.random.fold_in(key_of[10], 1), 0, ADAPTER_COUNT - 1).astype(jnp.int32)
    output_weight = noise(key_of[11], (QUERY_HEADS * HEAD_DIM, MODEL_DIM), (QUERY_HEADS * HEAD_DIM) ** -0.5, 0.0625, ((0, 4), (1, 16)))
    output_down_weight = noise(key_of[12], (QUERY_HEADS * HEAD_DIM, ADAPTER_COUNT, ADAPTER_RANK), (QUERY_HEADS * HEAD_DIM) ** -0.5, 0.0625, ((0, 4),))
    output_up_weight = noise(key_of[13], (ADAPTER_COUNT, ADAPTER_RANK, MODEL_DIM), 0.6, 3.59375, ((2, 16),))
    return {"prompt": prompt, "key_value_weight": key_value_weight, "adapter_down_weight": adapter_down_weight, "adapter_up_weight": adapter_up_weight, "request_adapter_index": request_adapter_index, "destination": destination, "rotated_query": rotated_query, "key_value_cache": key_value_cache, "current_key_value": current_key_value, "cached_length": cached_length, "row_adapter_index": row_adapter_index, "output_weight": output_weight, "output_down_weight": output_down_weight, "output_up_weight": output_up_weight}


def attend_rows(query_matrix, key_value_cache, prefill_state, lengths):
    decode_count = query_matrix.shape[0]
    query_groups = QUERY_HEADS // KEY_HEADS
    query_batch = query_matrix.astype(jnp.float32).reshape(decode_count, KEY_HEADS, query_groups, HEAD_DIM)
    key_matrix = key_value_cache[:, :, 0].astype(jnp.float32).reshape(decode_count, CONTEXT_SLOTS, KEY_HEADS, HEAD_DIM)
    value_matrix = key_value_cache[:, :, 1].astype(jnp.float32).reshape(decode_count, CONTEXT_SLOTS, KEY_HEADS, HEAD_DIM)
    prefill_key = prefill_state[:, 0].astype(jnp.float32).reshape(decode_count, KEY_HEADS, HEAD_DIM)
    prefill_value = prefill_state[:, 1].astype(jnp.float32).reshape(decode_count, KEY_HEADS, HEAD_DIM)
    factor = HEAD_DIM ** -0.5
    scores = jnp.einsum("rkgd,rckd->rkgc", query_batch, key_matrix) * factor
    own_score = jnp.einsum("rkgd,rkd->rkg", query_batch, prefill_key) * factor
    valid = (jnp.arange(CONTEXT_SLOTS, dtype=jnp.int32)[None, :] < lengths[:, None])[:, None, None, :]
    highest = jnp.maximum(jnp.max(jnp.where(valid, scores, -1e30), axis=-1), own_score)
    raw = jnp.where(valid, jnp.exp(scores - highest[..., None]), 0.0)
    own_raw = jnp.exp(own_score - highest)
    normer = jnp.sum(raw, axis=-1) + own_raw
    weights = lax.optimization_barrier((raw / normer[..., None]).astype(jnp.bfloat16)).astype(jnp.float32)
    own_weight = lax.optimization_barrier((own_raw / normer).astype(jnp.bfloat16)).astype(jnp.float32)
    mixed = jnp.einsum("rkgc,rckd->rkgd", weights, value_matrix)
    mixed = mixed + own_weight[..., None] * prefill_value[:, :, None, :]
    return mixed.reshape(decode_count, QUERY_HEADS * HEAD_DIM).astype(jnp.bfloat16)


def reference(prompt, key_value_weight, adapter_down_weight, adapter_up_weight, request_adapter_index, destination, rotated_query, key_value_cache, current_key_value, cached_length, row_adapter_index, output_weight, output_down_weight, output_up_weight):
    key_value_width = KEY_HEADS * HEAD_DIM
    token_matrix = prompt.reshape(REQS * PROMPT, MODEL_DIM)
    base_kv = jnp.dot(token_matrix, key_value_weight.reshape(MODEL_DIM, 2 * key_value_width), preferred_element_type=jnp.float32)
    reduced_everything = jnp.dot(token_matrix, adapter_down_weight, preferred_element_type=jnp.float32)
    reduced_everything = reduced_everything.reshape(REQS, PROMPT, ADAPTER_COUNT, 2, ADAPTER_RANK)
    adapter_selector = request_adapter_index[:, None] == jnp.arange(ADAPTER_COUNT, dtype=jnp.int32)[None, :]
    low_rank = jnp.sum(jnp.where(adapter_selector[:, None, :, None, None], reduced_everything, 0.0), axis=2)
    selected_up_weight = adapter_up_weight.astype(jnp.float32)[request_adapter_index]
    correction = jnp.einsum("rtkq,rkqf->rtkf", low_rank, selected_up_weight, precision=lax.Precision.HIGHEST)
    prefilled = (base_kv.reshape(REQS, PROMPT, 2, key_value_width) + correction).astype(jnp.bfloat16)

    owners = destination.reshape(N_POOL, REQ_POOL)
    order_index = jnp.arange(REQ_POOL, dtype=jnp.int32)
    earlier = (owners[:, :, None] == owners[:, None, :]) & (order_index[None, None, :] < order_index[None, :, None])
    slot_of = jnp.sum(earlier.astype(jnp.int32), axis=2).astype(jnp.int32)
    target_pool = (jnp.arange(N_POOL, dtype=jnp.int32) + 1) % N_POOL
    target = (target_pool[:, None] * DECODERS + owners).reshape(REQS).astype(jnp.int32)
    handed = jnp.zeros((OWNERS, CAP, PROMPT, 2, key_value_width), jnp.bfloat16)
    handed = handed.at[target, slot_of.reshape(REQS)].set(prefilled)

    blocks = DECODE_ROWS // ROWS_DEV

    def one_block(operands):
        return attend_rows(operands[0], operands[1], operands[2], operands[3])

    attended = lax.map(one_block, (rotated_query.reshape(blocks, ROWS_DEV, QUERY_HEADS * HEAD_DIM), key_value_cache.reshape(blocks, ROWS_DEV, CONTEXT_SLOTS, 2, key_value_width), current_key_value.reshape(blocks, ROWS_DEV, 2, key_value_width), cached_length.reshape(blocks, ROWS_DEV)))
    attended = attended.reshape(DECODE_ROWS, QUERY_HEADS * HEAD_DIM)
    low_rows = jnp.dot(attended, output_down_weight.reshape(QUERY_HEADS * HEAD_DIM, ADAPTER_COUNT * ADAPTER_RANK), preferred_element_type=jnp.float32)
    keep = row_adapter_index[:, None] == (jnp.arange(ADAPTER_COUNT * ADAPTER_RANK, dtype=jnp.int32) // ADAPTER_RANK)[None, :]
    low_rows = jnp.where(keep, low_rows, 0.0)
    decoded = jnp.dot(attended, output_weight, preferred_element_type=jnp.float32)
    decoded = decoded + jnp.dot(low_rows, output_up_weight.reshape(ADAPTER_COUNT * ADAPTER_RANK, MODEL_DIM).astype(jnp.float32), precision=lax.Precision.HIGHEST)
    return handed, decoded.astype(jnp.bfloat16)
```

```python
import jax
import jax.numpy as jnp
from jax import lax
from jax.experimental import pallas as pl
from jax.experimental.pallas import tpu as pltpu
from jax.sharding import Mesh
from jax.sharding import PartitionSpec as P

HEAD_DIM = 128
RANK = 16
ADAPTERS = 8
CAP = 2
REQ_POOL = 4
X_SLOTS = 3
MIB = 2**20


def params(limit=48):
    return pltpu.CompilerParams(vmem_limit_bytes=limit * MIB)


def x_shift(value, k):
    pairs = []
    for x in range(4):
        t = (x + k) % 4
        pairs.append(((x % 2) * 2 + x // 2, (t % 2) * 2 + t // 2))
    return lax.ppermute(value, ("pool", "xh"), pairs)


def y_shift(value, k):
    return lax.ppermute(value, "y", [(i, (i + k) % 4) for i in range(4)])


def core_swap(value):
    return lax.ppermute(value, "core", [(0, 1), (1, 0)])


def pack_kernel(meta, adapter, w_ref, d_ref, k_ref, v_ref, t_ref):
    k_ref[...] = w_ref[:, 0, :]
    v_ref[...] = w_ref[:, 1, :]
    column = lax.broadcasted_iota(jnp.int32, (256, 128), 0)
    lane = lax.broadcasted_iota(jnp.int32, (256, 128), 1)
    wanted = jnp.zeros((256, 128), jnp.int32)
    for r in range(REQ_POOL):
        wanted = jnp.where((lane >> 5) == r, adapter[r] * 32 + (lane & 31), wanted)
    pick = (column == wanted).astype(jnp.bfloat16)
    t_ref[...] = lax.dot_general(
        pick, d_ref[...], (((0,), (1,)), ((), ())), preferred_element_type=jnp.float32
    ).astype(jnp.bfloat16)


def pack(meta, adapter, weight, down):
    rows, half = weight.shape[0], weight.shape[0] // 2
    bf = jnp.bfloat16
    return pl.pallas_call(
        pack_kernel,
        grid_spec=pltpu.PrefetchScalarGridSpec(
            num_scalar_prefetch=2,
            grid=(1,),
            in_specs=[
                pl.BlockSpec((half, 2, 256), lambda i, m, a: (m[0], 0, 0)),
                pl.BlockSpec((rows, 256), lambda i, m, a: (0, 0)),
            ],
            out_specs=[
                pl.BlockSpec((half, 256), lambda i, m, a: (0, 0)),
                pl.BlockSpec((half, 256), lambda i, m, a: (0, 0)),
                pl.BlockSpec((128, rows), lambda i, m, a: (0, 0)),
            ],
        ),
        out_shape=[
            jax.ShapeDtypeStruct((half, 256), bf),
            jax.ShapeDtypeStruct((half, 256), bf),
            jax.ShapeDtypeStruct((128, rows), bf),
        ],
        compiler_params=params(),
        name="pack",
    )(meta, adapter, weight, down)


ROWS_STEP = 8


def attend_kernel(len_ref, q_ref, kv_ref, cur_ref, o_ref):
    first = pl.program_id(0) * ROWS_STEP
    factor = HEAD_DIM**-0.5
    lane = lax.broadcasted_iota(jnp.int32, (8, 256), 1)
    is_key = (lane & 1) == 0
    scores, own = [], []
    for i in range(ROWS_STEP):
        n = len_ref[first + i]
        valid = is_key & (lane < 2 * n)
        for h in range(2):
            both = kv_ref[i, :, :, h * 128 : (h + 1) * 128].reshape(256, 128)
            q = q_ref[i, h * 8 : (h + 1) * 8, :]
            s = lax.dot_general(
                q, both, (((1,), (1,)), ((), ())), preferred_element_type=jnp.float32
            )
            scores.append(jnp.where(valid, s * factor, -1e30))
            k = cur_ref[i, 0:1, h * 128 : (h + 1) * 128].astype(jnp.float32)
            own.append(jnp.sum(q.astype(jnp.float32) * k, axis=-1, keepdims=True) * factor)
    s = jnp.concatenate(scores, 0)
    o = jnp.concatenate(own, 0)
    highest = jnp.maximum(jnp.max(s, axis=-1, keepdims=True), o)
    raw = jnp.exp(s - highest)
    own_raw = jnp.exp(o - highest)
    norm = jnp.sum(raw, axis=-1, keepdims=True) + own_raw
    weights = pltpu.roll(raw / norm, 1, 1).astype(jnp.bfloat16)
    own_weight = (own_raw / norm).astype(jnp.bfloat16).astype(jnp.float32)
    for i in range(ROWS_STEP):
        for h in range(2):
            both = kv_ref[i, :, :, h * 128 : (h + 1) * 128].reshape(256, 128)
            j = (i * 2 + h) * 8
            v = cur_ref[i, 1:2, h * 128 : (h + 1) * 128].astype(jnp.float32)
            mixed = jnp.dot(weights[j : j + 8], both, preferred_element_type=jnp.float32)
            mixed = mixed + own_weight[j : j + 8] * v
            o_ref[i, h * 8 : (h + 1) * 8, :] = mixed.astype(jnp.bfloat16)


def attend(query, cache, current, lengths):
    rows = query.shape[0]
    heads = query.shape[1] // HEAD_DIM
    out = pl.pallas_call(
        attend_kernel,
        grid_spec=pltpu.PrefetchScalarGridSpec(
            num_scalar_prefetch=1,
            grid=(rows // ROWS_STEP,),
            in_specs=[
                pl.BlockSpec((ROWS_STEP, heads, 128), lambda g, n: (g, 0, 0)),
                pl.BlockSpec((ROWS_STEP, 128, 2, 256), lambda g, n: (g, 0, 0, 0)),
                pl.BlockSpec((ROWS_STEP, 2, 256), lambda g, n: (g, 0, 0)),
            ],
            out_specs=pl.BlockSpec((ROWS_STEP, heads, 128), lambda g, n: (g, 0, 0)),
        ),
        out_shape=jax.ShapeDtypeStruct((rows, heads, 128), jnp.bfloat16),
        compiler_params=params(),
        name="attend",
    )(lengths, query.reshape(rows, heads, 128), cache, current)
    return out.reshape(rows, heads * 128)


def split_dot(low, up):
    high = low.astype(jnp.bfloat16)
    rest = (low - high.astype(jnp.float32)).astype(jnp.bfloat16)
    return jnp.dot(high, up, preferred_element_type=jnp.float32) + jnp.dot(
        rest, up, preferred_element_type=jnp.float32
    )


def x_order(x):
    return [x, (x + 3) & 3, (x + 2) & 3, (x + 1) & 3]


def prefill_kernel(meta, adapter, dest, *refs):
    n_blocks = 16
    prompt, down, up = refs[0:3]
    blocks = refs[3 : 3 + n_blocks]
    near_ref, far_ref = refs[3 + n_blocks : 5 + n_blocks]
    p_buf, d_buf, u_buf, w_buf, res, sems, osem = refs[5 + n_blocks :]
    pool, xh, y, core = meta[0], meta[1], meta[2], meta[3]
    x = 2 * xh + pool
    copies = [
        pltpu.make_async_copy(prompt, p_buf, sems.at[16]),
        pltpu.make_async_copy(down, d_buf, sems.at[17]),
        pltpu.make_async_copy(up, u_buf, sems.at[18]),
    ]
    wcopies = [pltpu.make_async_copy(blocks[b], w_buf.at[b], sems.at[b]) for b in range(n_blocks)]
    copies[0].start()
    for c in wcopies:
        c.start()
    copies[1].start()
    copies[2].start()
    copies[0].wait()
    acc = [None, None]
    for b in range(n_blocks):
        wcopies[b].wait()
        kv = (b // 4) % 2
        c_of = core if b < 8 else 1 - core
        j = b % 4
        for i in range(4):
            xi = x_order(x)[i if kv == 0 else j]
            yi = x_order(y)[j if kv == 0 else i]
            shard = (xi >> 1) * 8 + yi * 2 + c_of
            at = pl.multiple_of(shard * 512 + (xi & 1) * 256, 256)
            part = jnp.dot(
                p_buf[:, pl.ds(at, 256)],
                w_buf[b, i * 256 : (i + 1) * 256, :],
                preferred_element_type=jnp.float32,
            )
            acc[kv] = part if acc[kv] is None else acc[kv] + part
    copies[1].wait()
    copies[2].wait()
    outs = []
    for r in range(REQ_POOL):
        rows = slice(r * 128, (r + 1) * 128)
        low = None
        for s in range(16):
            part = lax.dot_general(
                p_buf[rows, s * 512 : (s + 1) * 512],
                d_buf[s * 128 + r * 32 : s * 128 + (r + 1) * 32, :],
                (((1,), (1,)), ((), ())),
                preferred_element_type=jnp.float32,
            )
            low = part if low is None else low + part
        a = adapter[r]
        both = []
        for kv in range(2):
            value = acc[kv][rows] + split_dot(low[:, kv * 16 : (kv + 1) * 16], u_buf[a, kv])
            both.append(value.astype(jnp.bfloat16))
        res[r] = jnp.stack(both, axis=1)
    base = pool * REQ_POOL
    sides = [dest[base + r] >> 3 for r in range(REQ_POOL)]
    for r in range(REQ_POOL):
        slot = jnp.int32(0)
        for q in range(r):
            slot = slot + (sides[q] == sides[r]).astype(jnp.int32)

        @pl.when(sides[r] == xh)
        def _():
            pltpu.make_async_copy(res.at[r], near_ref.at[slot], osem.at[r]).start()

        @pl.when(sides[r] != xh)
        def _():
            pltpu.make_async_copy(res.at[r], far_ref.at[slot], osem.at[r]).start()

    for r in range(REQ_POOL):
        pltpu.make_async_copy(res.at[r], near_ref.at[0], osem.at[r]).wait()


def prefill(meta, adapter, dest, prompt, down, up, blocks):
    bf = jnp.bfloat16
    tokens, width = prompt.shape
    any_spec = pl.BlockSpec(memory_space=pl.ANY)
    shape = jax.ShapeDtypeStruct((X_SLOTS, 128, 2, 256), bf)
    return pl.pallas_call(
        prefill_kernel,
        grid_spec=pltpu.PrefetchScalarGridSpec(
            num_scalar_prefetch=3,
            grid=(1,),
            in_specs=[any_spec] * (3 + len(blocks)),
            out_specs=[any_spec, any_spec],
            scratch_shapes=[
                pltpu.VMEM((tokens, width), bf),
                pltpu.VMEM(down.shape, bf),
                pltpu.VMEM(up.shape, bf),
                pltpu.VMEM((len(blocks),) + blocks[0].shape, bf),
                pltpu.VMEM((REQ_POOL, 128, 2, 256), bf),
                pltpu.SemaphoreType.DMA((19,)),
                pltpu.SemaphoreType.DMA((REQ_POOL,)),
            ],
        ),
        out_shape=[shape, shape],
        compiler_params=params(56),
        name="prefill",
    )(meta, adapter, dest, prompt, down, up, *blocks)


def choose_kernel(meta, dest, *refs):
    ins, out, sems = refs[:8], refs[8], refs[9]
    pool, xh, y, core = meta[0], meta[1], meta[2], meta[3]
    index = slots_of(dest, 1 - pool, xh, xh * 8 + y * 2 + (1 - core))[0]
    copies = []
    for j in range(CAP):
        for b in range(8):
            copies.append(
                pltpu.make_async_copy(ins[b].at[index[j]], out.at[j, b], sems.at[j * 8 + b])
            )
    for c in copies:
        c.start()
    for c in copies:
        c.wait()


def slots_of(dest, pool, xh, owner):
    owners = [dest[pool * REQ_POOL + r] for r in range(REQ_POOL)]
    index = [jnp.int32(0)] * CAP
    used = [jnp.int32(0)] * CAP
    place, mine = jnp.int32(0), jnp.int32(0)
    for r in range(REQ_POOL):
        hit = (owners[r] == owner).astype(jnp.int32)
        for j in range(CAP):
            here = hit * (mine == j).astype(jnp.int32)
            index[j] = index[j] + here * place
            used[j] = used[j] + here
        mine = mine + hit
        place = place + ((owners[r] >> 3) == xh).astype(jnp.int32)
    return index, used


def choose(meta, dest, parts):
    any_spec = pl.BlockSpec(memory_space=pl.ANY)
    return pl.pallas_call(
        choose_kernel,
        grid_spec=pltpu.PrefetchScalarGridSpec(
            num_scalar_prefetch=2,
            grid=(1,),
            in_specs=[any_spec] * 8,
            out_specs=any_spec,
            scratch_shapes=[pltpu.SemaphoreType.DMA((16,))],
        ),
        out_shape=jax.ShapeDtypeStruct((CAP, 8, 128, 2, 256), jnp.bfloat16),
        compiler_params=params(),
        name="choose",
    )(meta, dest, *parts)


def place_kernel(meta, dest, *refs):
    ins, other, out, zero, sems = refs[:8], refs[8], refs[9], refs[10], refs[11]
    pool, xh, y, core = meta[0], meta[1], meta[2], meta[3]
    zero[...] = jnp.zeros_like(zero)
    index, used = slots_of(dest, 1 - pool, xh, xh * 8 + y * 2 + core)
    for j in range(CAP):
        for b in range(8):
            side = xh if b < 4 else 1 - xh
            row = x_order(y)[b % 4]
            mine = pl.multiple_of((side * 8 + row * 2 + core) * 128, 128)
            theirs = pl.multiple_of((side * 8 + row * 2 + (1 - core)) * 128, 128)

            @pl.when(used[j] == 1)
            def _():
                pltpu.make_async_copy(
                    ins[b].at[index[j]], out.at[0, j, pl.ds(mine, 128)], sems.at[j * 16 + b]
                ).start()
                pltpu.make_async_copy(
                    other.at[j, b], out.at[0, j, pl.ds(theirs, 128)], sems.at[j * 16 + 8 + b]
                ).start()

            @pl.when(used[j] == 0)
            def _():
                pltpu.make_async_copy(
                    zero, out.at[0, j, pl.ds(mine, 128)], sems.at[j * 16 + b]
                ).start()
                pltpu.make_async_copy(
                    zero, out.at[0, j, pl.ds(theirs, 128)], sems.at[j * 16 + 8 + b]
                ).start()

    for j in range(CAP):
        for b in range(16):
            pltpu.make_async_copy(zero, out.at[0, j, pl.ds(0, 128)], sems.at[j * 16 + b]).wait()


def place(meta, dest, parts, other):
    any_spec = pl.BlockSpec(memory_space=pl.ANY)
    return pl.pallas_call(
        place_kernel,
        grid_spec=pltpu.PrefetchScalarGridSpec(
            num_scalar_prefetch=2,
            grid=(1,),
            in_specs=[any_spec] * 9,
            out_specs=any_spec,
            scratch_shapes=[
                pltpu.VMEM((128, 2, 256), jnp.bfloat16),
                pltpu.SemaphoreType.DMA((32,)),
            ],
        ),
        out_shape=jax.ShapeDtypeStruct((1, CAP, 2048, 2, 256), jnp.bfloat16),
        compiler_params=params(),
        name="place",
    )(meta, dest, *parts, other)


def project_kernel(meta, keep_ref, down_ref, up_ref, w_ref, *refs):
    ins, out_ref, rows, sems = refs[:8], refs[8], refs[9], refs[10]
    xh, y, core = meta[1], meta[2], meta[3]
    copies = []
    for b in range(8):
        row = x_order(y)[b % 4]
        c_of = core if b < 4 else 1 - core
        for i in range(2):
            side = xh if i == 0 else 1 - xh
            at = pl.multiple_of((side * 8 + row * 2 + c_of) * 48, 16)
            copies.append(
                pltpu.make_async_copy(
                    ins[b].at[pl.ds(i * 48, 48)], rows.at[pl.ds(at, 48)], sems.at[b * 2 + i]
                )
            )
    for c in copies:
        c.start()
    for c in copies:
        c.wait()
    value = rows[...]
    low = lax.dot_general(
        value, down_ref[...], (((1,), (1,)), ((), ())), preferred_element_type=jnp.float32
    )
    owner = lax.broadcasted_iota(jnp.int32, low.shape, 1) >> 4
    low = jnp.where(keep_ref[...] == owner, low, 0.0)
    out = jnp.dot(value, w_ref[...], preferred_element_type=jnp.float32)
    out_ref[...] = (out + split_dot(low, up_ref[...])).astype(jnp.bfloat16)


def project(meta, keep, down, up, weight, parts):
    any_spec = pl.BlockSpec(memory_space=pl.ANY)
    rows = 768

    def whole(shape):
        return pl.BlockSpec(shape, lambda i, m: (0,) * len(shape))

    return pl.pallas_call(
        project_kernel,
        grid_spec=pltpu.PrefetchScalarGridSpec(
            num_scalar_prefetch=1,
            grid=(1,),
            in_specs=[
                whole(keep.shape),
                whole(down.shape),
                whole(up.shape),
                whole(weight.shape),
            ]
            + [any_spec] * 8,
            out_specs=whole((rows, weight.shape[1])),
            scratch_shapes=[
                pltpu.VMEM((rows, weight.shape[0]), jnp.bfloat16),
                pltpu.SemaphoreType.DMA((16,)),
            ],
        ),
        out_shape=jax.ShapeDtypeStruct((rows, weight.shape[1]), jnp.bfloat16),
        compiler_params=params(),
        name="project",
    )(meta, keep, down, up, weight, *parts)


def ring(value, shift):
    return [value, shift(value, 1), shift(value, 2), shift(value, -1)]


def body(
    prompt,
    key_value_weight,
    adapter_down_weight,
    adapter_up_weight,
    request_adapter_index,
    destination,
    rotated_query,
    key_value_cache,
    current_key_value,
    cached_length,
    row_adapter_index,
    output_weight,
    output_down_weight,
    output_up_weight,
):
    meta = jnp.stack([lax.axis_index(a) for a in ("pool", "xh", "y", "core")]).astype(jnp.int32)
    keys, values, low_down = pack(
        meta, request_adapter_index, key_value_weight, adapter_down_weight
    )
    all_down = lax.all_gather(low_down, ("xh", "y", "core"), axis=0, tiled=True)
    key_rows = jnp.concatenate(ring(keys, x_shift), 0)
    value_rows = jnp.concatenate(ring(values, y_shift), 0)
    near = ring(key_rows, y_shift) + ring(value_rows, x_shift)
    blocks = near + [core_swap(b) for b in near]

    attended = attend(rotated_query, key_value_cache, current_key_value, cached_length)
    across = lax.ppermute(attended, "xh", [(0, 1), (1, 0)])
    mine = ring(jnp.concatenate([attended, across], 0), y_shift)
    parts = mine + [core_swap(b) for b in mine]
    ranks = ADAPTERS * RANK
    down = jnp.transpose(output_down_weight, (1, 2, 0)).reshape(ranks, -1)
    up = output_up_weight.reshape(ranks, -1)
    partial = project(meta, row_adapter_index[:, None], down, up, output_weight, parts)
    shares = lax.all_to_all(partial, "head", split_axis=0, concat_axis=0, tiled=True)
    shares = shares.reshape(4, -1, partial.shape[1]).astype(jnp.float32)
    decoded = (shares[0] + shares[1] + shares[2] + shares[3]).astype(jnp.bfloat16)

    tokens = prompt.reshape(-1, prompt.shape[2])
    same, other = prefill(
        meta, request_adapter_index, destination, tokens, all_down, adapter_up_weight, blocks
    )
    b0 = lax.ppermute(same, "pool", [(0, 1), (1, 0)])
    a0 = lax.ppermute(other, ("pool", "xh"), [(i, 3 - i) for i in range(4)])
    b1, b3 = y_shift(b0, 1), y_shift(b0, -1)
    a1, a3 = y_shift(a0, 1), y_shift(a0, -1)
    b2, a2 = y_shift(b1, 1), y_shift(a3, -1)
    held = [b0, b1, b2, b3, a0, a1, a2, a3]
    theirs = core_swap(choose(meta, destination, held))
    handed = place(meta, destination, held, theirs)
    return handed, decoded


def solution(mesh):
    fine = Mesh(mesh.devices.reshape(2, 2, 4, 2, 4), ("pool", "xh", "y", "core", "head"))
    seq = ("xh", "y", "core")
    every = ("pool",) + seq
    in_specs = (
        P("pool", seq, None),
        P(seq, None, "head"),
        P(seq, None),
        P(None, None, None, "head"),
        P("pool"),
        P(),
        P(every, "head"),
        P(every, None, None, "head"),
        P(every, None, "head"),
        P(every),
        P("pool"),
        P("head", seq),
        P("head", None, None),
        P(None, None, seq),
    )
    out_specs = (P(every, None, None, None, "head"), P(("pool", "head"), seq))
    return jax.shard_map(body, mesh=fine, in_specs=in_specs, out_specs=out_specs, check_vma=False)
```

```python
import jax
import jax.numpy as jnp
from jax import lax
from jax.experimental import pallas as pl
from jax.experimental.pallas import tpu as pltpu
from jax.sharding import Mesh
from jax.sharding import PartitionSpec as P

HEAD_DIM = 128
RANK = 16
ADAPTERS = 8
CAP = 2
REQ_POOL = 4
X_SLOTS = 3
MIB = 2**20


def params(limit=48):
    return pltpu.CompilerParams(vmem_limit_bytes=limit * MIB)


def x_shift(value, k):
    pairs = []
    for x in range(4):
        t = (x + k) % 4
        pairs.append(((x % 2) * 2 + x // 2, (t % 2) * 2 + t // 2))
    return lax.ppermute(value, ("pool", "xh"), pairs)


def y_shift(value, k):
    return lax.ppermute(value, "y", [(i, (i + k) % 4) for i in range(4)])


def xh_swap(value):
    return lax.ppermute(value, "xh", [(0, 1), (1, 0)])


def z_shift(value, k):
    return lax.ppermute(value, "head", [(i, (i + k) % 4) for i in range(4)])


def core_swap(value):
    return lax.ppermute(value, "core", [(0, 1), (1, 0)])


def pack_kernel(meta, adapter, w_ref, d_ref, k_ref, v_ref, t_ref):
    k_ref[...] = w_ref[:, 0, :]
    v_ref[...] = w_ref[:, 1, :]
    column = lax.broadcasted_iota(jnp.int32, (256, 128), 0)
    lane = lax.broadcasted_iota(jnp.int32, (256, 128), 1)
    pick = (column == adapter[meta[4]] * 32 + lane) & (lane < 32)
    low = lax.dot_general(
        pick.astype(jnp.bfloat16),
        d_ref[...],
        (((0,), (1,)), ((), ())),
        preferred_element_type=jnp.float32,
    ).astype(jnp.bfloat16)
    t_ref[0:32] = low[0:32, 0:256]
    t_ref[32:64] = low[0:32, 256:512]


def pack(meta, adapter, weight, down):
    rows, half = weight.shape[0], weight.shape[0] // 2

    def shape(n):
        return jax.ShapeDtypeStruct((n, 256), jnp.bfloat16)

    def spec(n):
        return pl.BlockSpec((n, 256), lambda i, m, a: (0, 0))

    return pl.pallas_call(
        pack_kernel,
        grid_spec=pltpu.PrefetchScalarGridSpec(
            num_scalar_prefetch=2,
            grid=(1,),
            in_specs=[
                pl.BlockSpec((half, 2, 256), lambda i, m, a: (m[0], 0, 0)),
                pl.BlockSpec((rows, 256), lambda i, m, a: (0, 0)),
            ],
            out_specs=[spec(half), spec(half), spec(64)],
        ),
        out_shape=[shape(half), shape(half), shape(64)],
        compiler_params=params(),
        name="pack",
    )(meta, adapter, weight, down)


ROWS_STEP = 8


def attend_kernel(len_ref, q_ref, kv_ref, cur_ref, o_ref):
    first = pl.program_id(0) * ROWS_STEP
    factor = HEAD_DIM**-0.5
    lane = lax.broadcasted_iota(jnp.int32, (8, 256), 1)
    is_key = (lane & 1) == 0
    scores, own = [], []
    for i in range(ROWS_STEP):
        n = len_ref[first + i]
        valid = is_key & (lane < 2 * n)
        for h in range(2):
            both = kv_ref[i, :, :, h * 128 : (h + 1) * 128].reshape(256, 128)
            q = q_ref[i, h * 8 : (h + 1) * 8, :]
            s = lax.dot_general(
                q, both, (((1,), (1,)), ((), ())), preferred_element_type=jnp.float32
            )
            scores.append(jnp.where(valid, s * factor, -1e30))
            k = cur_ref[i, 0:1, h * 128 : (h + 1) * 128].astype(jnp.float32)
            own.append(jnp.sum(q.astype(jnp.float32) * k, axis=-1, keepdims=True) * factor)
    s = jnp.concatenate(scores, 0)
    o = jnp.concatenate(own, 0)
    highest = jnp.maximum(jnp.max(s, axis=-1, keepdims=True), o)
    raw = jnp.exp(s - highest)
    own_raw = jnp.exp(o - highest)
    norm = jnp.sum(raw, axis=-1, keepdims=True) + own_raw
    weights = pltpu.roll(raw / norm, 1, 1).astype(jnp.bfloat16)
    own_weight = (own_raw / norm).astype(jnp.bfloat16).astype(jnp.float32)
    for i in range(ROWS_STEP):
        for h in range(2):
            both = kv_ref[i, :, :, h * 128 : (h + 1) * 128].reshape(256, 128)
            j = (i * 2 + h) * 8
            v = cur_ref[i, 1:2, h * 128 : (h + 1) * 128].astype(jnp.float32)
            mixed = jnp.dot(weights[j : j + 8], both, preferred_element_type=jnp.float32)
            mixed = mixed + own_weight[j : j + 8] * v
            o_ref[i, h * 8 : (h + 1) * 8, :] = mixed.astype(jnp.bfloat16)


def attend(query, cache, current, lengths):
    rows = query.shape[0]
    heads = query.shape[1] // HEAD_DIM
    out = pl.pallas_call(
        attend_kernel,
        grid_spec=pltpu.PrefetchScalarGridSpec(
            num_scalar_prefetch=1,
            grid=(rows // ROWS_STEP,),
            in_specs=[
                pl.BlockSpec((ROWS_STEP, heads, 128), lambda g, n: (g, 0, 0)),
                pl.BlockSpec((ROWS_STEP, 128, 2, 256), lambda g, n: (g, 0, 0, 0)),
                pl.BlockSpec((ROWS_STEP, 2, 256), lambda g, n: (g, 0, 0)),
            ],
            out_specs=pl.BlockSpec((ROWS_STEP, heads, 128), lambda g, n: (g, 0, 0)),
        ),
        out_shape=jax.ShapeDtypeStruct((rows, heads, 128), jnp.bfloat16),
        compiler_params=params(),
        name="attend",
    )(lengths, query.reshape(rows, heads, 128), cache, current)
    return out.reshape(rows, heads * 128)


def split_dot(low, up, dims=(((1,), (0,)), ((), ()))):
    high = low.astype(jnp.bfloat16)
    rest = (low - high.astype(jnp.float32)).astype(jnp.bfloat16)
    return lax.dot_general(high, up, dims, preferred_element_type=jnp.float32) + lax.dot_general(
        rest, up, dims, preferred_element_type=jnp.float32
    )


def x_order(x):
    return [x, (x + 3) & 3, (x + 2) & 3, (x + 1) & 3]


def chunk_start(xi, yi, core):
    return pl.multiple_of(((xi >> 1) * 8 + yi * 2 + core) * 512 + (xi & 1) * 256, 256)


def low_kernel(meta, *refs):
    prompt, blocks, out_ref = refs[0], refs[1:9], refs[9]
    p_buf, d_buf, sems = refs[10:]
    xh, y, core, z = meta[1], meta[2], meta[3], meta[4]
    first = pltpu.make_async_copy(prompt.at[z], p_buf, sems.at[8])
    first.start()
    copies = [
        pltpu.make_async_copy(blocks[n].at[pl.ds(1024, 128)], d_buf.at[n], sems.at[n])
        for n in range(8)
    ]
    for c in copies:
        c.start()
    first.wait()
    low = jnp.zeros((32, 128), jnp.float32)
    for n in range(8):
        copies[n].wait()
        c_of = core if n < 4 else 1 - core
        tokens = []
        for i in range(4):
            side = xh if i < 2 else 1 - xh
            shard = side * 8 + x_order(y)[n % 4] * 2 + c_of
            at = pl.multiple_of(shard * 512 + (i % 2) * 256, 256)
            tokens.append(p_buf[:, pl.ds(at, 256)])
        low = low + lax.dot_general(
            jnp.concatenate([d_buf[n, i * 32 : (i + 1) * 32] for i in range(4)], 1),
            jnp.concatenate(tokens, 1),
            (((1,), (1,)), ((), ())),
            preferred_element_type=jnp.float32,
        )
    out_ref[...] = low


def low_rank(meta, prompt, blocks):
    bf = jnp.bfloat16
    any_spec = pl.BlockSpec(memory_space=pl.ANY)
    return pl.pallas_call(
        low_kernel,
        grid_spec=pltpu.PrefetchScalarGridSpec(
            num_scalar_prefetch=1,
            grid=(1,),
            in_specs=[any_spec] * 9,
            out_specs=pl.BlockSpec((32, 128), lambda i, m: (0, 0)),
            scratch_shapes=[
                pltpu.VMEM(prompt.shape[1:], bf),
                pltpu.VMEM((8, 128, 256), bf),
                pltpu.SemaphoreType.DMA((9,)),
            ],
        ),
        out_shape=jax.ShapeDtypeStruct((32, 128), jnp.float32),
        compiler_params=params(),
        name="low_rank",
    )(meta, prompt, *blocks)


def main_kernel(meta, *refs):
    prompt, blocks, k_ref, v_ref = refs[0], refs[1:17], refs[17], refs[18]
    p_buf, w_buf, sems = refs[19:]
    pool, xh, y, core = meta[0], meta[1], meta[2], meta[3]
    x = 2 * xh + pool
    first = pltpu.make_async_copy(prompt, p_buf, sems.at[16])
    first.start()
    copies = [
        pltpu.make_async_copy(blocks[b].at[pl.ds(0, 1024)], w_buf.at[b], sems.at[b])
        for b in range(16)
    ]
    for c in copies:
        c.start()
    first.wait()
    for b in range(16):
        copies[b].wait()
        kv = (b // 4) % 2
        c_of = core if b < 8 else 1 - core
        j = b % 4
        tokens = []
        for i in range(4):
            xi = x_order(x)[i if kv == 0 else j]
            yi = x_order(y)[j if kv == 0 else i]
            tokens.append(p_buf[:, pl.ds(chunk_start(xi, yi, c_of), 256)])
        part = jnp.dot(
            jnp.concatenate(tokens, 1),
            w_buf[b],
            preferred_element_type=jnp.float32,
        )
        out_ref = v_ref if kv else k_ref
        if b == 4 * kv:
            out_ref[...] = part
        else:
            out_ref[...] += part


def main_product(meta, tokens, blocks):
    bf = jnp.bfloat16
    any_spec = pl.BlockSpec(memory_space=pl.ANY)
    shape = jax.ShapeDtypeStruct((tokens.shape[0], 256), jnp.float32)
    return pl.pallas_call(
        main_kernel,
        grid_spec=pltpu.PrefetchScalarGridSpec(
            num_scalar_prefetch=1,
            grid=(1,),
            in_specs=[any_spec] * 17,
            out_specs=[pl.BlockSpec(shape.shape, lambda i, m: (0, 0))] * 2,
            scratch_shapes=[
                pltpu.VMEM(tokens.shape, bf),
                pltpu.VMEM((16, 1024, 256), bf),
                pltpu.SemaphoreType.DMA((17,)),
            ],
        ),
        out_shape=[shape, shape],
        compiler_params=params(56),
        name="main_product",
    )(meta, tokens, *blocks)


def finish_kernel(meta, adapter, dest, *refs):
    lows, k_ref, v_ref, up_ref = refs[0:4], refs[4], refs[5], refs[6]
    near_ref, far_ref, res, sems = refs[7:]
    pool, xh, z = meta[0], meta[1], meta[4]
    owners = [dest[pool * REQ_POOL + r] for r in range(REQ_POOL)]
    dims = (((0,), (0,)), ((), ()))
    for n in range(REQ_POOL):
        r = x_order(z)[n]
        a = adapter[r]
        rows = pl.ds(pl.multiple_of(r * 128, 128), 128)
        low = lows[n][...]
        both = []
        for kv, ref in enumerate((k_ref, v_ref)):
            value = ref[rows, :] + split_dot(low[kv * 16 : (kv + 1) * 16], up_ref[a, kv], dims)
            both.append(value.astype(jnp.bfloat16))
        res[n] = jnp.stack(both, axis=1)
        owner = dest[pool * REQ_POOL + r]
        slot = jnp.int32(0)
        for q in range(REQ_POOL):
            slot = slot + (((owners[q] >> 3) == (owner >> 3)) & (q < r)).astype(jnp.int32)

        @pl.when((owner >> 3) == xh)
        def _():
            pltpu.make_async_copy(res.at[n], near_ref.at[slot], sems.at[n]).start()

        @pl.when((owner >> 3) != xh)
        def _():
            pltpu.make_async_copy(res.at[n], far_ref.at[slot], sems.at[n]).start()

    for n in range(REQ_POOL):
        pltpu.make_async_copy(res.at[n], near_ref.at[0], sems.at[n]).wait()


def finish(meta, adapters, dest, lows, keys, values, up):
    bf = jnp.bfloat16
    any_spec = pl.BlockSpec(memory_space=pl.ANY)
    shape = jax.ShapeDtypeStruct((X_SLOTS, 128, 2, 256), bf)

    def whole(a):
        return pl.BlockSpec(a.shape, lambda i, m, b, d: (0,) * a.ndim)

    ins = [*lows, keys, values, up]
    return pl.pallas_call(
        finish_kernel,
        grid_spec=pltpu.PrefetchScalarGridSpec(
            num_scalar_prefetch=3,
            grid=(1,),
            in_specs=[whole(a) for a in ins],
            out_specs=[any_spec, any_spec],
            scratch_shapes=[
                pltpu.VMEM((REQ_POOL, 128, 2, 256), bf),
                pltpu.SemaphoreType.DMA((REQ_POOL,)),
            ],
        ),
        out_shape=[shape, shape],
        compiler_params=params(56),
        name="finish",
    )(meta, adapters, dest, *ins)


def choose_kernel(meta, dest, *refs):
    ins, out, sems = refs[:8], refs[8], refs[9]
    pool, xh, y, core = meta[0], meta[1], meta[2], meta[3]
    index = slots_of(dest, 1 - pool, xh, xh * 8 + y * 2 + (1 - core))[0]
    copies = []
    for j in range(CAP):
        for b in range(8):
            copies.append(
                pltpu.make_async_copy(ins[b].at[index[j]], out.at[j, b], sems.at[j * 8 + b])
            )
    for c in copies:
        c.start()
    for c in copies:
        c.wait()


def slots_of(dest, pool, xh, owner):
    owners = [dest[pool * REQ_POOL + r] for r in range(REQ_POOL)]
    index = [jnp.int32(0)] * CAP
    used = [jnp.int32(0)] * CAP
    place, mine = jnp.int32(0), jnp.int32(0)
    for r in range(REQ_POOL):
        hit = (owners[r] == owner).astype(jnp.int32)
        for j in range(CAP):
            here = hit * (mine == j).astype(jnp.int32)
            index[j] = index[j] + here * place
            used[j] = used[j] + here
        mine = mine + hit
        place = place + ((owners[r] >> 3) == xh).astype(jnp.int32)
    return index, used


def choose(meta, dest, parts):
    any_spec = pl.BlockSpec(memory_space=pl.ANY)
    return pl.pallas_call(
        choose_kernel,
        grid_spec=pltpu.PrefetchScalarGridSpec(
            num_scalar_prefetch=2,
            grid=(1,),
            in_specs=[any_spec] * 8,
            out_specs=any_spec,
            scratch_shapes=[pltpu.SemaphoreType.DMA((16,))],
        ),
        out_shape=jax.ShapeDtypeStruct((CAP, 8, 128, 2, 256), jnp.bfloat16),
        compiler_params=params(),
        name="choose",
    )(meta, dest, *parts)


def place_kernel(meta, dest, *refs):
    ins, other, out, zero, sems = refs[:8], refs[8], refs[9], refs[10], refs[11]
    pool, xh, y, core = meta[0], meta[1], meta[2], meta[3]
    zero[...] = jnp.zeros_like(zero)
    index, used = slots_of(dest, 1 - pool, xh, xh * 8 + y * 2 + core)
    for j in range(CAP):
        for b in range(8):
            side = xh if b < 4 else 1 - xh
            row = x_order(y)[b % 4]
            mine = pl.multiple_of((side * 8 + row * 2 + core) * 128, 128)
            theirs = pl.multiple_of((side * 8 + row * 2 + (1 - core)) * 128, 128)

            @pl.when(used[j] == 1)
            def _():
                pltpu.make_async_copy(
                    ins[b].at[index[j]], out.at[0, j, pl.ds(mine, 128)], sems.at[j * 16 + b]
                ).start()
                pltpu.make_async_copy(
                    other.at[j, b], out.at[0, j, pl.ds(theirs, 128)], sems.at[j * 16 + 8 + b]
                ).start()

            @pl.when(used[j] == 0)
            def _():
                pltpu.make_async_copy(
                    zero, out.at[0, j, pl.ds(mine, 128)], sems.at[j * 16 + b]
                ).start()
                pltpu.make_async_copy(
                    zero, out.at[0, j, pl.ds(theirs, 128)], sems.at[j * 16 + 8 + b]
                ).start()

    for j in range(CAP):
        for b in range(16):
            pltpu.make_async_copy(zero, out.at[0, j, pl.ds(0, 128)], sems.at[j * 16 + b]).wait()


def place(meta, dest, parts, other):
    any_spec = pl.BlockSpec(memory_space=pl.ANY)
    return pl.pallas_call(
        place_kernel,
        grid_spec=pltpu.PrefetchScalarGridSpec(
            num_scalar_prefetch=2,
            grid=(1,),
            in_specs=[any_spec] * 9,
            out_specs=any_spec,
            scratch_shapes=[
                pltpu.VMEM((128, 2, 256), jnp.bfloat16),
                pltpu.SemaphoreType.DMA((32,)),
            ],
        ),
        out_shape=jax.ShapeDtypeStruct((1, CAP, 2048, 2, 256), jnp.bfloat16),
        compiler_params=params(),
        name="place",
    )(meta, dest, *parts, other)


def project_kernel(meta, keep_ref, down_ref, up_ref, w_ref, *refs):
    ins, outs, rows, sems = refs[:8], refs[8:12], refs[12], refs[13]
    xh, y, core, z = meta[1], meta[2], meta[3], meta[4]
    copies = []
    for b in range(8):
        row = x_order(y)[b % 4]
        c_of = core if b < 4 else 1 - core
        for i in range(2):
            side = xh if i == 0 else 1 - xh
            at = pl.multiple_of((side * 8 + row * 2 + c_of) * 48, 16)
            copies.append(
                pltpu.make_async_copy(
                    ins[b].at[pl.ds(i * 48, 48)], rows.at[pl.ds(at, 48)], sems.at[b * 2 + i]
                )
            )
    for c in copies:
        c.start()
    for c in copies:
        c.wait()
    for n in range(4):
        at = pl.ds(pl.multiple_of(((z + n) & 3) * 192, 64), 192)
        value = rows[at, :]
        low = lax.dot_general(
            value, down_ref[...], (((1,), (1,)), ((), ())), preferred_element_type=jnp.float32
        )
        owner = lax.broadcasted_iota(jnp.int32, low.shape, 1) >> 4
        low = jnp.where(keep_ref[at, :] == owner, low, 0.0)
        out = jnp.dot(value, w_ref[...], preferred_element_type=jnp.float32)
        outs[n][...] = (out + split_dot(low, up_ref[...])).astype(jnp.bfloat16)


def project(meta, keep, down, up, weight, parts):
    any_spec = pl.BlockSpec(memory_space=pl.ANY)
    rows = 768

    def whole(shape):
        return pl.BlockSpec(shape, lambda i, m: (0,) * len(shape))

    return pl.pallas_call(
        project_kernel,
        grid_spec=pltpu.PrefetchScalarGridSpec(
            num_scalar_prefetch=1,
            grid=(1,),
            in_specs=[
                whole(keep.shape),
                whole(down.shape),
                whole(up.shape),
                whole(weight.shape),
            ]
            + [any_spec] * 8,
            out_specs=[whole((rows // 4, weight.shape[1]))] * 4,
            scratch_shapes=[
                pltpu.VMEM((rows, weight.shape[0]), jnp.bfloat16),
                pltpu.SemaphoreType.DMA((16,)),
            ],
        ),
        out_shape=[jax.ShapeDtypeStruct((rows // 4, weight.shape[1]), jnp.bfloat16)] * 4,
        compiler_params=params(),
        name="project",
    )(meta, keep, down, up, weight, *parts)


def ring(value, shift):
    return [value, shift(value, 1), shift(value, 2), shift(value, -1)]


def body(
    prompt,
    key_value_weight,
    adapter_down_weight,
    adapter_up_weight,
    request_adapter_index,
    destination,
    rotated_query,
    key_value_cache,
    current_key_value,
    cached_length,
    row_adapter_index,
    output_weight,
    output_down_weight,
    output_up_weight,
):
    axes = ("pool", "xh", "y", "core", "head")
    meta = jnp.stack([lax.axis_index(a) for a in axes]).astype(jnp.int32)
    keys, values, low_down = pack(
        meta, request_adapter_index, key_value_weight, adapter_down_weight
    )
    key_ring = ring(keys, x_shift)
    value_ring = ring(values, y_shift)
    attended = attend(rotated_query, key_value_cache, current_key_value, cached_length)
    key_rows, value_rows, attended = lax.optimization_barrier(
        (
            jnp.concatenate(key_ring + [low_down, xh_swap(low_down)], 0),
            jnp.concatenate(value_ring, 0),
            attended,
        )
    )
    near = ring(key_rows, y_shift) + ring(value_rows, x_shift)
    across = xh_swap(attended)
    blocks = near + [core_swap(b) for b in near]

    blocks, across = lax.optimization_barrier((blocks, across))
    pair = jnp.concatenate([attended, across], 0)
    low = low_rank(meta, prompt, blocks[0:4] + blocks[8:12])
    lows = ring(low, z_shift)
    mine = ring(pair, y_shift)
    tokens = prompt.reshape(-1, prompt.shape[2])
    base_keys, base_values = main_product(meta, tokens, blocks)
    base_keys, base_values, mine[1], mine[3] = lax.optimization_barrier(
        (base_keys, base_values, mine[1], mine[3])
    )
    same, other = finish(
        meta, request_adapter_index, destination, lows, base_keys, base_values, adapter_up_weight
    )
    b0 = lax.ppermute(same, "pool", [(0, 1), (1, 0)])
    a0 = lax.ppermute(other, ("pool", "xh"), [(i, 3 - i) for i in range(4)])
    b0, a0, mine[2] = lax.optimization_barrier((b0, a0, mine[2]))
    b1, b3 = y_shift(b0, 1), y_shift(b0, -1)
    a1, a3 = y_shift(a0, 1), y_shift(a0, -1)

    parts = mine + [core_swap(b) for b in mine]
    ranks = ADAPTERS * RANK
    down = jnp.transpose(output_down_weight, (1, 2, 0)).reshape(ranks, -1)
    up = output_up_weight.reshape(ranks, -1)
    shares = project(meta, row_adapter_index[:, None], down, up, output_weight, parts)
    b1, b3, a1, a3, shares = lax.optimization_barrier((b1, b3, a1, a3, shares))
    b2, a2 = y_shift(b1, 1), y_shift(a3, -1)
    decoded = shares[0].astype(jnp.float32)
    for k, share in ((1, shares[1]), (2, shares[2]), (-1, shares[3])):
        decoded = decoded + z_shift(share, k).astype(jnp.float32)
    decoded = decoded.astype(jnp.bfloat16)

    held = [b0, b1, b2, b3, a0, a1, a2, a3]
    held, decoded = lax.optimization_barrier((held, decoded))
    theirs = core_swap(choose(meta, destination, held))
    handed = place(meta, destination, held, theirs)
    return handed, decoded


def solution(mesh):
    fine = Mesh(mesh.devices.reshape(2, 2, 4, 2, 4), ("pool", "xh", "y", "core", "head"))
    seq = ("xh", "y", "core")
    every = ("pool",) + seq
    in_specs = (
        P("pool", seq, None),
        P(seq, None, "head"),
        P(seq, None),
        P(None, None, None, "head"),
        P("pool"),
        P(),
        P(every, "head"),
        P(every, None, None, "head"),
        P(every, None, "head"),
        P(every),
        P("pool"),
        P("head", seq),
        P("head", None, None),
        P(None, None, seq),
    )
    out_specs = (P(every, None, None, None, "head"), P(("pool", "head"), seq))
    return jax.shard_map(body, mesh=fine, in_specs=in_specs, out_specs=out_specs, check_vma=False)
```

```python
import functools

import jax
import jax.numpy as jnp
from jax import lax
from jax.experimental import pallas as pl
from jax.experimental.pallas import tpu as pltpu
from jax.sharding import Mesh
from jax.sharding import PartitionSpec as P

HEAD_DIM = 128
RANK = 16
ADAPTERS = 8
CAP = 2
REQ_POOL = 4
X_SLOTS = 3
MIB = 2**20


POOL, XH, Y, CORE, HEAD, DEST, ADAPTER = 0, 1, 2, 3, 4, 5, 13
VMEM = pl.BlockSpec(memory_space=pltpu.VMEM)
SMEM = pl.BlockSpec(memory_space=pltpu.SMEM)
ANY = pl.BlockSpec(memory_space=pl.ANY)


def params(limit=48):
    return pltpu.CompilerParams(vmem_limit_bytes=limit * MIB)


def x_shift(value, k):
    pairs = []
    for x in range(4):
        t = (x + k) % 4
        pairs.append(((x % 2) * 2 + x // 2, (t % 2) * 2 + t // 2))
    return lax.ppermute(value, ("pool", "xh"), pairs)


def y_shift(value, k):
    return lax.ppermute(value, "y", [(i, (i + k) % 4) for i in range(4)])


def xh_swap(value):
    return lax.ppermute(value, "xh", [(0, 1), (1, 0)])


def z_shift(value, k):
    return lax.ppermute(value, "head", [(i, (i + k) % 4) for i in range(4)])


def core_swap(value):
    return lax.ppermute(value, "core", [(0, 1), (1, 0)])


def pack_kernel(info, w_ref, d_ref, k_ref, v_ref):
    half = pl.ds(pl.multiple_of(info[POOL] * 256, 256), 256)
    k_ref[...] = w_ref[half, 0, :]
    v_ref[0:256] = w_ref[half, 1, :]
    column = lax.broadcasted_iota(jnp.int32, (256, 128), 0)
    lane = lax.broadcasted_iota(jnp.int32, (256, 128), 1)
    pick = (column == info[ADAPTER + info[HEAD]] * 32 + lane) & (lane < 32)
    low = lax.dot_general(
        pick.astype(jnp.bfloat16),
        d_ref[...],
        (((0,), (1,)), ((), ())),
        preferred_element_type=jnp.float32,
    ).astype(jnp.bfloat16)
    v_ref[256:288] = low[0:32, 0:256]
    v_ref[288:320] = low[0:32, 256:512]


def pack(info, weight, down):
    return pl.pallas_call(
        pack_kernel,
        in_specs=[SMEM, VMEM, VMEM],
        out_specs=[VMEM, VMEM],
        out_shape=[
            jax.ShapeDtypeStruct((256, 256), jnp.bfloat16),
            jax.ShapeDtypeStruct((320, 256), jnp.bfloat16),
        ],
        compiler_params=params(),
        name="pack",
    )(info, weight, down)


ROWS_STEP = 8


def attend_kernel(offset, len_ref, q_ref, kv_ref, cur_ref, o_ref):
    first = pl.program_id(0) * ROWS_STEP + offset
    factor = HEAD_DIM**-0.5
    lane = lax.broadcasted_iota(jnp.int32, (8, 256), 1)
    is_key = (lane & 1) == 0
    scores, own = [], []
    for i in range(ROWS_STEP):
        n = len_ref[first + i]
        valid = is_key & (lane < 2 * n)
        for h in range(2):
            both = kv_ref[i, :, :, h * 128 : (h + 1) * 128].reshape(256, 128)
            q = q_ref[i, h * 8 : (h + 1) * 8, :]
            s = lax.dot_general(
                q, both, (((1,), (1,)), ((), ())), preferred_element_type=jnp.float32
            )
            scores.append(jnp.where(valid, s * factor, -1e30))
            k = cur_ref[i, 0:1, h * 128 : (h + 1) * 128].astype(jnp.float32)
            own.append(jnp.sum(q.astype(jnp.float32) * k, axis=-1, keepdims=True) * factor)
    s = jnp.concatenate(scores, 0)
    o = jnp.concatenate(own, 0)
    highest = jnp.maximum(jnp.max(s, axis=-1, keepdims=True), o)
    raw = jnp.exp(s - highest)
    own_raw = jnp.exp(o - highest)
    norm = jnp.sum(raw, axis=-1, keepdims=True) + own_raw
    weights = pltpu.roll(raw / norm, 1, 1).astype(jnp.bfloat16)
    own_weight = (own_raw / norm).astype(jnp.bfloat16).astype(jnp.float32)
    for i in range(ROWS_STEP):
        for h in range(2):
            both = kv_ref[i, :, :, h * 128 : (h + 1) * 128].reshape(256, 128)
            j = (i * 2 + h) * 8
            v = cur_ref[i, 1:2, h * 128 : (h + 1) * 128].astype(jnp.float32)
            mixed = jnp.dot(weights[j : j + 8], both, preferred_element_type=jnp.float32)
            mixed = mixed + own_weight[j : j + 8] * v
            o_ref[i, h * 8 : (h + 1) * 8, :] = mixed.astype(jnp.bfloat16)


def attend(query, cache, current, lengths, part, parts):
    rows, heads = query.shape[0] // parts, query.shape[1]
    first = part * (rows // ROWS_STEP)
    return pl.pallas_call(
        functools.partial(attend_kernel, first * ROWS_STEP),
        grid_spec=pltpu.PrefetchScalarGridSpec(
            num_scalar_prefetch=1,
            grid=(rows // ROWS_STEP,),
            in_specs=[
                pl.BlockSpec((ROWS_STEP, heads, 128), lambda g, n: (g + first, 0, 0)),
                pl.BlockSpec((ROWS_STEP, 128, 2, 256), lambda g, n: (g + first, 0, 0, 0)),
                pl.BlockSpec((ROWS_STEP, 2, 256), lambda g, n: (g + first, 0, 0)),
            ],
            out_specs=pl.BlockSpec((ROWS_STEP, heads, 128), lambda g, n: (g, 0, 0)),
        ),
        out_shape=jax.ShapeDtypeStruct((rows, heads, 128), jnp.bfloat16),
        compiler_params=params(),
        name="attend",
    )(lengths, query, cache, current)


def split_dot(low, up, dims=(((1,), (0,)), ((), ()))):
    high = low.astype(jnp.bfloat16)
    rest = (low - high.astype(jnp.float32)).astype(jnp.bfloat16)
    return lax.dot_general(high, up, dims, preferred_element_type=jnp.float32) + lax.dot_general(
        rest, up, dims, preferred_element_type=jnp.float32
    )


def x_order(x):
    return [x, (x + 3) & 3, (x + 2) & 3, (x + 1) & 3]


def chunk_start(xi, yi, core):
    return pl.multiple_of(((xi >> 1) * 8 + yi * 2 + core) * 512 + (xi & 1) * 256, 256)


def low_kernel(info, prompt, own_ref, other_ref, out_ref):
    xh, y, core = info[XH], info[Y], info[CORE]
    rows = pl.ds(pl.multiple_of(info[HEAD] * 128, 128), 128)
    low = jnp.zeros((32, 128), jnp.float32)
    for n in range(2):
        ref, c_of = ((own_ref, core), (other_ref, 1 - core))[n]
        downs, tokens = [], []
        for i in range(16):
            side = xh if i < 8 else 1 - xh
            shard = side * 8 + x_order(y)[(i // 2) % 4] * 2 + c_of
            at = pl.multiple_of(shard * 512 + (i % 2) * 256, 256)
            tokens.append(prompt[rows, pl.ds(at, 256)])
            downs.append(ref[i * 32 : (i + 1) * 32])
        low = low + lax.dot_general(
            jnp.concatenate(downs, 1),
            jnp.concatenate(tokens, 1),
            (((1,), (1,)), ((), ())),
            preferred_element_type=jnp.float32,
        )
    out_ref[...] = low


def low_rank(info, tokens, own, other):
    return pl.pallas_call(
        low_kernel,
        in_specs=[SMEM, VMEM, VMEM, VMEM],
        out_specs=VMEM,
        out_shape=jax.ShapeDtypeStruct((32, 128), jnp.float32),
        compiler_params=params(),
        name="low_rank",
    )(info, tokens, own, other)


def main_kernel(kinds, fresh, info, prompt, *refs):
    n = len(kinds)
    blocks, sums, outs = refs[:n], refs[n:-2], refs[-2:]
    pool, xh, y, core = info[POOL], info[XH], info[Y], info[CORE]
    x = 2 * xh + pool
    done = [fresh, fresh]
    for (kv, j, partner), ref in zip(kinds, blocks):
        c_of = 1 - core if partner else core
        tokens = []
        for i in range(4):
            xi = x_order(x)[i if kv == 0 else j]
            yi = x_order(y)[j if kv == 0 else i]
            tokens.append(prompt[:, pl.ds(chunk_start(xi, yi, c_of), 256)])
        part = jnp.dot(
            jnp.concatenate(tokens, 1), ref[...], preferred_element_type=jnp.float32
        )
        if done[kv] is True:
            outs[kv][...] = part
        elif done[kv] is False:
            outs[kv][...] = sums[kv][...] + part
        else:
            outs[kv][...] += part
        done[kv] = None


def main_product(info, tokens, kinds, blocks, sums=()):
    shape = jax.ShapeDtypeStruct((tokens.shape[0], 256), jnp.float32)
    return pl.pallas_call(
        functools.partial(main_kernel, kinds, not sums),
        in_specs=[SMEM] + [VMEM] * (1 + len(blocks) + len(sums)),
        out_specs=[VMEM, VMEM],
        out_shape=[shape, shape],
        compiler_params=params(),
        name="main_product",
    )(info, tokens, *blocks, *sums)


def finish_kernel(info, *refs):
    lows, k_ref, v_ref, up_ref, near_ref, far_ref = refs[0:4], *refs[4:]
    pool, xh, z = info[POOL], info[XH], info[HEAD]
    owners = [info[DEST + pool * REQ_POOL + r] for r in range(REQ_POOL)]
    dims = (((0,), (0,)), ((), ()))
    for n in range(REQ_POOL):
        r = x_order(z)[n]
        a = info[ADAPTER + r]
        rows = pl.ds(pl.multiple_of(r * 128, 128), 128)
        low = lows[n][...]
        both = []
        for kv, ref in enumerate((k_ref, v_ref)):
            value = ref[rows, :] + split_dot(low[kv * 16 : (kv + 1) * 16], up_ref[a, kv], dims)
            both.append(value.astype(jnp.bfloat16))
        result = jnp.stack(both, axis=1)
        owner = info[DEST + pool * REQ_POOL + r]
        slot = jnp.int32(0)
        for q in range(REQ_POOL):
            slot = slot + (((owners[q] >> 3) == (owner >> 3)) & (q < r)).astype(jnp.int32)

        @pl.when((owner >> 3) == xh)
        def _():
            near_ref[slot] = result

        @pl.when((owner >> 3) != xh)
        def _():
            far_ref[slot] = result


def finish(info, lows, sums, up):
    shape = jax.ShapeDtypeStruct((X_SLOTS, 128, 2, 256), jnp.bfloat16)
    return pl.pallas_call(
        finish_kernel,
        in_specs=[SMEM] + [VMEM] * 7,
        out_specs=[VMEM, VMEM],
        out_shape=[shape, shape],
        compiler_params=params(),
        name="finish",
    )(info, *lows, *sums, up)


def slots_of(info, pool, xh, owner):
    owners = [info[DEST + pool * REQ_POOL + r] for r in range(REQ_POOL)]
    index = [jnp.int32(0)] * CAP
    used = [jnp.int32(0)] * CAP
    place, mine = jnp.int32(0), jnp.int32(0)
    for r in range(REQ_POOL):
        hit = (owners[r] == owner).astype(jnp.int32)
        for j in range(CAP):
            here = hit * (mine == j).astype(jnp.int32)
            index[j] = index[j] + here * place
            used[j] = used[j] + here
        mine = mine + hit
        place = place + ((owners[r] >> 3) == xh).astype(jnp.int32)
    return index, used


def choose_kernel(info, *refs):
    ins, out, sems = refs[:-2], refs[-2], refs[-1]
    xh = info[XH]
    owner = xh * 8 + info[Y] * 2 + (1 - info[CORE])
    index = slots_of(info, 1 - info[POOL], xh, owner)[0]
    n = len(ins)
    copies = [
        pltpu.make_async_copy(ins[b].at[index[j]], out.at[j, b], sems.at[j * n + b])
        for j in range(CAP)
        for b in range(n)
    ]
    for c in copies:
        c.start()
    for c in copies:
        c.wait()


def choose(info, parts):
    n = len(parts)
    return pl.pallas_call(
        choose_kernel,
        in_specs=[SMEM] + [VMEM] * n,
        out_specs=VMEM,
        out_shape=jax.ShapeDtypeStruct((CAP, n, 128, 2, 256), jnp.bfloat16),
        scratch_shapes=[pltpu.SemaphoreType.DMA((CAP * n,))],
        compiler_params=params(),
        name="choose",
    )(info, *parts)


def place_kernel(kinds, rest, info, *refs):
    n = len(kinds)
    ins, others = refs[:n], refs[n]
    out, zero, sems = refs[-3], refs[-2], refs[-1]
    xh, y, core = info[XH], info[Y], info[CORE]
    index, used = slots_of(info, 1 - info[POOL], xh, xh * 8 + y * 2 + core)
    if rest:
        zero[...] = jnp.zeros_like(zero)

    def spot(j, kind, c_of):
        side = xh if kind[0] == 0 else 1 - xh
        at = (side * 8 + x_order(y)[kind[1]] * 2 + c_of) * 128
        return out.at[0, j, pl.ds(pl.multiple_of(at, 128), 128)]

    def transfers(j):
        full = []
        for b, kind in enumerate(kinds):
            full.append((ins[b].at[index[j]], spot(j, kind, core)))
            full.append((others.at[j, b], spot(j, kind, 1 - core)))
        return [
            pltpu.make_async_copy(src, dst, sems.at[j, i]) for i, (src, dst) in enumerate(full)
        ]

    def clears(j):
        spots = [spot(j, kind, c) for kind in kinds + rest for c in (core, 1 - core)]
        return [pltpu.make_async_copy(zero, dst, sems.at[j, i]) for i, dst in enumerate(spots)]

    for step in ("start", "wait"):
        for j in range(CAP):

            @pl.when(used[j] == 1)
            def _():
                for c in transfers(j):
                    getattr(c, step)()

            if rest:

                @pl.when(used[j] == 0)
                def _():
                    for c in clears(j):
                        getattr(c, step)()


def place(info, kinds, rest, parts, others, out=None):
    shape = jax.ShapeDtypeStruct((1, CAP, 2048, 2, 256), jnp.bfloat16)
    ins = [info, *parts, others] + ([] if out is None else [out])
    return pl.pallas_call(
        functools.partial(place_kernel, kinds, rest),
        in_specs=[SMEM] + [VMEM] * (len(parts) + 1) + ([] if out is None else [ANY]),
        out_specs=ANY,
        out_shape=shape,
        scratch_shapes=[
            pltpu.VMEM((128, 2, 256), jnp.bfloat16),
            pltpu.SemaphoreType.DMA((CAP, 16)),
        ],
        input_output_aliases={} if out is None else {len(ins) - 1: 0},
        compiler_params=params(),
        name="place",
    )(*ins)


def project_kernel(info, keep, down, up, w_ref, *refs):
    ins, outs, res = refs[:8], refs[8:12], refs[12]
    xh, y, core, z = info[XH], info[Y], info[CORE], info[HEAD]
    value = jnp.concatenate([ref[...] for ref in ins], 0)
    out = jnp.dot(value, w_ref[...], preferred_element_type=jnp.float32)
    low = lax.dot_general(
        value, down[...], (((1,), (1,)), ((), ())), preferred_element_type=jnp.float32
    )
    owner = lax.broadcasted_iota(jnp.int32, (48, ADAPTERS * RANK), 1) >> 4
    spots, lows = [], []
    for b in range(8):
        row, c_of = x_order(y)[b % 4], core if b < 4 else 1 - core
        for i in range(2):
            side = xh if i == 0 else 1 - xh
            at = pl.ds(pl.multiple_of((side * 8 + row * 2 + c_of) * 48, 16), 48)
            n = b * 96 + i * 48
            spots.append(at)
            lows.append(jnp.where(keep[at, :] == owner, low[n : n + 48], 0.0))
    out = (out + split_dot(jnp.concatenate(lows, 0), up[...])).astype(jnp.bfloat16)
    for n in range(16):
        res[spots[n], :] = out[n * 48 : (n + 1) * 48]
    for n in range(4):
        outs[n][...] = res[pl.ds(pl.multiple_of(((z + n) & 3) * 192, 64), 192), :]


def project(info, keep, down, up, weight, parts):
    rows, width = 768, weight.shape[1]
    return pl.pallas_call(
        project_kernel,
        in_specs=[SMEM] + [VMEM] * 12,
        out_specs=[VMEM] * 4,
        out_shape=[jax.ShapeDtypeStruct((rows // 4, width), jnp.bfloat16)] * 4,
        scratch_shapes=[pltpu.VMEM((rows, width), jnp.bfloat16)],
        compiler_params=params(),
        name="project",
    )(info, keep, down, up, weight, *parts)


def ring(value, shift):
    return [value, shift(value, 1), shift(value, 2), shift(value, -1)]


def body(
    prompt,
    key_value_weight,
    adapter_down_weight,
    adapter_up_weight,
    request_adapter_index,
    destination,
    rotated_query,
    key_value_cache,
    current_key_value,
    cached_length,
    row_adapter_index,
    output_weight,
    output_down_weight,
    output_up_weight,
):
    barrier = lax.optimization_barrier
    axes = ("pool", "xh", "y", "core", "head")
    place_of = jnp.stack([lax.axis_index(a) for a in axes]).astype(jnp.int32)
    info = jnp.concatenate([place_of, destination, request_adapter_index])
    tokens = prompt.reshape(-1, prompt.shape[2])
    rows, heads = rotated_query.shape[0], rotated_query.shape[1] // HEAD_DIM
    query = rotated_query.reshape(rows, heads, HEAD_DIM)

    keys, values = pack(info, key_value_weight, adapter_down_weight)
    kx1, kx2, kx3 = x_shift(keys, 1), x_shift(keys, 2), x_shift(keys, -1)
    vy1, vy3 = y_shift(values, 1), y_shift(values, -1)
    att0 = attend(query, key_value_cache, current_key_value, cached_length, 0, 2)
    keys, kx1, kx2, kx3, values, vy1, vy3, att0, cached_length = barrier(
        (keys, kx1, kx2, kx3, values, vy1, vy3, att0, cached_length)
    )
    vy2 = y_shift(values, 2)
    key0 = jnp.concatenate([keys, kx1, kx2, kx3], 0)
    key1, key3 = y_shift(key0, 1), y_shift(key0, -1)
    att1 = attend(query, key_value_cache, current_key_value, cached_length, 1, 2)
    vy2, att1 = barrier((vy2, att1))
    both = [values, vy1, vy2, vy3]
    value0 = jnp.concatenate([v[:256] for v in both], 0)
    value1, value3 = x_shift(value0, 1), x_shift(value0, -1)
    down0 = jnp.concatenate([v[256:] for v in both], 0)
    down_own = jnp.concatenate([down0, xh_swap(down0)], 0)
    sums = main_product(info, tokens, ((0, 0, 0), (1, 0, 0)), (key0, value0))
    attended = jnp.concatenate([att0, att1], 0).reshape(rows, heads * HEAD_DIM)
    key0, value0, key1, key3, value1, value3, down_own, sums, attended = barrier(
        (key0, value0, key1, key3, value1, value3, down_own, sums, attended)
    )
    key2, value2 = y_shift(key0, 2), x_shift(value0, 2)
    low = low_rank(info, tokens, down_own, core_swap(down_own))
    kinds = ((0, 1, 0), (0, 3, 0), (1, 1, 0), (1, 3, 0))
    sums = main_product(info, tokens, kinds, (key1, key3, value1, value3), tuple(sums))
    ready = [core_swap(b) for b in (key0, value0, key1, key3, value1, value3)]
    across = xh_swap(attended)
    lows = ring(low, z_shift)
    key2, value2, ready, sums, across, lows, attended = barrier(
        (key2, value2, ready, sums, across, lows, attended)
    )
    mine = ring(jnp.concatenate([attended, across], 0), y_shift)
    last = [key2, value2, core_swap(key2), core_swap(value2)]
    kinds = ((0, 0, 1), (1, 0, 1), (0, 1, 1), (0, 3, 1), (1, 1, 1), (1, 3, 1))
    sums = main_product(info, tokens, kinds, ready, tuple(sums))
    kinds = ((0, 2, 0), (1, 2, 0), (0, 2, 1), (1, 2, 1))
    sums = main_product(info, tokens, kinds, last, tuple(sums))
    same, other = finish(info, lows, sums, adapter_up_weight)

    b0 = lax.ppermute(same, "pool", [(0, 1), (1, 0)])
    a0 = lax.ppermute(other, ("pool", "xh"), [(i, 3 - i) for i in range(4)])
    b0, a0, mine = barrier((b0, a0, mine))
    b1, b3 = y_shift(b0, 1), y_shift(b0, -1)
    a1, a3 = y_shift(a0, 1), y_shift(a0, -1)
    parts = mine + [core_swap(b) for b in mine]
    ranks = ADAPTERS * RANK
    down = jnp.transpose(output_down_weight, (1, 2, 0)).reshape(ranks, -1)
    up = output_up_weight.reshape(ranks, -1)
    shares = project(info, row_adapter_index[:, None], down, up, output_weight, parts)
    theirs0 = core_swap(choose(info, [b0, a0]))
    b0, a0, b1, b3, a1, a3, shares, theirs0 = barrier((b0, a0, b1, b3, a1, a3, shares, theirs0))
    b2, a2 = y_shift(b1, 1), y_shift(a3, -1)
    decoded = shares[0].astype(jnp.float32)
    for k, share in ((1, shares[1]), (2, shares[2]), (-1, shares[3])):
        decoded = decoded + z_shift(share, k).astype(jnp.float32)
    decoded = decoded.astype(jnp.bfloat16)
    theirs1 = core_swap(choose(info, [b1, b3, a1, a3]))
    theirs = jnp.concatenate([theirs0, theirs1], 1)
    kinds = ((0, 0), (1, 0), (0, 1), (0, 3), (1, 1), (1, 3))
    rest = ((0, 2), (1, 2))
    handed = place(info, kinds, rest, [b0, a0, b1, b3, a1, a3], theirs)
    b2, a2, decoded, handed = barrier((b2, a2, decoded, handed))
    theirs2 = core_swap(choose(info, [b2, a2]))
    handed = place(info, rest, (), [b2, a2], theirs2, handed)
    return handed, decoded


def solution(mesh):
    fine = Mesh(mesh.devices.reshape(2, 2, 4, 2, 4), ("pool", "xh", "y", "core", "head"))
    seq = ("xh", "y", "core")
    every = ("pool",) + seq
    in_specs = (
        P("pool", seq, None),
        P(seq, None, "head"),
        P(seq, None),
        P(None, None, None, "head"),
        P("pool"),
        P(),
        P(every, "head"),
        P(every, None, None, "head"),
        P(every, None, "head"),
        P(every),
        P("pool"),
        P("head", seq),
        P("head", None, None),
        P(None, None, seq),
    )
    out_specs = (P(every, None, None, None, "head"), P(("pool", "head"), seq))
    return jax.shard_map(body, mesh=fine, in_specs=in_specs, out_specs=out_specs, check_vma=False)
```

```python
import functools

import jax
import jax.numpy as jnp
from jax import lax
from jax.experimental import pallas as pl
from jax.experimental.pallas import tpu as pltpu
from jax.sharding import Mesh
from jax.sharding import PartitionSpec as P

HEAD_DIM = 128
RANK = 16
ADAPTERS = 8
CAP = 2
REQ_POOL = 4
X_SLOTS = 3
MIB = 2**20


POOL, XH, Y, CORE, HEAD, DEST, ADAPTER = 0, 1, 2, 3, 4, 5, 13
VMEM = pl.BlockSpec(memory_space=pltpu.VMEM)
SMEM = pl.BlockSpec(memory_space=pltpu.SMEM)
ANY = pl.BlockSpec(memory_space=pl.ANY)


def params(limit=8):
    return pltpu.CompilerParams(vmem_limit_bytes=limit * MIB)


def x_shift(value, k):
    pairs = []
    for x in range(4):
        t = (x + k) % 4
        pairs.append(((x % 2) * 2 + x // 2, (t % 2) * 2 + t // 2))
    return lax.ppermute(value, ("pool", "xh"), pairs)


def y_shift(value, k):
    return lax.ppermute(value, "y", [(i, (i + k) % 4) for i in range(4)])


def xh_swap(value):
    return lax.ppermute(value, "xh", [(0, 1), (1, 0)])


def z_shift(value, k):
    return lax.ppermute(value, "head", [(i, (i + k) % 4) for i in range(4)])


def z_flip(value, mask):
    return lax.ppermute(value, "head", [(i, i ^ mask) for i in range(4)])


def core_swap(value):
    return lax.ppermute(value, "core", [(0, 1), (1, 0)])


def pack_kernel(info, w_ref, d_ref, k_ref, v_ref):
    half = pl.ds(pl.multiple_of(info[POOL] * 256, 256), 256)
    k_ref[...] = w_ref[half, 0, :]
    v_ref[0:256] = w_ref[half, 1, :]
    column = lax.broadcasted_iota(jnp.int32, (256, 128), 0)
    lane = lax.broadcasted_iota(jnp.int32, (256, 128), 1)
    pick = (column == info[ADAPTER + info[HEAD]] * 32 + lane) & (lane < 32)
    low = lax.dot_general(
        pick.astype(jnp.bfloat16),
        d_ref[...],
        (((0,), (1,)), ((), ())),
        preferred_element_type=jnp.float32,
    ).astype(jnp.bfloat16)
    v_ref[256:288] = low[0:32, 0:256]
    v_ref[288:320] = low[0:32, 256:512]


def pack(info, weight, down):
    return pl.pallas_call(
        pack_kernel,
        in_specs=[SMEM, VMEM, VMEM],
        out_specs=[VMEM, VMEM],
        out_shape=[
            jax.ShapeDtypeStruct((256, 256), jnp.bfloat16),
            jax.ShapeDtypeStruct((320, 256), jnp.bfloat16),
        ],
        compiler_params=params(),
        name="pack",
    )(info, weight, down)


ROWS_STEP = 8


def attend_kernel(offset, len_ref, q_ref, kv_ref, cur_ref, o_ref):
    first = pl.program_id(0) * ROWS_STEP + offset
    factor = HEAD_DIM**-0.5
    lane = lax.broadcasted_iota(jnp.int32, (8, 256), 1)
    is_key = (lane & 1) == 0
    scores, own = [], []
    for i in range(ROWS_STEP):
        n = len_ref[first + i]
        valid = is_key & (lane < 2 * n)
        for h in range(2):
            both = kv_ref[i, :, :, h * 128 : (h + 1) * 128].reshape(256, 128)
            q = q_ref[i, h * 8 : (h + 1) * 8, :]
            s = lax.dot_general(
                q, both, (((1,), (1,)), ((), ())), preferred_element_type=jnp.float32
            )
            scores.append(jnp.where(valid, s * factor, -1e30))
            k = cur_ref[i, 0:1, h * 128 : (h + 1) * 128].astype(jnp.float32)
            own.append(jnp.sum(q.astype(jnp.float32) * k, axis=-1, keepdims=True) * factor)
    s = jnp.concatenate(scores, 0)
    o = jnp.concatenate(own, 0)
    highest = jnp.maximum(jnp.max(s, axis=-1, keepdims=True), o)
    raw = jnp.exp(s - highest)
    own_raw = jnp.exp(o - highest)
    norm = jnp.sum(raw, axis=-1, keepdims=True) + own_raw
    weights = pltpu.roll(raw / norm, 1, 1).astype(jnp.bfloat16)
    own_weight = (own_raw / norm).astype(jnp.bfloat16).astype(jnp.float32)
    for i in range(ROWS_STEP):
        for h in range(2):
            both = kv_ref[i, :, :, h * 128 : (h + 1) * 128].reshape(256, 128)
            j = (i * 2 + h) * 8
            v = cur_ref[i, 1:2, h * 128 : (h + 1) * 128].astype(jnp.float32)
            mixed = jnp.dot(weights[j : j + 8], both, preferred_element_type=jnp.float32)
            mixed = mixed + own_weight[j : j + 8] * v
            o_ref[i, h * 8 : (h + 1) * 8, :] = mixed.astype(jnp.bfloat16)


def attend(query, cache, current, lengths, part, parts):
    rows, heads = query.shape[0] // parts, query.shape[1]
    first = part * (rows // ROWS_STEP)
    return pl.pallas_call(
        functools.partial(attend_kernel, first * ROWS_STEP),
        grid_spec=pltpu.PrefetchScalarGridSpec(
            num_scalar_prefetch=1,
            grid=(rows // ROWS_STEP,),
            in_specs=[
                pl.BlockSpec((ROWS_STEP, heads, 128), lambda g, n: (g + first, 0, 0)),
                pl.BlockSpec((ROWS_STEP, 128, 2, 256), lambda g, n: (g + first, 0, 0, 0)),
                pl.BlockSpec((ROWS_STEP, 2, 256), lambda g, n: (g + first, 0, 0)),
            ],
            out_specs=pl.BlockSpec((ROWS_STEP, heads, 128), lambda g, n: (g, 0, 0)),
        ),
        out_shape=jax.ShapeDtypeStruct((rows, heads, 128), jnp.bfloat16),
        compiler_params=params(),
        name="attend",
    )(lengths, query, cache, current)


def split_dot(low, up, dims=(((1,), (0,)), ((), ()))):
    high = low.astype(jnp.bfloat16)
    rest = (low - high.astype(jnp.float32)).astype(jnp.bfloat16)
    return lax.dot_general(high, up, dims, preferred_element_type=jnp.float32) + lax.dot_general(
        rest, up, dims, preferred_element_type=jnp.float32
    )


def x_order(x):
    return [x, (x + 3) & 3, (x + 2) & 3, (x + 1) & 3]


def chunk_start(xi, yi, core):
    return pl.multiple_of(((xi >> 1) * 8 + yi * 2 + core) * 512 + (xi & 1) * 256, 256)


def low_kernel(info, prompt, own_ref, other_ref, out_ref):
    xh, y, core = info[XH], info[Y], info[CORE]
    rows = pl.ds(pl.multiple_of(info[HEAD] * 128, 128), 128)
    low = jnp.zeros((32, 128), jnp.float32)
    for n in range(2):
        ref, c_of = ((own_ref, core), (other_ref, 1 - core))[n]
        downs, tokens = [], []
        for i in range(16):
            side = xh if i < 8 else 1 - xh
            shard = side * 8 + x_order(y)[(i // 2) % 4] * 2 + c_of
            at = pl.multiple_of(shard * 512 + (i % 2) * 256, 256)
            tokens.append(prompt[rows, pl.ds(at, 256)])
            downs.append(ref[i * 32 : (i + 1) * 32])
        low = low + lax.dot_general(
            jnp.concatenate(downs, 1),
            jnp.concatenate(tokens, 1),
            (((1,), (1,)), ((), ())),
            preferred_element_type=jnp.float32,
        )
    out_ref[...] = low


def low_rank(info, tokens, own, other):
    return pl.pallas_call(
        low_kernel,
        in_specs=[SMEM, VMEM, VMEM, VMEM],
        out_specs=VMEM,
        out_shape=jax.ShapeDtypeStruct((32, 128), jnp.float32),
        compiler_params=params(),
        name="low_rank",
    )(info, tokens, own, other)


def main_kernel(kinds, fresh, info, prompt, *refs):
    n = max(kind[3] for kind in kinds) + 1
    blocks, sums, outs = refs[:n], refs[n:-2], refs[-2:]
    pool, xh, y, core = info[POOL], info[XH], info[Y], info[CORE]
    x = 2 * xh + pool
    done = [fresh, fresh]
    for kv, j, partner, which, block in kinds:
        c_of = 1 - core if partner else core
        tokens = []
        for i in range(4):
            xi = x_order(x)[i if kv == 0 else j]
            yi = x_order(y)[j if kv == 0 else i]
            tokens.append(prompt[:, pl.ds(chunk_start(xi, yi, c_of), 256)])
        part = jnp.dot(
            jnp.concatenate(tokens, 1),
            blocks[which][block * 1024 : (block + 1) * 1024],
            preferred_element_type=jnp.float32,
        )
        if done[kv] is True:
            outs[kv][...] = part
        elif done[kv] is False:
            outs[kv][...] = sums[kv][...] + part
        else:
            outs[kv][...] += part
        done[kv] = None


def main_product(info, tokens, kinds, blocks, sums=()):
    shape = jax.ShapeDtypeStruct((tokens.shape[0], 256), jnp.float32)
    return pl.pallas_call(
        functools.partial(main_kernel, kinds, not sums),
        in_specs=[SMEM] + [VMEM] * (1 + len(blocks) + len(sums)),
        out_specs=[VMEM, VMEM],
        out_shape=[shape, shape],
        compiler_params=params(),
        name="main_product",
    )(info, tokens, *blocks, *sums)


def finish_kernel(info, *refs):
    lows, k_ref, v_ref, up_ref, near_ref, far_ref = refs
    pool, xh, z = info[POOL], info[XH], info[HEAD]
    owners = [info[DEST + pool * REQ_POOL + r] for r in range(REQ_POOL)]
    dims = (((0,), (0,)), ((), ()))
    for n in range(REQ_POOL):
        r = z ^ n
        a = info[ADAPTER + r]
        rows = pl.ds(pl.multiple_of(r * 128, 128), 128)
        low = lows[n * 32 : (n + 1) * 32]
        both = []
        for kv, ref in enumerate((k_ref, v_ref)):
            value = ref[rows, :] + split_dot(low[kv * 16 : (kv + 1) * 16], up_ref[a, kv], dims)
            both.append(value.astype(jnp.bfloat16))
        result = jnp.stack(both, axis=1)
        owner = info[DEST + pool * REQ_POOL + r]
        slot = jnp.int32(0)
        for q in range(REQ_POOL):
            slot = slot + (((owners[q] >> 3) == (owner >> 3)) & (q < r)).astype(jnp.int32)

        @pl.when((owner >> 3) == xh)
        def _():
            near_ref[slot] = result

        @pl.when((owner >> 3) != xh)
        def _():
            far_ref[slot] = result


def finish(info, lows, sums, up):
    shape = jax.ShapeDtypeStruct((X_SLOTS, 128, 2, 256), jnp.bfloat16)
    return pl.pallas_call(
        finish_kernel,
        in_specs=[SMEM] + [VMEM] * 4,
        out_specs=[VMEM, VMEM],
        out_shape=[shape, shape],
        compiler_params=params(),
        name="finish",
    )(info, lows, *sums, up)


def slots_of(info, pool, xh, owner):
    owners = [info[DEST + pool * REQ_POOL + r] for r in range(REQ_POOL)]
    index = [jnp.int32(0)] * CAP
    used = [jnp.int32(0)] * CAP
    place, mine = jnp.int32(0), jnp.int32(0)
    for r in range(REQ_POOL):
        hit = (owners[r] == owner).astype(jnp.int32)
        for j in range(CAP):
            here = hit * (mine == j).astype(jnp.int32)
            index[j] = index[j] + here * place
            used[j] = used[j] + here
        mine = mine + hit
        place = place + ((owners[r] >> 3) == xh).astype(jnp.int32)
    return index, used


def place_kernel(kinds, rest, sizes, info, *refs):
    n = len(sizes)
    at = [(i, b) for i, size in enumerate(sizes) for b in range(size)]
    ins, others = refs[:n], refs[n : 2 * n]
    out, zero, sems = refs[-3], refs[-2], refs[-1]
    xh, y, core = info[XH], info[Y], info[CORE]
    index, used = slots_of(info, 1 - info[POOL], xh, xh * 8 + y * 2 + core)
    if rest:
        zero[...] = jnp.zeros_like(zero)

    def spot(j, kind, c_of):
        side = xh if kind[0] == 0 else 1 - xh
        token = (side * 8 + x_order(y)[kind[1]] * 2 + c_of) * 128
        return out.at[0, j, pl.ds(pl.multiple_of(token, 128), 128)]

    def transfers(j):
        full = []
        for b, kind in enumerate(kinds):
            i, k = at[b]
            full.append((ins[i].at[k, index[j]], spot(j, kind, core)))
            full.append((others[i].at[k, index[j]], spot(j, kind, 1 - core)))
        return [
            pltpu.make_async_copy(src, dst, sems.at[j, i]) for i, (src, dst) in enumerate(full)
        ]

    def clears(j):
        spots = [spot(j, kind, c) for kind in kinds + rest for c in (core, 1 - core)]
        return [pltpu.make_async_copy(zero, dst, sems.at[j, i]) for i, dst in enumerate(spots)]

    for step in ("start", "wait"):
        for j in range(CAP):

            @pl.when(used[j] == 1)
            def _():
                for c in transfers(j):
                    getattr(c, step)()

            if rest:

                @pl.when(used[j] == 0)
                def _():
                    for c in clears(j):
                        getattr(c, step)()


def place(info, kinds, rest, parts, others, out=None):
    shape = jax.ShapeDtypeStruct((1, CAP, 2048, 2, 256), jnp.bfloat16)
    ins = [info, *parts, *others] + ([] if out is None else [out])
    return pl.pallas_call(
        functools.partial(place_kernel, kinds, rest, tuple(p.shape[0] for p in parts)),
        in_specs=[SMEM] + [VMEM] * (len(parts) + len(others)) + ([] if out is None else [ANY]),
        out_specs=ANY,
        out_shape=shape,
        scratch_shapes=[
            pltpu.VMEM((128, 2, 256), jnp.bfloat16),
            pltpu.SemaphoreType.DMA((CAP, 16)),
        ],
        input_output_aliases={} if out is None else {len(ins) - 1: 0},
        compiler_params=params(),
        name="place",
    )(*ins)


def project_kernel(info, keep, down, up, w_ref, *refs):
    ins, outs, res = refs[:2], refs[2:6], refs[6]
    xh, y, core, z = info[XH], info[Y], info[CORE], info[HEAD]
    value = jnp.concatenate([ref[...] for ref in ins], 0)
    out = jnp.dot(value, w_ref[...], preferred_element_type=jnp.float32)
    low = lax.dot_general(
        value, down[...], (((1,), (1,)), ((), ())), preferred_element_type=jnp.float32
    )
    owner = lax.broadcasted_iota(jnp.int32, (48, ADAPTERS * RANK), 1) >> 4
    spots, lows = [], []
    for b in range(8):
        row, c_of = x_order(y)[b % 4], core if b < 4 else 1 - core
        for i in range(2):
            side = xh if i == 0 else 1 - xh
            at = pl.ds(pl.multiple_of((side * 8 + row * 2 + c_of) * 48, 16), 48)
            n = b * 96 + i * 48
            spots.append(at)
            lows.append(jnp.where(keep[at, :] == owner, low[n : n + 48], 0.0))
    out = (out + split_dot(jnp.concatenate(lows, 0), up[...])).astype(jnp.bfloat16)
    for n in range(16):
        res[spots[n], :] = out[n * 48 : (n + 1) * 48]
    for n in range(4):
        outs[n][...] = res[pl.ds(pl.multiple_of(((z + n) & 3) * 192, 64), 192), :]


def project(info, keep, down, up, weight, parts):
    rows, width = 768, weight.shape[1]
    return pl.pallas_call(
        project_kernel,
        in_specs=[SMEM] + [VMEM] * 6,
        out_specs=[VMEM] * 4,
        out_shape=[jax.ShapeDtypeStruct((rows // 4, width), jnp.bfloat16)] * 4,
        scratch_shapes=[pltpu.VMEM((rows, width), jnp.bfloat16)],
        compiler_params=params(),
        name="project",
    )(info, keep, down, up, weight, *parts)


def ring(value, shift):
    return [value, shift(value, 1), shift(value, 2), shift(value, -1)]


def body(
    prompt,
    key_value_weight,
    adapter_down_weight,
    adapter_up_weight,
    request_adapter_index,
    destination,
    rotated_query,
    key_value_cache,
    current_key_value,
    cached_length,
    row_adapter_index,
    output_weight,
    output_down_weight,
    output_up_weight,
):
    barrier = lax.optimization_barrier
    axes = ("pool", "xh", "y", "core", "head")
    place_of = jnp.stack([lax.axis_index(a) for a in axes]).astype(jnp.int32)
    info = jnp.concatenate([place_of, destination, request_adapter_index])
    tokens = prompt.reshape(-1, prompt.shape[2])
    tokens = pltpu.with_memory_space_constraint(tokens, pltpu.VMEM)
    rows, heads = rotated_query.shape[0], rotated_query.shape[1] // HEAD_DIM
    query = rotated_query.reshape(rows, heads, HEAD_DIM)

    keys, values = pack(info, key_value_weight, adapter_down_weight)
    kx1, kx2, kx3 = x_shift(keys, 1), x_shift(keys, 2), x_shift(keys, -1)
    vy1, vy3 = y_shift(values, 1), y_shift(values, -1)
    att0 = attend(query, key_value_cache, current_key_value, cached_length, 0, 2)
    keys, kx1, kx2, kx3, values, vy1, vy3, att0 = barrier(
        (keys, kx1, kx2, kx3, values, vy1, vy3, att0)
    )
    vy2 = y_shift(values, 2)
    key0 = jnp.concatenate([keys, kx1, kx2, kx3], 0)
    key1, key3 = y_shift(key0, 1), y_shift(key0, -1)
    vy2, cached_length = barrier((vy2, cached_length))
    both = [values, vy1, vy2, vy3]
    value0 = jnp.concatenate([v[:256] for v in both], 0)
    value1, value3 = x_shift(value0, 1), x_shift(value0, -1)
    down0 = jnp.concatenate([v[256:] for v in both], 0)
    down_own = jnp.concatenate([down0, xh_swap(down0)], 0)
    att1 = attend(query, key_value_cache, current_key_value, cached_length, 1, 2)
    attended = jnp.concatenate([att0, att1], 0).reshape(rows, heads * HEAD_DIM)
    low = low_rank(info, tokens, down_own, core_swap(down_own))
    key0, value0, key1, key3, value1, value3, low, attended = barrier(
        (key0, value0, key1, key3, value1, value3, low, attended)
    )
    first = [key0, value0, key1, key3, value1, value3]
    key2, value2 = y_shift(key0, 2), x_shift(value0, 2)
    theirs = core_swap(jnp.concatenate(first, 0))
    across = xh_swap(attended)
    pair = jnp.concatenate([low, z_flip(low, 1)], 0)
    lows = jnp.concatenate([pair, z_flip(pair, 2)], 0)
    key2, value2, theirs, across, lows, attended = barrier(
        (key2, value2, theirs, across, lows, attended)
    )
    mine = ring(jnp.concatenate([attended, across], 0), y_shift)
    last = [core_swap(key2), core_swap(value2)]
    order = ((0, 0), (1, 0), (0, 1), (0, 3), (1, 1), (1, 3))
    kinds = tuple((kv, j, 0, n, 0) for n, (kv, j) in enumerate(order))
    kinds += ((0, 2, 0, 6, 0), (1, 2, 0, 7, 0))
    kinds += tuple((kv, j, 1, 8, n) for n, (kv, j) in enumerate(order))
    sums = main_product(info, tokens, kinds, first + [key2, value2, theirs])
    sums = main_product(info, tokens, ((0, 2, 1, 0, 0), (1, 2, 1, 1, 0)), last, tuple(sums))
    same, other = finish(info, lows, sums, adapter_up_weight)

    b0 = lax.ppermute(same, "pool", [(0, 1), (1, 0)])
    a0 = lax.ppermute(other, ("pool", "xh"), [(i, 3 - i) for i in range(4)])
    mine = jnp.concatenate(mine, 0)
    partner = core_swap(mine)
    b0, a0, mine, partner = barrier((b0, a0, mine, partner))
    both0 = jnp.stack([b0, a0])
    both1, both3 = y_shift(both0, 1), y_shift(both0, -1)
    ranks = ADAPTERS * RANK
    down = jnp.transpose(output_down_weight, (1, 2, 0)).reshape(ranks, -1)
    up = output_up_weight.reshape(ranks, -1)
    keep = row_adapter_index[:, None]
    shares = project(info, keep, down, up, output_weight, [mine, partner])
    decoded = shares[0].astype(jnp.float32)
    for k, share in ((1, shares[1]), (2, shares[2]), (-1, shares[3])):
        decoded = decoded + z_shift(share, k).astype(jnp.float32)
    decoded = decoded.astype(jnp.bfloat16)
    both0, both1, both3, decoded = barrier((both0, both1, both3, decoded))
    b2, a2 = y_shift(both1[0], 1), y_shift(both3[1], -1)
    middle = [both0, both1, both3]
    theirs = [core_swap(v) for v in middle]
    b2, a2, theirs = barrier((b2, a2, theirs))
    theirs2 = [core_swap(b2), core_swap(a2)]
    kinds = ((0, 0), (1, 0), (0, 1), (1, 1), (0, 3), (1, 3))
    rest = ((0, 2), (1, 2))
    handed = place(info, kinds, rest, middle, theirs)
    handed = place(info, rest, (), [b2[None], a2[None]], [v[None] for v in theirs2], handed)
    return handed, decoded


def solution(mesh):
    fine = Mesh(mesh.devices.reshape(2, 2, 4, 2, 4), ("pool", "xh", "y", "core", "head"))
    seq = ("xh", "y", "core")
    every = ("pool",) + seq
    in_specs = (
        P("pool", seq, None),
        P(seq, None, "head"),
        P(seq, None),
        P(None, None, None, "head"),
        P("pool"),
        P(),
        P(every, "head"),
        P(every, None, None, "head"),
        P(every, None, "head"),
        P(every),
        P("pool"),
        P("head", seq),
        P("head", None, None),
        P(None, None, seq),
    )
    out_specs = (P(every, None, None, None, "head"), P(("pool", "head"), seq))
    return jax.shard_map(body, mesh=fine, in_specs=in_specs, out_specs=out_specs, check_vma=False)
```

```python
import functools

import jax
import jax.numpy as jnp
from jax import lax
from jax.experimental import pallas as pl
from jax.experimental.pallas import tpu as pltpu
from jax.sharding import Mesh
from jax.sharding import PartitionSpec as P

HEAD_DIM = 128
RANK = 16
ADAPTERS = 8
CAP = 2
REQ_POOL = 4
X_SLOTS = 3
MIB = 2**20


POOL, XH, Y, CORE, HEAD, DEST, ADAPTER = 0, 1, 2, 3, 4, 5, 13
VMEM = pl.BlockSpec(memory_space=pltpu.VMEM)
SMEM = pl.BlockSpec(memory_space=pltpu.SMEM)
ANY = pl.BlockSpec(memory_space=pl.ANY)


def params(limit=8):
    return pltpu.CompilerParams(vmem_limit_bytes=limit * MIB)


def x_shift(value, k):
    pairs = []
    for x in range(4):
        t = (x + k) % 4
        pairs.append(((x % 2) * 2 + x // 2, (t % 2) * 2 + t // 2))
    return lax.ppermute(value, ("pool", "xh"), pairs)


def y_shift(value, k):
    return lax.ppermute(value, "y", [(i, (i + k) % 4) for i in range(4)])


def xh_swap(value):
    return lax.ppermute(value, "xh", [(0, 1), (1, 0)])


def z_shift(value, k):
    return lax.ppermute(value, "head", [(i, (i + k) % 4) for i in range(4)])


def z_flip(value, mask):
    return lax.ppermute(value, "head", [(i, i ^ mask) for i in range(4)])


def core_swap(value):
    return lax.ppermute(value, "core", [(0, 1), (1, 0)])


def pack_kernel(info, w_ref, d_ref, k_ref, v_ref):
    half = pl.ds(pl.multiple_of(info[POOL] * 256, 256), 256)
    k_ref[...] = w_ref[half, 0, :]
    v_ref[0:256] = w_ref[half, 1, :]
    column = lax.broadcasted_iota(jnp.int32, (256, 128), 0)
    lane = lax.broadcasted_iota(jnp.int32, (256, 128), 1)
    pick = (column == info[ADAPTER + info[HEAD]] * 32 + lane) & (lane < 32)
    low = lax.dot_general(
        pick.astype(jnp.bfloat16),
        d_ref[...],
        (((0,), (1,)), ((), ())),
        preferred_element_type=jnp.float32,
    ).astype(jnp.bfloat16)
    v_ref[256:288] = low[0:32, 0:256]
    v_ref[288:320] = low[0:32, 256:512]


def pack(info, weight, down):
    return pl.pallas_call(
        pack_kernel,
        in_specs=[SMEM, VMEM, VMEM],
        out_specs=[VMEM, VMEM],
        out_shape=[
            jax.ShapeDtypeStruct((256, 256), jnp.bfloat16),
            jax.ShapeDtypeStruct((320, 256), jnp.bfloat16),
        ],
        compiler_params=params(),
        name="pack",
    )(info, weight, down)


ROWS_STEP = 8


def attend_kernel(offset, len_ref, q_ref, kv_ref, cur_ref, o_ref):
    first = pl.program_id(0) * ROWS_STEP + offset
    factor = HEAD_DIM**-0.5
    lane = lax.broadcasted_iota(jnp.int32, (8, 256), 1)
    is_key = (lane & 1) == 0
    scores, own = [], []
    for i in range(ROWS_STEP):
        n = len_ref[first + i]
        valid = is_key & (lane < 2 * n)
        for h in range(2):
            both = kv_ref[i, :, :, h * 128 : (h + 1) * 128].reshape(256, 128)
            q = q_ref[i, h * 8 : (h + 1) * 8, :]
            s = lax.dot_general(
                q, both, (((1,), (1,)), ((), ())), preferred_element_type=jnp.float32
            )
            scores.append(jnp.where(valid, s * factor, -1e30))
            k = cur_ref[i, 0:1, h * 128 : (h + 1) * 128].astype(jnp.float32)
            own.append(jnp.sum(q.astype(jnp.float32) * k, axis=-1, keepdims=True) * factor)
    s = jnp.concatenate(scores, 0)
    o = jnp.concatenate(own, 0)
    highest = jnp.maximum(jnp.max(s, axis=-1, keepdims=True), o)
    raw = jnp.exp(s - highest)
    own_raw = jnp.exp(o - highest)
    norm = jnp.sum(raw, axis=-1, keepdims=True) + own_raw
    weights = pltpu.roll(raw / norm, 1, 1).astype(jnp.bfloat16)
    own_weight = (own_raw / norm).astype(jnp.bfloat16).astype(jnp.float32)
    for i in range(ROWS_STEP):
        for h in range(2):
            both = kv_ref[i, :, :, h * 128 : (h + 1) * 128].reshape(256, 128)
            j = (i * 2 + h) * 8
            v = cur_ref[i, 1:2, h * 128 : (h + 1) * 128].astype(jnp.float32)
            mixed = jnp.dot(weights[j : j + 8], both, preferred_element_type=jnp.float32)
            mixed = mixed + own_weight[j : j + 8] * v
            o_ref[i, h * 8 : (h + 1) * 8, :] = mixed.astype(jnp.bfloat16)


def attend(query, cache, current, lengths, part, parts):
    rows, heads = query.shape[0] // parts, query.shape[1]
    first = part * (rows // ROWS_STEP)
    return pl.pallas_call(
        functools.partial(attend_kernel, first * ROWS_STEP),
        grid_spec=pltpu.PrefetchScalarGridSpec(
            num_scalar_prefetch=1,
            grid=(rows // ROWS_STEP,),
            in_specs=[
                pl.BlockSpec((ROWS_STEP, heads, 128), lambda g, n: (g + first, 0, 0)),
                pl.BlockSpec((ROWS_STEP, 128, 2, 256), lambda g, n: (g + first, 0, 0, 0)),
                pl.BlockSpec((ROWS_STEP, 2, 256), lambda g, n: (g + first, 0, 0)),
            ],
            out_specs=pl.BlockSpec((ROWS_STEP, heads, 128), lambda g, n: (g, 0, 0)),
        ),
        out_shape=jax.ShapeDtypeStruct((rows, heads, 128), jnp.bfloat16),
        compiler_params=params(),
        name="attend",
    )(lengths, query, cache, current)


def split_dot(low, up, dims=(((1,), (0,)), ((), ()))):
    high = low.astype(jnp.bfloat16)
    rest = (low - high.astype(jnp.float32)).astype(jnp.bfloat16)
    return lax.dot_general(high, up, dims, preferred_element_type=jnp.float32) + lax.dot_general(
        rest, up, dims, preferred_element_type=jnp.float32
    )


def x_order(x):
    return [x, (x + 3) & 3, (x + 2) & 3, (x + 1) & 3]


def chunk_start(xi, yi, core):
    return pl.multiple_of(((xi >> 1) * 8 + yi * 2 + core) * 512 + (xi & 1) * 256, 256)


def low_kernel(info, prompt, own_ref, other_ref, out_ref):
    xh, y, core = info[XH], info[Y], info[CORE]
    rows = pl.ds(pl.multiple_of(info[HEAD] * 128, 128), 128)
    low = jnp.zeros((32, 128), jnp.float32)
    for n in range(2):
        ref, c_of = ((own_ref, core), (other_ref, 1 - core))[n]
        downs, tokens = [], []
        for i in range(16):
            side = xh if i < 8 else 1 - xh
            shard = side * 8 + x_order(y)[(i // 2) % 4] * 2 + c_of
            at = pl.multiple_of(shard * 512 + (i % 2) * 256, 256)
            tokens.append(prompt[rows, pl.ds(at, 256)])
            downs.append(ref[i * 32 : (i + 1) * 32])
        low = low + lax.dot_general(
            jnp.concatenate(downs, 1),
            jnp.concatenate(tokens, 1),
            (((1,), (1,)), ((), ())),
            preferred_element_type=jnp.float32,
        )
    out_ref[...] = low


def low_rank(info, tokens, own, other):
    return pl.pallas_call(
        low_kernel,
        in_specs=[SMEM, VMEM, VMEM, VMEM],
        out_specs=VMEM,
        out_shape=jax.ShapeDtypeStruct((32, 128), jnp.float32),
        compiler_params=params(),
        name="low_rank",
    )(info, tokens, own, other)


def main_kernel(kinds, fresh, info, prompt, *refs):
    n = max(kind[3] for kind in kinds) + 1
    blocks, sums, outs = refs[:n], refs[n:-2], refs[-2:]
    pool, xh, y, core = info[POOL], info[XH], info[Y], info[CORE]
    x = 2 * xh + pool
    done = [fresh, fresh]
    for kv, j, partner, which, block in kinds:
        c_of = 1 - core if partner else core
        tokens = []
        for i in range(4):
            xi = x_order(x)[i if kv == 0 else j]
            yi = x_order(y)[j if kv == 0 else i]
            tokens.append(prompt[:, pl.ds(chunk_start(xi, yi, c_of), 256)])
        part = jnp.dot(
            jnp.concatenate(tokens, 1),
            blocks[which][block * 1024 : (block + 1) * 1024],
            preferred_element_type=jnp.float32,
        )
        if done[kv] is True:
            outs[kv][...] = part
        elif done[kv] is False:
            outs[kv][...] = sums[kv][...] + part
        else:
            outs[kv][...] += part
        done[kv] = None


def main_product(info, tokens, kinds, blocks, sums=()):
    shape = jax.ShapeDtypeStruct((tokens.shape[0], 256), jnp.float32)
    return pl.pallas_call(
        functools.partial(main_kernel, kinds, not sums),
        in_specs=[SMEM] + [VMEM] * (1 + len(blocks) + len(sums)),
        out_specs=[VMEM, VMEM],
        out_shape=[shape, shape],
        compiler_params=params(),
        name="main_product",
    )(info, tokens, *blocks, *sums)


def finish_kernel(info, *refs):
    lows, k_ref, v_ref, up_ref, near_ref, far_ref = refs
    pool, xh, z = info[POOL], info[XH], info[HEAD]
    owners = [info[DEST + pool * REQ_POOL + r] for r in range(REQ_POOL)]
    dims = (((0,), (0,)), ((), ()))
    for n in range(REQ_POOL):
        r = z ^ n
        a = info[ADAPTER + r]
        rows = pl.ds(pl.multiple_of(r * 128, 128), 128)
        low = lows[n * 32 : (n + 1) * 32]
        both = []
        for kv, ref in enumerate((k_ref, v_ref)):
            value = ref[rows, :] + split_dot(low[kv * 16 : (kv + 1) * 16], up_ref[a, kv], dims)
            both.append(value.astype(jnp.bfloat16))
        result = jnp.stack(both, axis=1)
        owner = info[DEST + pool * REQ_POOL + r]
        slot = jnp.int32(0)
        for q in range(REQ_POOL):
            slot = slot + (((owners[q] >> 3) == (owner >> 3)) & (q < r)).astype(jnp.int32)

        @pl.when((owner >> 3) == xh)
        def _():
            near_ref[slot] = result

        @pl.when((owner >> 3) != xh)
        def _():
            far_ref[slot] = result


def finish(info, lows, sums, up):
    shape = jax.ShapeDtypeStruct((X_SLOTS, 128, 2, 256), jnp.bfloat16)
    return pl.pallas_call(
        finish_kernel,
        in_specs=[SMEM] + [VMEM] * 4,
        out_specs=[VMEM, VMEM],
        out_shape=[shape, shape],
        compiler_params=params(),
        name="finish",
    )(info, lows, *sums, up)


def slots_of(info, pool, xh, owner):
    owners = [info[DEST + pool * REQ_POOL + r] for r in range(REQ_POOL)]
    index = [jnp.int32(0)] * CAP
    used = [jnp.int32(0)] * CAP
    place, mine = jnp.int32(0), jnp.int32(0)
    for r in range(REQ_POOL):
        hit = (owners[r] == owner).astype(jnp.int32)
        for j in range(CAP):
            here = hit * (mine == j).astype(jnp.int32)
            index[j] = index[j] + here * place
            used[j] = used[j] + here
        mine = mine + hit
        place = place + ((owners[r] >> 3) == xh).astype(jnp.int32)
    return index, used


def place_kernel(kinds, rest, sizes, info, *refs):
    n = len(sizes)
    at = [(i, b) for i, size in enumerate(sizes) for b in range(size)]
    ins, others = refs[:n], refs[n : 2 * n]
    out, zero, sems = refs[-3], refs[-2], refs[-1]
    xh, y, core = info[XH], info[Y], info[CORE]
    index, used = slots_of(info, 1 - info[POOL], xh, xh * 8 + y * 2 + core)
    if rest:
        zero[...] = jnp.zeros_like(zero)

    def spot(j, kind, c_of):
        side = xh if kind[0] == 0 else 1 - xh
        token = (side * 8 + x_order(y)[kind[1]] * 2 + c_of) * 128
        return out.at[0, j, pl.ds(pl.multiple_of(token, 128), 128)]

    def transfers(j):
        full = []
        for b, kind in enumerate(kinds):
            i, k = at[b]
            full.append((ins[i].at[k, index[j]], spot(j, kind, core)))
            full.append((others[i].at[k, index[j]], spot(j, kind, 1 - core)))
        return [
            pltpu.make_async_copy(src, dst, sems.at[j, i]) for i, (src, dst) in enumerate(full)
        ]

    def clears(j):
        spots = [spot(j, kind, c) for kind in kinds + rest for c in (core, 1 - core)]
        return [pltpu.make_async_copy(zero, dst, sems.at[j, i]) for i, dst in enumerate(spots)]

    for step in ("start", "wait"):
        for j in range(CAP):

            @pl.when(used[j] == 1)
            def _():
                for c in transfers(j):
                    getattr(c, step)()

            if rest:

                @pl.when(used[j] == 0)
                def _():
                    for c in clears(j):
                        getattr(c, step)()


def place(info, kinds, rest, parts, others, out=None):
    shape = jax.ShapeDtypeStruct((1, CAP, 2048, 2, 256), jnp.bfloat16)
    ins = [info, *parts, *others] + ([] if out is None else [out])
    return pl.pallas_call(
        functools.partial(place_kernel, kinds, rest, tuple(p.shape[0] for p in parts)),
        in_specs=[SMEM] + [VMEM] * (len(parts) + len(others)) + ([] if out is None else [ANY]),
        out_specs=ANY,
        out_shape=shape,
        scratch_shapes=[
            pltpu.VMEM((128, 2, 256), jnp.bfloat16),
            pltpu.SemaphoreType.DMA((CAP, 16)),
        ],
        input_output_aliases={} if out is None else {len(ins) - 1: 0},
        compiler_params=params(),
        name="place",
    )(*ins)


def project_kernel(info, keep, down, up, w_ref, *refs):
    ins, outs, res = refs[:2], refs[2:6], refs[6]
    xh, y, core, z = info[XH], info[Y], info[CORE], info[HEAD]
    value = jnp.concatenate([ref[...] for ref in ins], 0)
    out = jnp.dot(value, w_ref[...], preferred_element_type=jnp.float32)
    low = lax.dot_general(
        value, down[...], (((1,), (1,)), ((), ())), preferred_element_type=jnp.float32
    )
    owner = lax.broadcasted_iota(jnp.int32, (48, ADAPTERS * RANK), 1) >> 4
    spots, lows = [], []
    for b in range(8):
        row, c_of = x_order(y)[b % 4], core if b < 4 else 1 - core
        for i in range(2):
            side = xh if i == 0 else 1 - xh
            at = pl.ds(pl.multiple_of((side * 8 + row * 2 + c_of) * 48, 16), 48)
            n = b * 96 + i * 48
            spots.append(at)
            lows.append(jnp.where(keep[at, :] == owner, low[n : n + 48], 0.0))
    out = (out + split_dot(jnp.concatenate(lows, 0), up[...])).astype(jnp.bfloat16)
    for n in range(16):
        res[spots[n], :] = out[n * 48 : (n + 1) * 48]
    for n in range(4):
        outs[n][...] = res[pl.ds(pl.multiple_of(((z + n) & 3) * 192, 64), 192), :]


def project(info, keep, down, up, weight, parts):
    rows, width = 768, weight.shape[1]
    return pl.pallas_call(
        project_kernel,
        in_specs=[SMEM] + [VMEM] * 6,
        out_specs=[VMEM] * 4,
        out_shape=[jax.ShapeDtypeStruct((rows // 4, width), jnp.bfloat16)] * 4,
        scratch_shapes=[pltpu.VMEM((rows, width), jnp.bfloat16)],
        compiler_params=params(),
        name="project",
    )(info, keep, down, up, weight, *parts)


def ring(value, shift):
    return [value, shift(value, 1), shift(value, 2), shift(value, -1)]


def body(
    prompt,
    key_value_weight,
    adapter_down_weight,
    adapter_up_weight,
    request_adapter_index,
    destination,
    rotated_query,
    key_value_cache,
    current_key_value,
    cached_length,
    row_adapter_index,
    output_weight,
    output_down_weight,
    output_up_weight,
):
    barrier = lax.optimization_barrier
    axes = ("pool", "xh", "y", "core", "head")
    place_of = jnp.stack([lax.axis_index(a) for a in axes]).astype(jnp.int32)
    info = jnp.concatenate([place_of, destination, request_adapter_index])
    tokens = prompt.reshape(-1, prompt.shape[2])
    tokens = pltpu.with_memory_space_constraint(tokens, pltpu.VMEM)
    rows, heads = rotated_query.shape[0], rotated_query.shape[1] // HEAD_DIM
    query = rotated_query.reshape(rows, heads, HEAD_DIM)

    keys, values = pack(info, key_value_weight, adapter_down_weight)
    kx1, kx2, kx3 = x_shift(keys, 1), x_shift(keys, 2), x_shift(keys, -1)
    vy1, vy3 = y_shift(values, 1), y_shift(values, -1)
    keys, kx1, kx2, kx3, values, vy1, vy3 = barrier((keys, kx1, kx2, kx3, values, vy1, vy3))
    vy2 = y_shift(values, 2)
    key0 = jnp.concatenate([keys, kx1, kx2, kx3], 0)
    key1, key3 = y_shift(key0, 1), y_shift(key0, -1)
    vy2, cached_length = barrier((vy2, cached_length))
    both = [values, vy1, vy2, vy3]
    value0 = jnp.concatenate([v[:256] for v in both], 0)
    value1, value3 = x_shift(value0, 1), x_shift(value0, -1)
    down0 = jnp.concatenate([v[256:] for v in both], 0)
    down_own = jnp.concatenate([down0, xh_swap(down0)], 0)
    attended = attend(query, key_value_cache, current_key_value, cached_length, 0, 1)
    attended = attended.reshape(rows, heads * HEAD_DIM)
    key0, value0, key1, key3, value1, value3, down_own, attended = barrier(
        (key0, value0, key1, key3, value1, value3, down_own, attended)
    )
    first = [key0, value0, key1, key3, value1, value3]
    key2, value2 = y_shift(key0, 2), x_shift(value0, 2)
    theirs = core_swap(jnp.concatenate(first, 0))
    across = xh_swap(attended)
    low = low_rank(info, tokens, down_own, core_swap(down_own))
    pair = jnp.concatenate([low, z_flip(low, 1)], 0)
    lows = jnp.concatenate([pair, z_flip(pair, 2)], 0)
    key2, value2, theirs, across, lows, attended = barrier(
        (key2, value2, theirs, across, lows, attended)
    )
    mine = ring(jnp.concatenate([attended, across], 0), y_shift)
    last = [core_swap(key2), core_swap(value2)]
    order = ((0, 0), (1, 0), (0, 1), (0, 3), (1, 1), (1, 3))
    kinds = tuple((kv, j, 0, n, 0) for n, (kv, j) in enumerate(order))
    kinds += ((0, 2, 0, 6, 0), (1, 2, 0, 7, 0))
    kinds += tuple((kv, j, 1, 8, n) for n, (kv, j) in enumerate(order))
    sums = main_product(info, tokens, kinds, first + [key2, value2, theirs])
    sums = main_product(info, tokens, ((0, 2, 1, 0, 0), (1, 2, 1, 1, 0)), last, tuple(sums))
    same, other = finish(info, lows, sums, adapter_up_weight)

    b0 = lax.ppermute(same, "pool", [(0, 1), (1, 0)])
    a0 = lax.ppermute(other, ("pool", "xh"), [(i, 3 - i) for i in range(4)])
    b0, a0, mine = barrier((b0, a0, mine))
    mine = jnp.concatenate(mine, 0)
    partner = core_swap(mine)
    both0 = jnp.stack([b0, a0])
    both1, both3 = y_shift(both0, 1), y_shift(both0, -1)
    ranks = ADAPTERS * RANK
    down = jnp.transpose(output_down_weight, (1, 2, 0)).reshape(ranks, -1)
    up = output_up_weight.reshape(ranks, -1)
    keep = row_adapter_index[:, None]
    shares = project(info, keep, down, up, output_weight, [mine, partner])
    decoded = shares[0].astype(jnp.float32)
    for k, share in ((1, shares[1]), (2, shares[2]), (-1, shares[3])):
        decoded = decoded + z_shift(share, k).astype(jnp.float32)
    decoded = decoded.astype(jnp.bfloat16)
    both0, both1, both3, decoded = barrier((both0, both1, both3, decoded))
    b2, a2 = y_shift(both1[0], 1), y_shift(both3[1], -1)
    middle = [both0, both1, both3]
    theirs = [core_swap(v) for v in middle]
    b2, a2, theirs = barrier((b2, a2, theirs))
    theirs2 = [core_swap(b2), core_swap(a2)]
    kinds = ((0, 0), (1, 0), (0, 1), (1, 1), (0, 3), (1, 3))
    rest = ((0, 2), (1, 2))
    handed = place(info, kinds, rest, middle, theirs)
    handed = place(info, rest, (), [b2[None], a2[None]], [v[None] for v in theirs2], handed)
    return handed, decoded


def solution(mesh):
    fine = Mesh(mesh.devices.reshape(2, 2, 4, 2, 4), ("pool", "xh", "y", "core", "head"))
    seq = ("xh", "y", "core")
    every = ("pool",) + seq
    in_specs = (
        P("pool", seq, None),
        P(seq, None, "head"),
        P(seq, None),
        P(None, None, None, "head"),
        P("pool"),
        P(),
        P(every, "head"),
        P(every, None, None, "head"),
        P(every, None, "head"),
        P(every),
        P("pool"),
        P("head", seq),
        P("head", None, None),
        P(None, None, seq),
    )
    out_specs = (P(every, None, None, None, "head"), P(("pool", "head"), seq))
    return jax.shard_map(body, mesh=fine, in_specs=in_specs, out_specs=out_specs, check_vma=False)
```

```python
import functools

import jax
import jax.numpy as jnp
from jax import lax
from jax.experimental import pallas as pl
from jax.experimental.pallas import tpu as pltpu
from jax.sharding import Mesh
from jax.sharding import PartitionSpec as P

HEAD_DIM = 128
RANK = 16
ADAPTERS = 8
CAP = 2
REQ_POOL = 4
X_SLOTS = 3
MIB = 2**20


POOL, XH, Y, CORE, HEAD, DEST, ADAPTER = 0, 1, 2, 3, 4, 5, 13
VMEM = pl.BlockSpec(memory_space=pltpu.VMEM)
SMEM = pl.BlockSpec(memory_space=pltpu.SMEM)
ANY = pl.BlockSpec(memory_space=pl.ANY)


def params(limit=8):
    return pltpu.CompilerParams(vmem_limit_bytes=limit * MIB)


def x_mirror(value):
    return lax.ppermute(value, ("pool", "xh"), [(i, 3 - i) for i in range(4)])


def y_shift(value, k):
    return lax.ppermute(value, "y", [(i, (i + k) % 4) for i in range(4)])


def xh_swap(value):
    return lax.ppermute(value, "xh", [(0, 1), (1, 0)])


def z_shift(value, k):
    return lax.ppermute(value, "head", [(i, (i + k) % 4) for i in range(4)])


def z_flip(value, mask):
    return lax.ppermute(value, "head", [(i, i ^ mask) for i in range(4)])


def core_swap(value):
    return lax.ppermute(value, "core", [(0, 1), (1, 0)])


def pack_kernel(info, w_ref, d_ref, k_ref, v_ref):
    k_ref[...] = w_ref[:, 0, :]
    v_ref[0:512] = w_ref[:, 1, :]
    column = lax.broadcasted_iota(jnp.int32, (256, 128), 0)
    lane = lax.broadcasted_iota(jnp.int32, (256, 128), 1)
    pick = (column == info[ADAPTER + info[HEAD]] * 32 + lane) & (lane < 32)
    low = lax.dot_general(
        pick.astype(jnp.bfloat16),
        d_ref[...],
        (((0,), (1,)), ((), ())),
        preferred_element_type=jnp.float32,
    ).astype(jnp.bfloat16)
    v_ref[512:544] = low[0:32, 0:256]
    v_ref[544:576] = low[0:32, 256:512]


def pack(info, weight, down):
    return pl.pallas_call(
        pack_kernel,
        in_specs=[SMEM, VMEM, VMEM],
        out_specs=[VMEM, VMEM],
        out_shape=[
            jax.ShapeDtypeStruct((512, 256), jnp.bfloat16),
            jax.ShapeDtypeStruct((576, 256), jnp.bfloat16),
        ],
        compiler_params=params(),
        name="pack",
    )(info, weight, down)


ROWS_STEP = 8


def attend_kernel(offset, len_ref, q_ref, kv_ref, cur_ref, o_ref):
    first = pl.program_id(0) * ROWS_STEP + offset
    factor = HEAD_DIM**-0.5
    lane = lax.broadcasted_iota(jnp.int32, (8, 256), 1)
    is_key = (lane & 1) == 0
    scores, own = [], []
    for i in range(ROWS_STEP):
        n = len_ref[first + i]
        valid = is_key & (lane < 2 * n)
        for h in range(2):
            both = kv_ref[i, :, :, h * 128 : (h + 1) * 128].reshape(256, 128)
            q = q_ref[i, h * 8 : (h + 1) * 8, :]
            s = lax.dot_general(
                q, both, (((1,), (1,)), ((), ())), preferred_element_type=jnp.float32
            )
            scores.append(jnp.where(valid, s * factor, -1e30))
            k = cur_ref[i, 0:1, h * 128 : (h + 1) * 128].astype(jnp.float32)
            own.append(jnp.sum(q.astype(jnp.float32) * k, axis=-1, keepdims=True) * factor)
    s = jnp.concatenate(scores, 0)
    o = jnp.concatenate(own, 0)
    highest = jnp.maximum(jnp.max(s, axis=-1, keepdims=True), o)
    raw = jnp.exp(s - highest)
    own_raw = jnp.exp(o - highest)
    norm = jnp.sum(raw, axis=-1, keepdims=True) + own_raw
    weights = pltpu.roll(raw / norm, 1, 1).astype(jnp.bfloat16)
    own_weight = (own_raw / norm).astype(jnp.bfloat16).astype(jnp.float32)
    for i in range(ROWS_STEP):
        for h in range(2):
            both = kv_ref[i, :, :, h * 128 : (h + 1) * 128].reshape(256, 128)
            j = (i * 2 + h) * 8
            v = cur_ref[i, 1:2, h * 128 : (h + 1) * 128].astype(jnp.float32)
            mixed = jnp.dot(weights[j : j + 8], both, preferred_element_type=jnp.float32)
            mixed = mixed + own_weight[j : j + 8] * v
            o_ref[i, h * 8 : (h + 1) * 8, :] = mixed.astype(jnp.bfloat16)


def attend(query, cache, current, lengths, part, parts):
    rows, heads = query.shape[0] // parts, query.shape[1]
    first = part * (rows // ROWS_STEP)
    return pl.pallas_call(
        functools.partial(attend_kernel, first * ROWS_STEP),
        grid_spec=pltpu.PrefetchScalarGridSpec(
            num_scalar_prefetch=1,
            grid=(rows // ROWS_STEP,),
            in_specs=[
                pl.BlockSpec((ROWS_STEP, heads, 128), lambda g, n: (g + first, 0, 0)),
                pl.BlockSpec((ROWS_STEP, 128, 2, 256), lambda g, n: (g + first, 0, 0, 0)),
                pl.BlockSpec((ROWS_STEP, 2, 256), lambda g, n: (g + first, 0, 0)),
            ],
            out_specs=pl.BlockSpec((ROWS_STEP, heads, 128), lambda g, n: (g, 0, 0)),
        ),
        out_shape=jax.ShapeDtypeStruct((rows, heads, 128), jnp.bfloat16),
        compiler_params=params(),
        name="attend",
    )(lengths, query, cache, current)


def split_dot(low, up, dims=(((1,), (0,)), ((), ()))):
    high = low.astype(jnp.bfloat16)
    rest = (low - high.astype(jnp.float32)).astype(jnp.bfloat16)
    return lax.dot_general(high, up, dims, preferred_element_type=jnp.float32) + lax.dot_general(
        rest, up, dims, preferred_element_type=jnp.float32
    )


def x_order(x):
    return [x, (x + 3) & 3, (x + 2) & 3, (x + 1) & 3]


def low_kernel(info, prompt, own_ref, other_ref, out_ref):
    xh, y, core = info[XH], info[Y], info[CORE]
    rows = pl.ds(pl.multiple_of(info[HEAD] * 128, 128), 128)
    low = jnp.zeros((32, 128), jnp.float32)
    for n in range(2):
        ref, c_of = ((own_ref, core), (other_ref, 1 - core))[n]
        downs, tokens = [], []
        for i in range(16):
            side = xh if i < 8 else 1 - xh
            shard = side * 8 + x_order(y)[(i // 2) % 4] * 2 + c_of
            at = pl.multiple_of(shard * 512 + (i % 2) * 256, 256)
            tokens.append(prompt[rows, pl.ds(at, 256)])
            downs.append(ref[i * 32 : (i + 1) * 32])
        low = low + lax.dot_general(
            jnp.concatenate(downs, 1),
            jnp.concatenate(tokens, 1),
            (((1,), (1,)), ((), ())),
            preferred_element_type=jnp.float32,
        )
    out_ref[...] = low


def low_rank(info, tokens, own, other):
    return pl.pallas_call(
        low_kernel,
        in_specs=[SMEM, VMEM, VMEM, VMEM],
        out_specs=VMEM,
        out_shape=jax.ShapeDtypeStruct((32, 128), jnp.float32),
        compiler_params=params(),
        name="low_rank",
    )(info, tokens, own, other)


def add_products(pieces, fresh, info, prompt, blocks, outs):
    xh, y, core = info[XH], info[Y], info[CORE]
    fresh = [fresh, fresh]
    for kv, partner, which, row, shards in pieces:
        c_of = 1 - core if partner else core
        tokens = []
        for other, j in shards:
            side = 1 - xh if other else xh
            at = pl.multiple_of((side * 8 + x_order(y)[j] * 2 + c_of) * 512, 512)
            tokens.append(prompt[:, pl.ds(at, 512)])
        part = jnp.dot(
            jnp.concatenate(tokens, 1),
            blocks[which][row : row + 512 * len(shards)],
            preferred_element_type=jnp.float32,
        )
        if fresh[kv]:
            outs[kv][...] = part
        else:
            outs[kv][...] += part
        fresh[kv] = False


def key_piece(partner, which, row, j):
    return (0, partner, which, row, ((0, j), (1, j)))


def value_pieces(partner, which, row, other):
    return tuple(
        (1, partner, which, row + 1024 * n, ((other, 2 * n), (other, 2 * n + 1))) for n in range(2)
    )


def main_kernel(pieces, info, prompt, *refs):
    add_products(pieces, True, info, prompt, refs[:-2], refs[-2:])


def main_product(info, tokens, pieces, blocks):
    shape = jax.ShapeDtypeStruct((tokens.shape[0], 256), jnp.float32)
    return pl.pallas_call(
        functools.partial(main_kernel, pieces),
        in_specs=[SMEM] + [VMEM] * (1 + len(blocks)),
        out_specs=[VMEM, VMEM],
        out_shape=[shape, shape],
        compiler_params=params(),
        name="main_product",
    )(info, tokens, *blocks)


def finish_kernel(pieces, n_sums, info, prompt, *refs):
    n = len(refs) - 6 - 2 * n_sums
    blocks, sums = refs[:n], refs[n : n + 2 * n_sums]
    lows, up_ref, near_ref, far_ref, k_ref, v_ref = refs[n + 2 * n_sums :]
    pool, xh, z = info[POOL], info[XH], info[HEAD]
    for kv, ref in enumerate((k_ref, v_ref)):
        total = sums[kv][...]
        for m in range(1, n_sums):
            total = total + sums[2 * m + kv][...]
        ref[...] = total
    add_products(pieces, False, info, prompt, blocks, (k_ref, v_ref))
    owners = [info[DEST + pool * REQ_POOL + r] for r in range(REQ_POOL)]
    dims = (((0,), (0,)), ((), ()))
    for n in range(REQ_POOL):
        r = z ^ n
        a = info[ADAPTER + r]
        rows = pl.ds(pl.multiple_of(r * 128, 128), 128)
        low = lows[n * 32 : (n + 1) * 32]
        both = []
        for kv, ref in enumerate((k_ref, v_ref)):
            value = ref[rows, :] + split_dot(low[kv * 16 : (kv + 1) * 16], up_ref[a, kv], dims)
            both.append(value.astype(jnp.bfloat16))
        result = jnp.stack(both, axis=1)
        owner = info[DEST + pool * REQ_POOL + r]
        slot = jnp.int32(0)
        for q in range(REQ_POOL):
            slot = slot + (((owners[q] >> 3) == (owner >> 3)) & (q < r)).astype(jnp.int32)

        @pl.when((owner >> 3) == xh)
        def _():
            near_ref[slot] = result

        @pl.when((owner >> 3) != xh)
        def _():
            far_ref[slot] = result


def finish(info, tokens, pieces, blocks, sums, lows, up):
    shape = jax.ShapeDtypeStruct((X_SLOTS, 128, 2, 256), jnp.bfloat16)
    total = pltpu.VMEM((tokens.shape[0], 256), jnp.float32)
    flat = [v for pair in sums for v in pair]
    return pl.pallas_call(
        functools.partial(finish_kernel, pieces, len(sums)),
        in_specs=[SMEM] + [VMEM] * (3 + len(blocks) + len(flat)),
        out_specs=[VMEM, VMEM],
        out_shape=[shape, shape],
        scratch_shapes=[total, total],
        compiler_params=params(),
        name="finish",
    )(info, tokens, *blocks, *flat, lows, up)


def slots_of(info, pool, xh, owner):
    owners = [info[DEST + pool * REQ_POOL + r] for r in range(REQ_POOL)]
    index = [jnp.int32(0)] * CAP
    used = [jnp.int32(0)] * CAP
    place, mine = jnp.int32(0), jnp.int32(0)
    for r in range(REQ_POOL):
        hit = (owners[r] == owner).astype(jnp.int32)
        for j in range(CAP):
            here = hit * (mine == j).astype(jnp.int32)
            index[j] = index[j] + here * place
            used[j] = used[j] + here
        mine = mine + hit
        place = place + ((owners[r] >> 3) == xh).astype(jnp.int32)
    return index, used


def place_kernel(kinds, rest, sizes, info, *refs):
    n = len(sizes)
    at = [(i, b) for i, size in enumerate(sizes) for b in range(size)]
    ins, others = refs[:n], refs[n : 2 * n]
    out, zero, sems = refs[-3], refs[-2], refs[-1]
    xh, y, core = info[XH], info[Y], info[CORE]
    index, used = slots_of(info, 1 - info[POOL], xh, xh * 8 + y * 2 + core)
    if rest:
        zero[...] = jnp.zeros_like(zero)

    def spot(j, kind, c_of):
        side = xh if kind[0] == 0 else 1 - xh
        token = (side * 8 + x_order(y)[kind[1]] * 2 + c_of) * 128
        return out.at[0, j, pl.ds(pl.multiple_of(token, 128), 128)]

    def transfers(j):
        full = []
        for b, kind in enumerate(kinds):
            i, k = at[b]
            full.append((ins[i].at[k, index[j]], spot(j, kind, core)))
            full.append((others[i].at[k, index[j]], spot(j, kind, 1 - core)))
        return [
            pltpu.make_async_copy(src, dst, sems.at[j, i]) for i, (src, dst) in enumerate(full)
        ]

    def clears(j):
        spots = [spot(j, kind, c) for kind in kinds + rest for c in (core, 1 - core)]
        return [pltpu.make_async_copy(zero, dst, sems.at[j, i]) for i, dst in enumerate(spots)]

    for step in ("start", "wait"):
        for j in range(CAP):

            @pl.when(used[j] == 1)
            def _():
                for c in transfers(j):
                    getattr(c, step)()

            if rest:

                @pl.when(used[j] == 0)
                def _():
                    for c in clears(j):
                        getattr(c, step)()


def place(info, kinds, rest, parts, others, out=None):
    shape = jax.ShapeDtypeStruct((1, CAP, 2048, 2, 256), jnp.bfloat16)
    ins = [info, *parts, *others] + ([] if out is None else [out])
    return pl.pallas_call(
        functools.partial(place_kernel, kinds, rest, tuple(p.shape[0] for p in parts)),
        in_specs=[SMEM] + [VMEM] * (len(parts) + len(others)) + ([] if out is None else [ANY]),
        out_specs=ANY,
        out_shape=shape,
        scratch_shapes=[
            pltpu.VMEM((128, 2, 256), jnp.bfloat16),
            pltpu.SemaphoreType.DMA((CAP, 16)),
        ],
        input_output_aliases={} if out is None else {len(ins) - 1: 0},
        compiler_params=params(),
        name="place",
    )(*ins)


def project_kernel(info, keep, down, up, w_ref, *refs):
    ins, outs, res = refs[:2], refs[2:6], refs[6]
    xh, y, core, z = info[XH], info[Y], info[CORE], info[HEAD]
    value = jnp.concatenate([ref[...] for ref in ins], 0)
    out = jnp.dot(value, w_ref[...], preferred_element_type=jnp.float32)
    low = lax.dot_general(
        value, down[...], (((1,), (1,)), ((), ())), preferred_element_type=jnp.float32
    )
    owner = lax.broadcasted_iota(jnp.int32, (48, ADAPTERS * RANK), 1) >> 4
    spots, lows = [], []
    for b in range(8):
        row, c_of = x_order(y)[b % 4], core if b < 4 else 1 - core
        for i in range(2):
            side = xh if i == 0 else 1 - xh
            at = pl.ds(pl.multiple_of((side * 8 + row * 2 + c_of) * 48, 16), 48)
            n = b * 96 + i * 48
            spots.append(at)
            lows.append(jnp.where(keep[at, :] == owner, low[n : n + 48], 0.0))
    out = (out + split_dot(jnp.concatenate(lows, 0), up[...])).astype(jnp.bfloat16)
    for n in range(16):
        res[spots[n], :] = out[n * 48 : (n + 1) * 48]
    for n in range(4):
        outs[n][...] = res[pl.ds(pl.multiple_of(((z + n) & 3) * 192, 64), 192), :]


def project(info, keep, down, up, weight, parts):
    rows, width = 768, weight.shape[1]
    return pl.pallas_call(
        project_kernel,
        in_specs=[SMEM] + [VMEM] * 6,
        out_specs=[VMEM] * 4,
        out_shape=[jax.ShapeDtypeStruct((rows // 4, width), jnp.bfloat16)] * 4,
        scratch_shapes=[pltpu.VMEM((rows, width), jnp.bfloat16)],
        compiler_params=params(),
        name="project",
    )(info, keep, down, up, weight, *parts)


def ring(value, shift):
    return [value, shift(value, 1), shift(value, 2), shift(value, -1)]


def body(
    prompt,
    key_value_weight,
    adapter_down_weight,
    adapter_up_weight,
    request_adapter_index,
    destination,
    rotated_query,
    key_value_cache,
    current_key_value,
    cached_length,
    row_adapter_index,
    output_weight,
    output_down_weight,
    output_up_weight,
):
    barrier = lax.optimization_barrier
    axes = ("pool", "xh", "y", "core", "head")
    place_of = jnp.stack([lax.axis_index(a) for a in axes]).astype(jnp.int32)
    info = jnp.concatenate([place_of, destination, request_adapter_index])
    tokens = prompt.reshape(-1, prompt.shape[2])
    tokens = pltpu.with_memory_space_constraint(tokens, pltpu.VMEM)
    rows, heads = rotated_query.shape[0], rotated_query.shape[1] // HEAD_DIM
    query = rotated_query.reshape(rows, heads, HEAD_DIM)

    keys, values = pack(info, key_value_weight, adapter_down_weight)
    keys_across = x_mirror(keys)
    ring_values = ring(values, y_shift)
    keys, keys_across, ring_values, cached_length = barrier(
        (keys, keys_across, ring_values, cached_length)
    )
    key0 = jnp.concatenate([keys, keys_across], 0)
    value0 = jnp.concatenate([v[:512] for v in ring_values], 0)
    down0 = jnp.concatenate([v[512:] for v in ring_values], 0)
    key1, key3 = y_shift(key0, 1), y_shift(key0, -1)
    value1 = xh_swap(value0)
    down_own = jnp.concatenate([down0, xh_swap(down0)], 0)
    attended = attend(query, key_value_cache, current_key_value, cached_length, 0, 1)
    attended = attended.reshape(rows, heads * HEAD_DIM)
    down_own, attended = barrier((down_own, attended))
    low = low_rank(info, tokens, down_own, core_swap(down_own))
    pieces = (key_piece(0, 0, 0, 0),) + value_pieces(0, 1, 0, 0)
    first = main_product(info, tokens, pieces, [key0, value0])
    own = core_swap(jnp.concatenate([key0, value0], 0))
    pieces = (key_piece(1, 0, 0, 0),) + value_pieces(1, 0, 1024, 0)
    second = main_product(info, tokens, pieces, [own])
    key0, key1, key3, low, attended, first, second = barrier(
        (key0, key1, key3, low, attended, first, second)
    )
    key2 = y_shift(key0, 2)
    across = xh_swap(attended)
    pair = jnp.concatenate([low, z_flip(low, 1)], 0)
    lows = jnp.concatenate([pair, z_flip(pair, 2)], 0)
    key1, key2, key3, value1, across, attended, lows = barrier(
        (key1, key2, key3, value1, across, attended, lows)
    )
    mine = ring(jnp.concatenate([attended, across], 0), y_shift)
    theirs_k = core_swap(jnp.concatenate([key1, key2, key3], 0))
    theirs_v = core_swap(value1)
    pieces = tuple(key_piece(0, n, 0, n + 1) for n in range(3)) + value_pieces(0, 3, 0, 1)
    third = main_product(info, tokens, pieces, [key1, key2, key3, value1])
    pieces = tuple(key_piece(1, 0, 1024 * n, n + 1) for n in range(3)) + value_pieces(1, 1, 0, 1)
    sums = [first, second, third]
    same, other = finish(
        info, tokens, pieces, [theirs_k, theirs_v], sums, lows, adapter_up_weight
    )

    b0 = lax.ppermute(same, "pool", [(0, 1), (1, 0)])
    a0 = x_mirror(other)
    b0, a0, mine = barrier((b0, a0, mine))
    mine = jnp.concatenate(mine, 0)
    partner = core_swap(mine)
    both0 = jnp.stack([b0, a0])
    both1, both3 = y_shift(both0, 1), y_shift(both0, -1)
    ranks = ADAPTERS * RANK
    down = jnp.transpose(output_down_weight, (1, 2, 0)).reshape(ranks, -1)
    up = output_up_weight.reshape(ranks, -1)
    keep = row_adapter_index[:, None]
    shares = project(info, keep, down, up, output_weight, [mine, partner])
    decoded = shares[0].astype(jnp.float32)
    for k, share in ((1, shares[1]), (2, shares[2]), (-1, shares[3])):
        decoded = decoded + z_shift(share, k).astype(jnp.float32)
    decoded = decoded.astype(jnp.bfloat16)
    both0, both1, both3, decoded = barrier((both0, both1, both3, decoded))
    b2, a2 = y_shift(both1[0], 1), y_shift(both3[1], -1)
    middle = [both0, both1, both3]
    theirs = [core_swap(v) for v in middle]
    b2, a2, theirs = barrier((b2, a2, theirs))
    theirs2 = [core_swap(b2), core_swap(a2)]
    kinds = ((0, 0), (1, 0), (0, 1), (1, 1), (0, 3), (1, 3))
    rest = ((0, 2), (1, 2))
    handed = place(info, kinds, rest, middle, theirs)
    handed = place(info, rest, (), [b2[None], a2[None]], [v[None] for v in theirs2], handed)
    return handed, decoded


def solution(mesh):
    fine = Mesh(mesh.devices.reshape(2, 2, 4, 2, 4), ("pool", "xh", "y", "core", "head"))
    seq = ("xh", "y", "core")
    every = ("pool",) + seq
    in_specs = (
        P("pool", seq, None),
        P(seq, None, "head"),
        P(seq, None),
        P(None, None, None, "head"),
        P("pool"),
        P(),
        P(every, "head"),
        P(every, None, None, "head"),
        P(every, None, "head"),
        P(every),
        P("pool"),
        P("head", seq),
        P("head", None, None),
        P(None, None, seq),
    )
    out_specs = (P(every, None, None, None, "head"), P(("pool", "head"), seq))
    return jax.shard_map(body, mesh=fine, in_specs=in_specs, out_specs=out_specs, check_vma=False)
```

```python
import functools

import jax
import jax.numpy as jnp
from jax import lax
from jax.experimental import pallas as pl
from jax.experimental.pallas import tpu as pltpu
from jax.sharding import Mesh
from jax.sharding import PartitionSpec as P

HEAD_DIM = 128
RANK = 16
ADAPTERS = 8
CAP = 2
REQ_POOL = 4
X_SLOTS = 3
MIB = 2**20


POOL, XH, Y, CORE, HEAD, DEST, ADAPTER = 0, 1, 2, 3, 4, 5, 13
VMEM = pl.BlockSpec(memory_space=pltpu.VMEM)
SMEM = pl.BlockSpec(memory_space=pltpu.SMEM)
ANY = pl.BlockSpec(memory_space=pl.ANY)


def params(limit=8):
    return pltpu.CompilerParams(vmem_limit_bytes=limit * MIB)


def x_mirror(value):
    return lax.ppermute(value, ("pool", "xh"), [(i, 3 - i) for i in range(4)])


def x_shift(value, k):
    pairs = []
    for x in range(4):
        t = (x + k) % 4
        pairs.append(((x % 2) * 2 + x // 2, (t % 2) * 2 + t // 2))
    return lax.ppermute(value, ("pool", "xh"), pairs)


def y_shift(value, k):
    return lax.ppermute(value, "y", [(i, (i + k) % 4) for i in range(4)])


def xh_swap(value):
    return lax.ppermute(value, "xh", [(0, 1), (1, 0)])


def z_shift(value, k):
    return lax.ppermute(value, "head", [(i, (i + k) % 4) for i in range(4)])


def z_flip(value, mask):
    return lax.ppermute(value, "head", [(i, i ^ mask) for i in range(4)])


def core_swap(value):
    return lax.ppermute(value, "core", [(0, 1), (1, 0)])


def pack_kernel(info, w_ref, d_ref, k_ref, v_ref):
    k_ref[...] = w_ref[:, 0, :]
    v_ref[0:256] = w_ref[pl.ds(pl.multiple_of(info[POOL] * 256, 256), 256), 1, :]
    column = lax.broadcasted_iota(jnp.int32, (256, 128), 0)
    lane = lax.broadcasted_iota(jnp.int32, (256, 128), 1)
    pick = (column == info[ADAPTER + info[HEAD]] * 32 + lane) & (lane < 32)
    low = lax.dot_general(
        pick.astype(jnp.bfloat16),
        d_ref[...],
        (((0,), (1,)), ((), ())),
        preferred_element_type=jnp.float32,
    ).astype(jnp.bfloat16)
    v_ref[256:288] = low[0:32, 0:256]
    v_ref[288:320] = low[0:32, 256:512]


def pack(info, weight, down):
    return pl.pallas_call(
        pack_kernel,
        in_specs=[SMEM, VMEM, VMEM],
        out_specs=[VMEM, VMEM],
        out_shape=[
            jax.ShapeDtypeStruct((512, 256), jnp.bfloat16),
            jax.ShapeDtypeStruct((320, 256), jnp.bfloat16),
        ],
        compiler_params=params(),
        name="pack",
    )(info, weight, down)


ROWS_STEP = 8


def attend_kernel(offset, len_ref, q_ref, kv_ref, cur_ref, o_ref):
    first = pl.program_id(0) * ROWS_STEP + offset
    factor = HEAD_DIM**-0.5
    lane = lax.broadcasted_iota(jnp.int32, (8, 256), 1)
    is_key = (lane & 1) == 0
    scores, own = [], []
    for i in range(ROWS_STEP):
        n = len_ref[first + i]
        valid = is_key & (lane < 2 * n)
        for h in range(2):
            both = kv_ref[i, :, :, h * 128 : (h + 1) * 128].reshape(256, 128)
            q = q_ref[i, h * 8 : (h + 1) * 8, :]
            s = lax.dot_general(
                q, both, (((1,), (1,)), ((), ())), preferred_element_type=jnp.float32
            )
            scores.append(jnp.where(valid, s * factor, -1e30))
            k = cur_ref[i, 0:1, h * 128 : (h + 1) * 128].astype(jnp.float32)
            own.append(jnp.sum(q.astype(jnp.float32) * k, axis=-1, keepdims=True) * factor)
    s = jnp.concatenate(scores, 0)
    o = jnp.concatenate(own, 0)
    highest = jnp.maximum(jnp.max(s, axis=-1, keepdims=True), o)
    raw = jnp.exp(s - highest)
    own_raw = jnp.exp(o - highest)
    norm = jnp.sum(raw, axis=-1, keepdims=True) + own_raw
    weights = pltpu.roll(raw / norm, 1, 1).astype(jnp.bfloat16)
    own_weight = (own_raw / norm).astype(jnp.bfloat16).astype(jnp.float32)
    for i in range(ROWS_STEP):
        for h in range(2):
            both = kv_ref[i, :, :, h * 128 : (h + 1) * 128].reshape(256, 128)
            j = (i * 2 + h) * 8
            v = cur_ref[i, 1:2, h * 128 : (h + 1) * 128].astype(jnp.float32)
            mixed = jnp.dot(weights[j : j + 8], both, preferred_element_type=jnp.float32)
            mixed = mixed + own_weight[j : j + 8] * v
            o_ref[i, h * 8 : (h + 1) * 8, :] = mixed.astype(jnp.bfloat16)


def attend(query, cache, current, lengths, part, parts):
    rows, heads = query.shape[0] // parts, query.shape[1]
    first = part * (rows // ROWS_STEP)
    return pl.pallas_call(
        functools.partial(attend_kernel, first * ROWS_STEP),
        grid_spec=pltpu.PrefetchScalarGridSpec(
            num_scalar_prefetch=1,
            grid=(rows // ROWS_STEP,),
            in_specs=[
                pl.BlockSpec((ROWS_STEP, heads, 128), lambda g, n: (g + first, 0, 0)),
                pl.BlockSpec((ROWS_STEP, 128, 2, 256), lambda g, n: (g + first, 0, 0, 0)),
                pl.BlockSpec((ROWS_STEP, 2, 256), lambda g, n: (g + first, 0, 0)),
            ],
            out_specs=pl.BlockSpec((ROWS_STEP, heads, 128), lambda g, n: (g, 0, 0)),
        ),
        out_shape=jax.ShapeDtypeStruct((rows, heads, 128), jnp.bfloat16),
        compiler_params=params(),
        name="attend",
    )(lengths, query, cache, current)


def split_dot(low, up, dims=(((1,), (0,)), ((), ()))):
    high = low.astype(jnp.bfloat16)
    rest = (low - high.astype(jnp.float32)).astype(jnp.bfloat16)
    return lax.dot_general(high, up, dims, preferred_element_type=jnp.float32) + lax.dot_general(
        rest, up, dims, preferred_element_type=jnp.float32
    )


def x_order(x):
    return [x, (x + 3) & 3, (x + 2) & 3, (x + 1) & 3]


def low_kernel(info, prompt, own_ref, other_ref, out_ref):
    xh, y, core = info[XH], info[Y], info[CORE]
    rows = pl.ds(pl.multiple_of(info[HEAD] * 128, 128), 128)
    low = jnp.zeros((32, 128), jnp.float32)
    for n in range(2):
        ref, c_of = ((own_ref, core), (other_ref, 1 - core))[n]
        downs, tokens = [], []
        for i in range(16):
            side = xh if i < 8 else 1 - xh
            shard = side * 8 + x_order(y)[(i // 2) % 4] * 2 + c_of
            at = pl.multiple_of(shard * 512 + (i % 2) * 256, 256)
            tokens.append(prompt[rows, pl.ds(at, 256)])
            downs.append(ref[i * 32 : (i + 1) * 32])
        low = low + lax.dot_general(
            jnp.concatenate(downs, 1),
            jnp.concatenate(tokens, 1),
            (((1,), (1,)), ((), ())),
            preferred_element_type=jnp.float32,
        )
    out_ref[...] = low


def low_rank(info, tokens, own, other):
    return pl.pallas_call(
        low_kernel,
        in_specs=[SMEM, VMEM, VMEM, VMEM],
        out_specs=VMEM,
        out_shape=jax.ShapeDtypeStruct((32, 128), jnp.float32),
        compiler_params=params(),
        name="low_rank",
    )(info, tokens, own, other)


def add_products(pieces, fresh, info, prompt, blocks, outs):
    pool, xh, y, core = info[POOL], info[XH], info[Y], info[CORE]
    fresh = [fresh, fresh]
    for kv, partner, which, row, j in pieces:
        c_of = 1 - core if partner else core
        tokens = []
        if kv == 0:
            for side in (xh, 1 - xh):
                at = pl.multiple_of((side * 8 + x_order(y)[j] * 2 + c_of) * 512, 512)
                tokens.append(prompt[:, pl.ds(at, 512)])
        else:
            xi = x_order(2 * xh + pool)[j]
            for yi in x_order(y):
                at = ((xi >> 1) * 8 + yi * 2 + c_of) * 512 + (xi & 1) * 256
                tokens.append(prompt[:, pl.ds(pl.multiple_of(at, 256), 256)])
        part = jnp.dot(
            jnp.concatenate(tokens, 1),
            blocks[which][row : row + 1024],
            preferred_element_type=jnp.float32,
        )
        if fresh[kv]:
            outs[kv][...] = part
        else:
            outs[kv][...] += part
        fresh[kv] = False


def main_kernel(pieces, info, prompt, *refs):
    add_products(pieces, True, info, prompt, refs[:-2], refs[-2:])


def main_product(info, tokens, pieces, blocks):
    shape = jax.ShapeDtypeStruct((tokens.shape[0], 256), jnp.float32)
    return pl.pallas_call(
        functools.partial(main_kernel, pieces),
        in_specs=[SMEM] + [VMEM] * (1 + len(blocks)),
        out_specs=[VMEM, VMEM],
        out_shape=[shape, shape],
        compiler_params=params(),
        name="main_product",
    )(info, tokens, *blocks)


def finish_kernel(pieces, n_sums, info, prompt, *refs):
    n = len(refs) - 6 - 2 * n_sums
    blocks, sums = refs[:n], refs[n : n + 2 * n_sums]
    lows, up_ref, near_ref, far_ref, k_ref, v_ref = refs[n + 2 * n_sums :]
    pool, xh, z = info[POOL], info[XH], info[HEAD]
    for kv, ref in enumerate((k_ref, v_ref)):
        total = sums[kv][...]
        for m in range(1, n_sums):
            total = total + sums[2 * m + kv][...]
        ref[...] = total
    add_products(pieces, False, info, prompt, blocks, (k_ref, v_ref))
    owners = [info[DEST + pool * REQ_POOL + r] for r in range(REQ_POOL)]
    dims = (((0,), (0,)), ((), ()))
    for n in range(REQ_POOL):
        r = z ^ n
        a = info[ADAPTER + r]
        rows = pl.ds(pl.multiple_of(r * 128, 128), 128)
        low = lows[n * 32 : (n + 1) * 32]
        both = []
        for kv, ref in enumerate((k_ref, v_ref)):
            value = ref[rows, :] + split_dot(low[kv * 16 : (kv + 1) * 16], up_ref[a, kv], dims)
            both.append(value.astype(jnp.bfloat16))
        result = jnp.stack(both, axis=1)
        owner = info[DEST + pool * REQ_POOL + r]
        slot = jnp.int32(0)
        for q in range(REQ_POOL):
            slot = slot + (((owners[q] >> 3) == (owner >> 3)) & (q < r)).astype(jnp.int32)

        @pl.when((owner >> 3) == xh)
        def _():
            near_ref[slot] = result

        @pl.when((owner >> 3) != xh)
        def _():
            far_ref[slot] = result


def finish(info, tokens, pieces, blocks, sums, lows, up):
    shape = jax.ShapeDtypeStruct((X_SLOTS, 128, 2, 256), jnp.bfloat16)
    total = pltpu.VMEM((tokens.shape[0], 256), jnp.float32)
    flat = [v for pair in sums for v in pair]
    return pl.pallas_call(
        functools.partial(finish_kernel, pieces, len(sums)),
        in_specs=[SMEM] + [VMEM] * (3 + len(blocks) + len(flat)),
        out_specs=[VMEM, VMEM],
        out_shape=[shape, shape],
        scratch_shapes=[total, total],
        compiler_params=params(),
        name="finish",
    )(info, tokens, *blocks, *flat, lows, up)


def slots_of(info, pool, xh, owner):
    owners = [info[DEST + pool * REQ_POOL + r] for r in range(REQ_POOL)]
    index = [jnp.int32(0)] * CAP
    used = [jnp.int32(0)] * CAP
    place, mine = jnp.int32(0), jnp.int32(0)
    for r in range(REQ_POOL):
        hit = (owners[r] == owner).astype(jnp.int32)
        for j in range(CAP):
            here = hit * (mine == j).astype(jnp.int32)
            index[j] = index[j] + here * place
            used[j] = used[j] + here
        mine = mine + hit
        place = place + ((owners[r] >> 3) == xh).astype(jnp.int32)
    return index, used


def place_kernel(kinds, rest, sizes, info, *refs):
    n = len(sizes)
    at = [(i, b) for i, size in enumerate(sizes) for b in range(size)]
    ins, others = refs[:n], refs[n : 2 * n]
    out, zero, sems = refs[-3], refs[-2], refs[-1]
    xh, y, core = info[XH], info[Y], info[CORE]
    index, used = slots_of(info, 1 - info[POOL], xh, xh * 8 + y * 2 + core)
    if rest:
        zero[...] = jnp.zeros_like(zero)

    def spot(j, kind, c_of):
        side = xh if kind[0] == 0 else 1 - xh
        token = (side * 8 + x_order(y)[kind[1]] * 2 + c_of) * 128
        return out.at[0, j, pl.ds(pl.multiple_of(token, 128), 128)]

    def transfers(j):
        full = []
        for b, kind in enumerate(kinds):
            i, k = at[b]
            full.append((ins[i].at[k, index[j]], spot(j, kind, core)))
            full.append((others[i].at[k, index[j]], spot(j, kind, 1 - core)))
        return [
            pltpu.make_async_copy(src, dst, sems.at[j, i]) for i, (src, dst) in enumerate(full)
        ]

    def clears(j):
        spots = [spot(j, kind, c) for kind in kinds + rest for c in (core, 1 - core)]
        return [pltpu.make_async_copy(zero, dst, sems.at[j, i]) for i, dst in enumerate(spots)]

    for step in ("start", "wait"):
        for j in range(CAP):

            @pl.when(used[j] == 1)
            def _():
                for c in transfers(j):
                    getattr(c, step)()

            if rest:

                @pl.when(used[j] == 0)
                def _():
                    for c in clears(j):
                        getattr(c, step)()


def place(info, kinds, rest, parts, others, out=None):
    shape = jax.ShapeDtypeStruct((1, CAP, 2048, 2, 256), jnp.bfloat16)
    ins = [info, *parts, *others] + ([] if out is None else [out])
    return pl.pallas_call(
        functools.partial(place_kernel, kinds, rest, tuple(p.shape[0] for p in parts)),
        in_specs=[SMEM] + [VMEM] * (len(parts) + len(others)) + ([] if out is None else [ANY]),
        out_specs=ANY,
        out_shape=shape,
        scratch_shapes=[
            pltpu.VMEM((128, 2, 256), jnp.bfloat16),
            pltpu.SemaphoreType.DMA((CAP, 16)),
        ],
        input_output_aliases={} if out is None else {len(ins) - 1: 0},
        compiler_params=params(),
        name="place",
    )(*ins)


def project_kernel(info, keep, down, up, w_ref, *refs):
    ins, outs, res = refs[:2], refs[2:6], refs[6]
    xh, y, core, z = info[XH], info[Y], info[CORE], info[HEAD]
    value = jnp.concatenate([ref[...] for ref in ins], 0)
    out = jnp.dot(value, w_ref[...], preferred_element_type=jnp.float32)
    low = lax.dot_general(
        value, down[...], (((1,), (1,)), ((), ())), preferred_element_type=jnp.float32
    )
    owner = lax.broadcasted_iota(jnp.int32, (48, ADAPTERS * RANK), 1) >> 4
    spots, lows = [], []
    for b in range(8):
        row, c_of = x_order(y)[b % 4], core if b < 4 else 1 - core
        for i in range(2):
            side = xh if i == 0 else 1 - xh
            at = pl.ds(pl.multiple_of((side * 8 + row * 2 + c_of) * 48, 16), 48)
            n = b * 96 + i * 48
            spots.append(at)
            lows.append(jnp.where(keep[at, :] == owner, low[n : n + 48], 0.0))
    out = (out + split_dot(jnp.concatenate(lows, 0), up[...])).astype(jnp.bfloat16)
    for n in range(16):
        res[spots[n], :] = out[n * 48 : (n + 1) * 48]
    for n in range(4):
        outs[n][...] = res[pl.ds(pl.multiple_of(((z + n) & 3) * 192, 64), 192), :]


def project(info, keep, down, up, weight, parts):
    rows, width = 768, weight.shape[1]
    return pl.pallas_call(
        project_kernel,
        in_specs=[SMEM] + [VMEM] * 6,
        out_specs=[VMEM] * 4,
        out_shape=[jax.ShapeDtypeStruct((rows // 4, width), jnp.bfloat16)] * 4,
        scratch_shapes=[pltpu.VMEM((rows, width), jnp.bfloat16)],
        compiler_params=params(),
        name="project",
    )(info, keep, down, up, weight, *parts)


def ring(value, shift):
    return [value, shift(value, 1), shift(value, 2), shift(value, -1)]


def body(
    prompt,
    key_value_weight,
    adapter_down_weight,
    adapter_up_weight,
    request_adapter_index,
    destination,
    rotated_query,
    key_value_cache,
    current_key_value,
    cached_length,
    row_adapter_index,
    output_weight,
    output_down_weight,
    output_up_weight,
):
    barrier = lax.optimization_barrier
    axes = ("pool", "xh", "y", "core", "head")
    place_of = jnp.stack([lax.axis_index(a) for a in axes]).astype(jnp.int32)
    info = jnp.concatenate([place_of, destination, request_adapter_index])
    tokens = prompt.reshape(-1, prompt.shape[2])
    tokens = pltpu.with_memory_space_constraint(tokens, pltpu.VMEM)
    rows, heads = rotated_query.shape[0], rotated_query.shape[1] // HEAD_DIM
    query = rotated_query.reshape(rows, heads, HEAD_DIM)

    keys, values = pack(info, key_value_weight, adapter_down_weight)
    keys_across = x_mirror(keys)
    ring_values = ring(values, y_shift)
    keys, keys_across, ring_values, cached_length = barrier(
        (keys, keys_across, ring_values, cached_length)
    )
    key0 = jnp.concatenate([keys, keys_across], 0)
    value0 = jnp.concatenate([v[:256] for v in ring_values], 0)
    down0 = jnp.concatenate([v[256:] for v in ring_values], 0)
    key1, key3 = y_shift(key0, 1), y_shift(key0, -1)
    value1, value3 = x_shift(value0, 1), x_shift(value0, -1)
    down_own = jnp.concatenate([down0, xh_swap(down0)], 0)
    attended = attend(query, key_value_cache, current_key_value, cached_length, 0, 1)
    attended = attended.reshape(rows, heads * HEAD_DIM)
    key0, value0, key1, key3, value1, value3, down_own, attended = barrier(
        (key0, value0, key1, key3, value1, value3, down_own, attended)
    )
    key2, value2 = y_shift(key0, 2), x_shift(value0, 2)
    blocks = [key0, value0, key1, key3, value1, value3]
    order = ((0, 0), (1, 0), (0, 1), (0, 3), (1, 1), (1, 3))
    theirs = core_swap(jnp.concatenate(blocks, 0))
    across = xh_swap(attended)
    low = low_rank(info, tokens, down_own, core_swap(down_own))
    pair = jnp.concatenate([low, z_flip(low, 1)], 0)
    lows = jnp.concatenate([pair, z_flip(pair, 2)], 0)
    pieces = tuple((kv, 0, n, 0, j) for n, (kv, j) in enumerate(order))
    first = main_product(info, tokens, pieces, blocks)
    pieces = tuple((kv, 1, 0, 1024 * n, j) for n, (kv, j) in enumerate(order))
    second = main_product(info, tokens, pieces, [theirs])
    key2, value2, first, second, across, lows, attended = barrier(
        (key2, value2, first, second, across, lows, attended)
    )
    mine = ring(jnp.concatenate([attended, across], 0), y_shift)
    last = [key2, value2, core_swap(key2), core_swap(value2)]
    pieces = ((0, 0, 0, 0, 2), (1, 0, 1, 0, 2), (0, 1, 2, 0, 2), (1, 1, 3, 0, 2))
    same, other = finish(info, tokens, pieces, last, [first, second], lows, adapter_up_weight)

    b0 = lax.ppermute(same, "pool", [(0, 1), (1, 0)])
    a0 = x_mirror(other)
    b0, a0, mine = barrier((b0, a0, mine))
    mine = jnp.concatenate(mine, 0)
    partner = core_swap(mine)
    both0 = jnp.stack([b0, a0])
    both1, both3 = y_shift(both0, 1), y_shift(both0, -1)
    ranks = ADAPTERS * RANK
    down = jnp.transpose(output_down_weight, (1, 2, 0)).reshape(ranks, -1)
    up = output_up_weight.reshape(ranks, -1)
    keep = row_adapter_index[:, None]
    shares = project(info, keep, down, up, output_weight, [mine, partner])
    decoded = shares[0].astype(jnp.float32)
    for k, share in ((1, shares[1]), (2, shares[2]), (-1, shares[3])):
        decoded = decoded + z_shift(share, k).astype(jnp.float32)
    decoded = decoded.astype(jnp.bfloat16)
    both0, both1, both3, decoded = barrier((both0, both1, both3, decoded))
    b2, a2 = y_shift(both1[0], 1), y_shift(both3[1], -1)
    middle = [both0, both1, both3]
    theirs = [core_swap(v) for v in middle]
    b2, a2, theirs = barrier((b2, a2, theirs))
    theirs2 = [core_swap(b2), core_swap(a2)]
    kinds = ((0, 0), (1, 0), (0, 1), (1, 1), (0, 3), (1, 3))
    rest = ((0, 2), (1, 2))
    handed = place(info, kinds, rest, middle, theirs)
    handed = place(info, rest, (), [b2[None], a2[None]], [v[None] for v in theirs2], handed)
    return handed, decoded


def solution(mesh):
    fine = Mesh(mesh.devices.reshape(2, 2, 4, 2, 4), ("pool", "xh", "y", "core", "head"))
    seq = ("xh", "y", "core")
    every = ("pool",) + seq
    in_specs = (
        P("pool", seq, None),
        P(seq, None, "head"),
        P(seq, None),
        P(None, None, None, "head"),
        P("pool"),
        P(),
        P(every, "head"),
        P(every, None, None, "head"),
        P(every, None, "head"),
        P(every),
        P("pool"),
        P("head", seq),
        P("head", None, None),
        P(None, None, seq),
    )
    out_specs = (P(every, None, None, None, "head"), P(("pool", "head"), seq))
    return jax.shard_map(body, mesh=fine, in_specs=in_specs, out_specs=out_specs, check_vma=False)
```

```python
import functools

import jax
import jax.numpy as jnp
from jax import lax
from jax.experimental import pallas as pl
from jax.experimental.pallas import tpu as pltpu
from jax.sharding import Mesh
from jax.sharding import PartitionSpec as P

HEAD_DIM = 128
RANK = 16
ADAPTERS = 8
CAP = 2
REQ_POOL = 4
X_SLOTS = 3
MIB = 2**20


POOL, XH, Y, CORE, HEAD, DEST, ADAPTER = 0, 1, 2, 3, 4, 5, 13
VMEM = pl.BlockSpec(memory_space=pltpu.VMEM)
SMEM = pl.BlockSpec(memory_space=pltpu.SMEM)
ANY = pl.BlockSpec(memory_space=pl.ANY)
HBM = pl.BlockSpec(memory_space=pltpu.HBM)


def params(limit=8):
    return pltpu.CompilerParams(vmem_limit_bytes=limit * MIB)


def x_mirror(value):
    return lax.ppermute(value, ("pool", "xh"), [(i, 3 - i) for i in range(4)])


def x_shift(value, k):
    pairs = []
    for x in range(4):
        t = (x + k) % 4
        pairs.append(((x % 2) * 2 + x // 2, (t % 2) * 2 + t // 2))
    return lax.ppermute(value, ("pool", "xh"), pairs)


def y_shift(value, k):
    return lax.ppermute(value, "y", [(i, (i + k) % 4) for i in range(4)])


def xh_swap(value):
    return lax.ppermute(value, "xh", [(0, 1), (1, 0)])


def z_shift(value, k):
    return lax.ppermute(value, "head", [(i, (i + k) % 4) for i in range(4)])


def z_flip(value, mask):
    return lax.ppermute(value, "head", [(i, i ^ mask) for i in range(4)])


def core_swap(value):
    return lax.ppermute(value, "core", [(0, 1), (1, 0)])


def pack_kernel(info, w_hbm, d_hbm, k_ref, v_ref, w_ref, d_ref, sems):
    weight = pltpu.make_async_copy(w_hbm, w_ref, sems.at[0])
    down = pltpu.make_async_copy(d_hbm, d_ref, sems.at[1])
    weight.start()
    down.start()
    weight.wait()
    k_ref[...] = w_ref[:, 0, :]
    v_ref[0:256] = w_ref[pl.ds(pl.multiple_of(info[POOL] * 256, 256), 256), 1, :]
    column = lax.broadcasted_iota(jnp.int32, (256, 128), 0)
    lane = lax.broadcasted_iota(jnp.int32, (256, 128), 1)
    pick = (column == info[ADAPTER + info[HEAD]] * 32 + lane) & (lane < 32)
    down.wait()
    low = lax.dot_general(
        pick.astype(jnp.bfloat16),
        d_ref[...],
        (((0,), (1,)), ((), ())),
        preferred_element_type=jnp.float32,
    ).astype(jnp.bfloat16)
    v_ref[256:288] = low[0:32, 0:256]
    v_ref[288:320] = low[0:32, 256:512]


def pack(info, weight, down):
    return pl.pallas_call(
        pack_kernel,
        in_specs=[SMEM, HBM, HBM],
        out_specs=[VMEM, VMEM],
        out_shape=[
            jax.ShapeDtypeStruct((512, 256), jnp.bfloat16),
            jax.ShapeDtypeStruct((320, 256), jnp.bfloat16),
        ],
        scratch_shapes=[
            pltpu.VMEM(weight.shape, weight.dtype),
            pltpu.VMEM(down.shape, down.dtype),
            pltpu.SemaphoreType.DMA((2,)),
        ],
        compiler_params=params(),
        name="pack",
    )(info, weight, down)


ROWS_STEP = 12


def attend_kernel(offset, len_ref, q_ref, kv_ref, cur_ref, o_ref):
    first = pl.program_id(0) * ROWS_STEP + offset
    factor = HEAD_DIM**-0.5
    lane = lax.broadcasted_iota(jnp.int32, (8, 256), 1)
    is_key = (lane & 1) == 0
    scores, own = [], []
    for i in range(ROWS_STEP):
        n = len_ref[first + i]
        valid = is_key & (lane < 2 * n)
        for h in range(2):
            both = kv_ref[i, :, :, h * 128 : (h + 1) * 128].reshape(256, 128)
            q = q_ref[i, h * 8 : (h + 1) * 8, :]
            s = lax.dot_general(
                q, both, (((1,), (1,)), ((), ())), preferred_element_type=jnp.float32
            )
            scores.append(jnp.where(valid, s * factor, -1e30))
            k = cur_ref[i, 0:1, h * 128 : (h + 1) * 128].astype(jnp.float32)
            own.append(jnp.sum(q.astype(jnp.float32) * k, axis=-1, keepdims=True) * factor)
    s = jnp.concatenate(scores, 0)
    o = jnp.concatenate(own, 0)
    highest = jnp.maximum(jnp.max(s, axis=-1, keepdims=True), o)
    raw = jnp.exp(s - highest)
    own_raw = jnp.exp(o - highest)
    norm = jnp.sum(raw, axis=-1, keepdims=True) + own_raw
    weights = pltpu.roll(raw / norm, 1, 1).astype(jnp.bfloat16)
    own_weight = (own_raw / norm).astype(jnp.bfloat16).astype(jnp.float32)
    for i in range(ROWS_STEP):
        for h in range(2):
            both = kv_ref[i, :, :, h * 128 : (h + 1) * 128].reshape(256, 128)
            j = (i * 2 + h) * 8
            v = cur_ref[i, 1:2, h * 128 : (h + 1) * 128].astype(jnp.float32)
            mixed = jnp.dot(weights[j : j + 8], both, preferred_element_type=jnp.float32)
            mixed = mixed + own_weight[j : j + 8] * v
            o_ref[i, h * 8 : (h + 1) * 8, :] = mixed.astype(jnp.bfloat16)


def attend(query, cache, current, lengths, part, parts):
    rows, heads = query.shape[0] // parts, query.shape[1]
    first = part * (rows // ROWS_STEP)
    return pl.pallas_call(
        functools.partial(attend_kernel, first * ROWS_STEP),
        grid_spec=pltpu.PrefetchScalarGridSpec(
            num_scalar_prefetch=1,
            grid=(rows // ROWS_STEP,),
            in_specs=[
                pl.BlockSpec((ROWS_STEP, heads, 128), lambda g, n: (g + first, 0, 0)),
                pl.BlockSpec((ROWS_STEP, 128, 2, 256), lambda g, n: (g + first, 0, 0, 0)),
                pl.BlockSpec((ROWS_STEP, 2, 256), lambda g, n: (g + first, 0, 0)),
            ],
            out_specs=pl.BlockSpec((ROWS_STEP, heads, 128), lambda g, n: (g, 0, 0)),
        ),
        out_shape=jax.ShapeDtypeStruct((rows, heads, 128), jnp.bfloat16),
        compiler_params=params(),
        name="attend",
    )(lengths, query, cache, current)


def split_dot(low, up, dims=(((1,), (0,)), ((), ()))):
    high = low.astype(jnp.bfloat16)
    rest = (low - high.astype(jnp.float32)).astype(jnp.bfloat16)
    return lax.dot_general(high, up, dims, preferred_element_type=jnp.float32) + lax.dot_general(
        rest, up, dims, preferred_element_type=jnp.float32
    )


def x_order(x):
    return [x, (x + 3) & 3, (x + 2) & 3, (x + 1) & 3]


def low_kernel(info, prompt, own_ref, other_ref, out_ref):
    xh, y, core = info[XH], info[Y], info[CORE]
    rows = pl.ds(pl.multiple_of(info[HEAD] * 128, 128), 128)
    low = jnp.zeros((32, 128), jnp.float32)
    for n in range(2):
        ref, c_of = ((own_ref, core), (other_ref, 1 - core))[n]
        downs, tokens = [], []
        for i in range(16):
            side = xh if i < 8 else 1 - xh
            shard = side * 8 + x_order(y)[(i // 2) % 4] * 2 + c_of
            at = pl.multiple_of(shard * 512 + (i % 2) * 256, 256)
            tokens.append(prompt[rows, pl.ds(at, 256)])
            downs.append(ref[i * 32 : (i + 1) * 32])
        low = low + lax.dot_general(
            jnp.concatenate(downs, 1),
            jnp.concatenate(tokens, 1),
            (((1,), (1,)), ((), ())),
            preferred_element_type=jnp.float32,
        )
    out_ref[...] = low


def low_rank(info, tokens, own, other):
    return pl.pallas_call(
        low_kernel,
        in_specs=[SMEM, VMEM, VMEM, VMEM],
        out_specs=VMEM,
        out_shape=jax.ShapeDtypeStruct((32, 128), jnp.float32),
        compiler_params=params(),
        name="low_rank",
    )(info, tokens, own, other)


def add_products(pieces, fresh, info, prompt, blocks, outs):
    pool, xh, y, core = info[POOL], info[XH], info[Y], info[CORE]
    fresh = [fresh, fresh]
    for kv, partner, which, row, j in pieces:
        c_of = 1 - core if partner else core
        tokens = []
        if kv == 0:
            for side in (xh, 1 - xh):
                at = pl.multiple_of((side * 8 + x_order(y)[j] * 2 + c_of) * 512, 512)
                tokens.append(prompt[:, pl.ds(at, 512)])
        else:
            xi = x_order(2 * xh + pool)[j]
            for yi in x_order(y):
                at = ((xi >> 1) * 8 + yi * 2 + c_of) * 512 + (xi & 1) * 256
                tokens.append(prompt[:, pl.ds(pl.multiple_of(at, 256), 256)])
        part = jnp.dot(
            jnp.concatenate(tokens, 1),
            blocks[which][row : row + 1024],
            preferred_element_type=jnp.float32,
        )
        if fresh[kv]:
            outs[kv][...] = part
        else:
            outs[kv][...] += part
        fresh[kv] = False


def main_kernel(pieces, info, prompt, *refs):
    add_products(pieces, True, info, prompt, refs[:-2], refs[-2:])


def main_product(info, tokens, pieces, blocks):
    shape = jax.ShapeDtypeStruct((tokens.shape[0], 256), jnp.float32)
    return pl.pallas_call(
        functools.partial(main_kernel, pieces),
        in_specs=[SMEM] + [VMEM] * (1 + len(blocks)),
        out_specs=[VMEM, VMEM],
        out_shape=[shape, shape],
        compiler_params=params(),
        name="main_product",
    )(info, tokens, *blocks)


def finish_kernel(pieces, n_sums, info, prompt, *refs):
    n = len(refs) - 6 - 2 * n_sums
    blocks, sums = refs[:n], refs[n : n + 2 * n_sums]
    lows, up_ref, near_ref, far_ref, k_ref, v_ref = refs[n + 2 * n_sums :]
    pool, xh, z = info[POOL], info[XH], info[HEAD]
    for kv, ref in enumerate((k_ref, v_ref)):
        total = sums[kv][...]
        for m in range(1, n_sums):
            total = total + sums[2 * m + kv][...]
        ref[...] = total
    add_products(pieces, False, info, prompt, blocks, (k_ref, v_ref))
    owners = [info[DEST + pool * REQ_POOL + r] for r in range(REQ_POOL)]
    dims = (((0,), (0,)), ((), ()))
    for n in range(REQ_POOL):
        r = z ^ n
        a = info[ADAPTER + r]
        rows = pl.ds(pl.multiple_of(r * 128, 128), 128)
        low = lows[n * 32 : (n + 1) * 32]
        both = []
        for kv, ref in enumerate((k_ref, v_ref)):
            value = ref[rows, :] + split_dot(low[kv * 16 : (kv + 1) * 16], up_ref[a, kv], dims)
            both.append(value.astype(jnp.bfloat16))
        result = jnp.stack(both, axis=1)
        owner = info[DEST + pool * REQ_POOL + r]
        slot = jnp.int32(0)
        for q in range(REQ_POOL):
            slot = slot + (((owners[q] >> 3) == (owner >> 3)) & (q < r)).astype(jnp.int32)

        @pl.when((owner >> 3) == xh)
        def _():
            near_ref[slot] = result

        @pl.when((owner >> 3) != xh)
        def _():
            far_ref[slot] = result


def finish(info, tokens, pieces, blocks, sums, lows, up):
    shape = jax.ShapeDtypeStruct((X_SLOTS, 128, 2, 256), jnp.bfloat16)
    total = pltpu.VMEM((tokens.shape[0], 256), jnp.float32)
    flat = [v for pair in sums for v in pair]
    return pl.pallas_call(
        functools.partial(finish_kernel, pieces, len(sums)),
        in_specs=[SMEM] + [VMEM] * (3 + len(blocks) + len(flat)),
        out_specs=[VMEM, VMEM],
        out_shape=[shape, shape],
        scratch_shapes=[total, total],
        compiler_params=params(),
        name="finish",
    )(info, tokens, *blocks, *flat, lows, up)


def slots_of(info, pool, xh, owner):
    owners = [info[DEST + pool * REQ_POOL + r] for r in range(REQ_POOL)]
    index = [jnp.int32(0)] * CAP
    used = [jnp.int32(0)] * CAP
    place, mine = jnp.int32(0), jnp.int32(0)
    for r in range(REQ_POOL):
        hit = (owners[r] == owner).astype(jnp.int32)
        for j in range(CAP):
            here = hit * (mine == j).astype(jnp.int32)
            index[j] = index[j] + here * place
            used[j] = used[j] + here
        mine = mine + hit
        place = place + ((owners[r] >> 3) == xh).astype(jnp.int32)
    return index, used


def place_kernel(kinds, rest, sizes, info, *refs):
    n = len(sizes)
    at = [(i, b) for i, size in enumerate(sizes) for b in range(size)]
    ins, others = refs[:n], refs[n : 2 * n]
    out, zero, sems = refs[-3], refs[-2], refs[-1]
    xh, y, core = info[XH], info[Y], info[CORE]
    index, used = slots_of(info, 1 - info[POOL], xh, xh * 8 + y * 2 + core)
    if rest:
        zero[...] = jnp.zeros_like(zero)

    def spot(j, kind, c_of):
        side = xh if kind[0] == 0 else 1 - xh
        token = (side * 8 + x_order(y)[kind[1]] * 2 + c_of) * 128
        return out.at[0, j, pl.ds(pl.multiple_of(token, 128), 128)]

    def transfers(j):
        full = []
        for b, kind in enumerate(kinds):
            i, k = at[b]
            full.append((ins[i].at[k, index[j]], spot(j, kind, core)))
            full.append((others[i].at[k, index[j]], spot(j, kind, 1 - core)))
        return [
            pltpu.make_async_copy(src, dst, sems.at[j, i]) for i, (src, dst) in enumerate(full)
        ]

    def clears(j):
        spots = [spot(j, kind, c) for kind in kinds + rest for c in (core, 1 - core)]
        return [pltpu.make_async_copy(zero, dst, sems.at[j, i]) for i, dst in enumerate(spots)]

    for step in ("start", "wait"):
        for j in range(CAP):

            @pl.when(used[j] == 1)
            def _():
                for c in transfers(j):
                    getattr(c, step)()

            if rest:

                @pl.when(used[j] == 0)
                def _():
                    for c in clears(j):
                        getattr(c, step)()


def place(info, kinds, rest, parts, others, out=None):
    shape = jax.ShapeDtypeStruct((1, CAP, 2048, 2, 256), jnp.bfloat16)
    ins = [info, *parts, *others] + ([] if out is None else [out])
    return pl.pallas_call(
        functools.partial(place_kernel, kinds, rest, tuple(p.shape[0] for p in parts)),
        in_specs=[SMEM] + [VMEM] * (len(parts) + len(others)) + ([] if out is None else [ANY]),
        out_specs=ANY,
        out_shape=shape,
        scratch_shapes=[
            pltpu.VMEM((128, 2, 256), jnp.bfloat16),
            pltpu.SemaphoreType.DMA((CAP, 16)),
        ],
        input_output_aliases={} if out is None else {len(ins) - 1: 0},
        compiler_params=params(),
        name="place",
    )(*ins)


def project_kernel(info, keep, down, up, w_ref, *refs):
    ins, outs, res = refs[:2], refs[2:6], refs[6]
    xh, y, core, z = info[XH], info[Y], info[CORE], info[HEAD]
    value = jnp.concatenate([ref[...] for ref in ins], 0)
    out = jnp.dot(value, w_ref[...], preferred_element_type=jnp.float32)
    low = lax.dot_general(
        value, down[...], (((1,), (1,)), ((), ())), preferred_element_type=jnp.float32
    )
    owner = lax.broadcasted_iota(jnp.int32, (48, ADAPTERS * RANK), 1) >> 4
    spots, lows = [], []
    for b in range(8):
        row, c_of = x_order(y)[b % 4], core if b < 4 else 1 - core
        for i in range(2):
            side = xh if i == 0 else 1 - xh
            at = pl.ds(pl.multiple_of((side * 8 + row * 2 + c_of) * 48, 16), 48)
            n = b * 96 + i * 48
            spots.append(at)
            lows.append(jnp.where(keep[at, :] == owner, low[n : n + 48], 0.0))
    out = (out + split_dot(jnp.concatenate(lows, 0), up[...])).astype(jnp.bfloat16)
    for n in range(16):
        res[spots[n], :] = out[n * 48 : (n + 1) * 48]
    for n in range(4):
        outs[n][...] = res[pl.ds(pl.multiple_of(((z + n) & 3) * 192, 64), 192), :]


def project(info, keep, down, up, weight, parts):
    rows, width = 768, weight.shape[1]
    return pl.pallas_call(
        project_kernel,
        in_specs=[SMEM] + [VMEM] * 6,
        out_specs=[VMEM] * 4,
        out_shape=[jax.ShapeDtypeStruct((rows // 4, width), jnp.bfloat16)] * 4,
        scratch_shapes=[pltpu.VMEM((rows, width), jnp.bfloat16)],
        compiler_params=params(),
        name="project",
    )(info, keep, down, up, weight, *parts)


def ring(value, shift):
    return [value, shift(value, 1), shift(value, 2), shift(value, -1)]


def body(
    prompt,
    key_value_weight,
    adapter_down_weight,
    adapter_up_weight,
    request_adapter_index,
    destination,
    rotated_query,
    key_value_cache,
    current_key_value,
    cached_length,
    row_adapter_index,
    output_weight,
    output_down_weight,
    output_up_weight,
):
    barrier = lax.optimization_barrier
    axes = ("pool", "xh", "y", "core", "head")
    place_of = jnp.stack([lax.axis_index(a) for a in axes]).astype(jnp.int32)
    info = jnp.concatenate([place_of, destination, request_adapter_index])
    tokens = prompt.reshape(-1, prompt.shape[2])
    tokens = pltpu.with_memory_space_constraint(tokens, pltpu.VMEM)
    rows, heads = rotated_query.shape[0], rotated_query.shape[1] // HEAD_DIM
    query = rotated_query.reshape(rows, heads, HEAD_DIM)

    cache = pltpu.with_memory_space_constraint(key_value_cache, pltpu.HBM)
    keys, values = pack(
        info,
        pltpu.with_memory_space_constraint(key_value_weight, pltpu.HBM),
        pltpu.with_memory_space_constraint(adapter_down_weight, pltpu.HBM),
    )
    keys_across = x_mirror(keys)
    ring_values = ring(values, y_shift)
    keys, keys_across, ring_values, cached_length = barrier(
        (keys, keys_across, ring_values, cached_length)
    )
    key0 = jnp.concatenate([keys, keys_across], 0)
    value0 = jnp.concatenate([v[:256] for v in ring_values], 0)
    down0 = jnp.concatenate([v[256:] for v in ring_values], 0)
    key1, key3 = y_shift(key0, 1), y_shift(key0, -1)
    value1, value3 = x_shift(value0, 1), x_shift(value0, -1)
    down_own = jnp.concatenate([down0, xh_swap(down0)], 0)
    attended = attend(query, cache, current_key_value, cached_length, 0, 1)
    attended = attended.reshape(rows, heads * HEAD_DIM)
    key0, value0, key1, key3, value1, value3, down_own, attended = barrier(
        (key0, value0, key1, key3, value1, value3, down_own, attended)
    )
    key2, value2 = y_shift(key0, 2), x_shift(value0, 2)
    blocks = [key0, value0, key1, key3, value1, value3]
    order = ((0, 0), (1, 0), (0, 1), (0, 3), (1, 1), (1, 3))
    theirs = core_swap(jnp.concatenate(blocks, 0))
    across = xh_swap(attended)
    low = low_rank(info, tokens, down_own, core_swap(down_own))
    pair = jnp.concatenate([low, z_flip(low, 1)], 0)
    lows = jnp.concatenate([pair, z_flip(pair, 2)], 0)
    pieces = tuple((kv, 0, n, 0, j) for n, (kv, j) in enumerate(order))
    first = main_product(info, tokens, pieces, blocks)
    pieces = tuple((kv, 1, 0, 1024 * n, j) for n, (kv, j) in enumerate(order))
    second = main_product(info, tokens, pieces, [theirs])
    key2, value2, first, second, across, lows, attended = barrier(
        (key2, value2, first, second, across, lows, attended)
    )
    mine = ring(jnp.concatenate([attended, across], 0), y_shift)
    last = [key2, value2, core_swap(key2), core_swap(value2)]
    pieces = ((0, 0, 0, 0, 2), (1, 0, 1, 0, 2), (0, 1, 2, 0, 2), (1, 1, 3, 0, 2))
    same, other = finish(info, tokens, pieces, last, [first, second], lows, adapter_up_weight)

    b0 = lax.ppermute(same, "pool", [(0, 1), (1, 0)])
    a0 = x_mirror(other)
    b0, a0, mine = barrier((b0, a0, mine))
    mine = jnp.concatenate(mine, 0)
    partner = core_swap(mine)
    both0 = jnp.stack([b0, a0])
    both1, both3 = y_shift(both0, 1), y_shift(both0, -1)
    ranks = ADAPTERS * RANK
    down = jnp.transpose(output_down_weight, (1, 2, 0)).reshape(ranks, -1)
    up = output_up_weight.reshape(ranks, -1)
    keep = row_adapter_index[:, None]
    shares = project(info, keep, down, up, output_weight, [mine, partner])
    decoded = shares[0].astype(jnp.float32)
    for k, share in ((1, shares[1]), (2, shares[2]), (-1, shares[3])):
        decoded = decoded + z_shift(share, k).astype(jnp.float32)
    decoded = decoded.astype(jnp.bfloat16)
    both1, both3 = barrier((both1, both3))
    b2, a2 = y_shift(both1[0], 1), y_shift(both3[1], -1)
    middle, decoded = barrier(([both0, both1, both3], decoded))
    theirs = [core_swap(v) for v in middle]
    b2, a2, theirs = barrier((b2, a2, theirs))
    theirs2 = [core_swap(b2), core_swap(a2)]
    kinds = ((0, 0), (1, 0), (0, 1), (1, 1), (0, 3), (1, 3))
    rest = ((0, 2), (1, 2))
    handed = place(info, kinds, rest, middle, theirs)
    handed = place(info, rest, (), [b2[None], a2[None]], [v[None] for v in theirs2], handed)
    return handed, decoded


def solution(mesh):
    fine = Mesh(mesh.devices.reshape(2, 2, 4, 2, 4), ("pool", "xh", "y", "core", "head"))
    seq = ("xh", "y", "core")
    every = ("pool",) + seq
    in_specs = (
        P("pool", seq, None),
        P(seq, None, "head"),
        P(seq, None),
        P(None, None, None, "head"),
        P("pool"),
        P(),
        P(every, "head"),
        P(every, None, None, "head"),
        P(every, None, "head"),
        P(every),
        P("pool"),
        P("head", seq),
        P("head", None, None),
        P(None, None, seq),
    )
    out_specs = (P(every, None, None, None, "head"), P(("pool", "head"), seq))
    return jax.shard_map(body, mesh=fine, in_specs=in_specs, out_specs=out_specs, check_vma=False)
```

```python
import functools

import jax
import jax.numpy as jnp
from jax import lax
from jax.experimental import pallas as pl
from jax.experimental.pallas import tpu as pltpu
from jax.sharding import Mesh
from jax.sharding import PartitionSpec as P

HEAD_DIM = 128
RANK = 16
ADAPTERS = 8
CAP = 2
REQ_POOL = 4
X_SLOTS = 3
MIB = 2**20


POOL, XH, Y, CORE, HEAD, DEST, ADAPTER = 0, 1, 2, 3, 4, 5, 13
VMEM = pl.BlockSpec(memory_space=pltpu.VMEM)
SMEM = pl.BlockSpec(memory_space=pltpu.SMEM)
ANY = pl.BlockSpec(memory_space=pl.ANY)
HBM = pl.BlockSpec(memory_space=pltpu.HBM)


def params(limit=8):
    return pltpu.CompilerParams(vmem_limit_bytes=limit * MIB)


def x_mirror(value):
    return lax.ppermute(value, ("pool", "xh"), [(i, 3 - i) for i in range(4)])


def x_shift(value, k):
    pairs = []
    for x in range(4):
        t = (x + k) % 4
        pairs.append(((x % 2) * 2 + x // 2, (t % 2) * 2 + t // 2))
    return lax.ppermute(value, ("pool", "xh"), pairs)


def y_shift(value, k):
    return lax.ppermute(value, "y", [(i, (i + k) % 4) for i in range(4)])


def xh_swap(value):
    return lax.ppermute(value, "xh", [(0, 1), (1, 0)])


def z_shift(value, k):
    return lax.ppermute(value, "head", [(i, (i + k) % 4) for i in range(4)])


def z_flip(value, mask):
    return lax.ppermute(value, "head", [(i, i ^ mask) for i in range(4)])


def core_swap(value):
    return lax.ppermute(value, "core", [(0, 1), (1, 0)])


def pack_kernel(info, w_hbm, d_hbm, k_ref, v_ref, w_ref, d_ref, sems):
    weight = pltpu.make_async_copy(w_hbm, w_ref, sems.at[0])
    down = pltpu.make_async_copy(d_hbm, d_ref, sems.at[1])
    weight.start()
    down.start()
    weight.wait()
    k_ref[...] = w_ref[:, 0, :]
    v_ref[0:256] = w_ref[pl.ds(pl.multiple_of(info[POOL] * 256, 256), 256), 1, :]
    column = lax.broadcasted_iota(jnp.int32, (256, 128), 0)
    lane = lax.broadcasted_iota(jnp.int32, (256, 128), 1)
    pick = (column == info[ADAPTER + info[HEAD]] * 32 + lane) & (lane < 32)
    down.wait()
    low = lax.dot_general(
        pick.astype(jnp.bfloat16),
        d_ref[...],
        (((0,), (1,)), ((), ())),
        preferred_element_type=jnp.float32,
    ).astype(jnp.bfloat16)
    v_ref[256:288] = low[0:32, 0:256]
    v_ref[288:320] = low[0:32, 256:512]


def pack(info, weight, down):
    return pl.pallas_call(
        pack_kernel,
        in_specs=[SMEM, HBM, HBM],
        out_specs=[VMEM, VMEM],
        out_shape=[
            jax.ShapeDtypeStruct((512, 256), jnp.bfloat16),
            jax.ShapeDtypeStruct((320, 256), jnp.bfloat16),
        ],
        scratch_shapes=[
            pltpu.VMEM(weight.shape, weight.dtype),
            pltpu.VMEM(down.shape, down.dtype),
            pltpu.SemaphoreType.DMA((2,)),
        ],
        compiler_params=params(),
        name="pack",
    )(info, weight, down)


ROWS_STEP = 12


def attend_kernel(offset, len_ref, q_ref, kv_ref, cur_ref, o_ref):
    first = pl.program_id(0) * ROWS_STEP + offset
    factor = HEAD_DIM**-0.5
    lane = lax.broadcasted_iota(jnp.int32, (8, 256), 1)
    is_key = (lane & 1) == 0
    scores, own = [], []
    for i in range(ROWS_STEP):
        n = len_ref[first + i]
        valid = is_key & (lane < 2 * n)
        for h in range(2):
            both = kv_ref[i, :, :, h * 128 : (h + 1) * 128].reshape(256, 128)
            q = q_ref[i, h * 8 : (h + 1) * 8, :]
            s = lax.dot_general(
                q, both, (((1,), (1,)), ((), ())), preferred_element_type=jnp.float32
            )
            scores.append(jnp.where(valid, s * factor, -1e30))
            k = cur_ref[i, 0:1, h * 128 : (h + 1) * 128].astype(jnp.float32)
            own.append(jnp.sum(q.astype(jnp.float32) * k, axis=-1, keepdims=True) * factor)
    s = jnp.concatenate(scores, 0)
    o = jnp.concatenate(own, 0)
    highest = jnp.maximum(jnp.max(s, axis=-1, keepdims=True), o)
    raw = jnp.exp(s - highest)
    own_raw = jnp.exp(o - highest)
    norm = jnp.sum(raw, axis=-1, keepdims=True) + own_raw
    weights = pltpu.roll(raw / norm, 1, 1).astype(jnp.bfloat16)
    own_weight = (own_raw / norm).astype(jnp.bfloat16).astype(jnp.float32)
    for i in range(ROWS_STEP):
        for h in range(2):
            both = kv_ref[i, :, :, h * 128 : (h + 1) * 128].reshape(256, 128)
            j = (i * 2 + h) * 8
            v = cur_ref[i, 1:2, h * 128 : (h + 1) * 128].astype(jnp.float32)
            mixed = jnp.dot(weights[j : j + 8], both, preferred_element_type=jnp.float32)
            mixed = mixed + own_weight[j : j + 8] * v
            o_ref[i, h * 8 : (h + 1) * 8, :] = mixed.astype(jnp.bfloat16)


def attend(query, cache, current, lengths, part, parts):
    rows, heads = query.shape[0] // parts, query.shape[1]
    first = part * (rows // ROWS_STEP)
    return pl.pallas_call(
        functools.partial(attend_kernel, first * ROWS_STEP),
        grid_spec=pltpu.PrefetchScalarGridSpec(
            num_scalar_prefetch=1,
            grid=(rows // ROWS_STEP,),
            in_specs=[
                pl.BlockSpec((ROWS_STEP, heads, 128), lambda g, n: (g + first, 0, 0)),
                pl.BlockSpec((ROWS_STEP, 128, 2, 256), lambda g, n: (g + first, 0, 0, 0)),
                pl.BlockSpec((ROWS_STEP, 2, 256), lambda g, n: (g + first, 0, 0)),
            ],
            out_specs=pl.BlockSpec((ROWS_STEP, heads, 128), lambda g, n: (g, 0, 0)),
        ),
        out_shape=jax.ShapeDtypeStruct((rows, heads, 128), jnp.bfloat16),
        compiler_params=params(),
        name="attend",
    )(lengths, query, cache, current)


def split_dot(low, up, dims=(((1,), (0,)), ((), ()))):
    high = low.astype(jnp.bfloat16)
    rest = (low - high.astype(jnp.float32)).astype(jnp.bfloat16)
    return lax.dot_general(high, up, dims, preferred_element_type=jnp.float32) + lax.dot_general(
        rest, up, dims, preferred_element_type=jnp.float32
    )


def x_order(x):
    return [x, (x + 3) & 3, (x + 2) & 3, (x + 1) & 3]


def low_kernel(info, prompt, own_ref, other_ref, out_ref):
    xh, y, core = info[XH], info[Y], info[CORE]
    rows = pl.ds(pl.multiple_of(info[HEAD] * 128, 128), 128)
    low = jnp.zeros((32, 128), jnp.float32)
    for n in range(2):
        ref, c_of = ((own_ref, core), (other_ref, 1 - core))[n]
        downs, tokens = [], []
        for i in range(16):
            side = xh if i < 8 else 1 - xh
            shard = side * 8 + x_order(y)[(i // 2) % 4] * 2 + c_of
            at = pl.multiple_of(shard * 512 + (i % 2) * 256, 256)
            tokens.append(prompt[rows, pl.ds(at, 256)])
            downs.append(ref[i * 32 : (i + 1) * 32])
        low = low + lax.dot_general(
            jnp.concatenate(downs, 1),
            jnp.concatenate(tokens, 1),
            (((1,), (1,)), ((), ())),
            preferred_element_type=jnp.float32,
        )
    out_ref[...] = low


def low_rank(info, tokens, own, other):
    return pl.pallas_call(
        low_kernel,
        in_specs=[SMEM, VMEM, VMEM, VMEM],
        out_specs=VMEM,
        out_shape=jax.ShapeDtypeStruct((32, 128), jnp.float32),
        compiler_params=params(),
        name="low_rank",
    )(info, tokens, own, other)


def add_products(pieces, fresh, info, prompt, blocks, outs):
    pool, xh, y, core = info[POOL], info[XH], info[Y], info[CORE]
    fresh = [fresh, fresh]
    for kv, partner, which, row, j in pieces:
        c_of = 1 - core if partner else core
        tokens = []
        if kv == 0:
            for side in (xh, 1 - xh):
                at = pl.multiple_of((side * 8 + x_order(y)[j] * 2 + c_of) * 512, 512)
                tokens.append(prompt[:, pl.ds(at, 512)])
        else:
            xi = x_order(2 * xh + pool)[j]
            for yi in x_order(y):
                at = ((xi >> 1) * 8 + yi * 2 + c_of) * 512 + (xi & 1) * 256
                tokens.append(prompt[:, pl.ds(pl.multiple_of(at, 256), 256)])
        part = jnp.dot(
            jnp.concatenate(tokens, 1),
            blocks[which][row : row + 1024],
            preferred_element_type=jnp.float32,
        )
        if fresh[kv]:
            outs[kv][...] = part
        else:
            outs[kv][...] += part
        fresh[kv] = False


def main_kernel(pieces, info, prompt, *refs):
    add_products(pieces, True, info, prompt, refs[:-2], refs[-2:])


def main_product(info, tokens, pieces, blocks):
    shape = jax.ShapeDtypeStruct((tokens.shape[0], 256), jnp.float32)
    return pl.pallas_call(
        functools.partial(main_kernel, pieces),
        in_specs=[SMEM] + [VMEM] * (1 + len(blocks)),
        out_specs=[VMEM, VMEM],
        out_shape=[shape, shape],
        compiler_params=params(),
        name="main_product",
    )(info, tokens, *blocks)


def finish_kernel(pieces, n_sums, info, prompt, *refs):
    n = len(refs) - 6 - 2 * n_sums
    blocks, sums = refs[:n], refs[n : n + 2 * n_sums]
    lows, up_ref, near_ref, far_ref, k_ref, v_ref = refs[n + 2 * n_sums :]
    pool, xh, z = info[POOL], info[XH], info[HEAD]
    for kv, ref in enumerate((k_ref, v_ref)):
        total = sums[kv][...]
        for m in range(1, n_sums):
            total = total + sums[2 * m + kv][...]
        ref[...] = total
    add_products(pieces, False, info, prompt, blocks, (k_ref, v_ref))
    owners = [info[DEST + pool * REQ_POOL + r] for r in range(REQ_POOL)]
    dims = (((0,), (0,)), ((), ()))
    for n in range(REQ_POOL):
        r = z ^ n
        a = info[ADAPTER + r]
        rows = pl.ds(pl.multiple_of(r * 128, 128), 128)
        low = lows[n * 32 : (n + 1) * 32]
        both = []
        for kv, ref in enumerate((k_ref, v_ref)):
            value = ref[rows, :] + split_dot(low[kv * 16 : (kv + 1) * 16], up_ref[a, kv], dims)
            both.append(value.astype(jnp.bfloat16))
        result = jnp.stack(both, axis=1)
        owner = info[DEST + pool * REQ_POOL + r]
        slot = jnp.int32(0)
        for q in range(REQ_POOL):
            slot = slot + (((owners[q] >> 3) == (owner >> 3)) & (q < r)).astype(jnp.int32)

        @pl.when((owner >> 3) == xh)
        def _():
            near_ref[slot] = result

        @pl.when((owner >> 3) != xh)
        def _():
            far_ref[slot] = result


def finish(info, tokens, pieces, blocks, sums, lows, up):
    shape = jax.ShapeDtypeStruct((X_SLOTS, 128, 2, 256), jnp.bfloat16)
    total = pltpu.VMEM((tokens.shape[0], 256), jnp.float32)
    flat = [v for pair in sums for v in pair]
    return pl.pallas_call(
        functools.partial(finish_kernel, pieces, len(sums)),
        in_specs=[SMEM] + [VMEM] * (3 + len(blocks) + len(flat)),
        out_specs=[VMEM, VMEM],
        out_shape=[shape, shape],
        scratch_shapes=[total, total],
        compiler_params=params(),
        name="finish",
    )(info, tokens, *blocks, *flat, lows, up)


def slots_of(info, pool, xh, owner):
    owners = [info[DEST + pool * REQ_POOL + r] for r in range(REQ_POOL)]
    index = [jnp.int32(0)] * CAP
    used = [jnp.int32(0)] * CAP
    place, mine = jnp.int32(0), jnp.int32(0)
    for r in range(REQ_POOL):
        hit = (owners[r] == owner).astype(jnp.int32)
        for j in range(CAP):
            here = hit * (mine == j).astype(jnp.int32)
            index[j] = index[j] + here * place
            used[j] = used[j] + here
        mine = mine + hit
        place = place + ((owners[r] >> 3) == xh).astype(jnp.int32)
    return index, used


def place_kernel(kinds, rest, sizes, info, *refs):
    n = len(sizes)
    at = [(i, b) for i, size in enumerate(sizes) for b in range(size)]
    ins, others = refs[:n], refs[n : 2 * n]
    out, zero, sems = refs[-3], refs[-2], refs[-1]
    xh, y, core = info[XH], info[Y], info[CORE]
    index, used = slots_of(info, 1 - info[POOL], xh, xh * 8 + y * 2 + core)
    if rest:
        zero[...] = jnp.zeros_like(zero)

    def spot(j, kind, c_of):
        side = xh if kind[0] == 0 else 1 - xh
        token = (side * 8 + x_order(y)[kind[1]] * 2 + c_of) * 128
        return out.at[0, j, pl.ds(pl.multiple_of(token, 128), 128)]

    def transfers(j):
        full = []
        for b, kind in enumerate(kinds):
            i, k = at[b]
            full.append((ins[i].at[k, index[j]], spot(j, kind, core)))
            full.append((others[i].at[k, index[j]], spot(j, kind, 1 - core)))
        return [
            pltpu.make_async_copy(src, dst, sems.at[j, i]) for i, (src, dst) in enumerate(full)
        ]

    def clears(j):
        spots = [spot(j, kind, c) for kind in kinds + rest for c in (core, 1 - core)]
        return [pltpu.make_async_copy(zero, dst, sems.at[j, i]) for i, dst in enumerate(spots)]

    for step in ("start", "wait"):
        for j in range(CAP):

            @pl.when(used[j] == 1)
            def _():
                for c in transfers(j):
                    getattr(c, step)()

            if rest:

                @pl.when(used[j] == 0)
                def _():
                    for c in clears(j):
                        getattr(c, step)()


def place(info, kinds, rest, parts, others, out=None):
    shape = jax.ShapeDtypeStruct((1, CAP, 2048, 2, 256), jnp.bfloat16)
    ins = [info, *parts, *others] + ([] if out is None else [out])
    return pl.pallas_call(
        functools.partial(place_kernel, kinds, rest, tuple(p.shape[0] for p in parts)),
        in_specs=[SMEM] + [VMEM] * (len(parts) + len(others)) + ([] if out is None else [ANY]),
        out_specs=ANY,
        out_shape=shape,
        scratch_shapes=[
            pltpu.VMEM((128, 2, 256), jnp.bfloat16),
            pltpu.SemaphoreType.DMA((CAP, 16)),
        ],
        input_output_aliases={} if out is None else {len(ins) - 1: 0},
        compiler_params=params(),
        name="place",
    )(*ins)


def project_kernel(last, info, keep, down, up, w_ref, rows_ref, *refs):
    xh, y, core, z = info[XH], info[Y], info[CORE], info[HEAD]
    value = rows_ref[...]
    out = jnp.dot(value, w_ref[...], preferred_element_type=jnp.float32)
    low = lax.dot_general(
        value, down[...], (((1,), (1,)), ((), ())), preferred_element_type=jnp.float32
    )
    owner = lax.broadcasted_iota(jnp.int32, (48, ADAPTERS * RANK), 1) >> 4

    def spot(b, c_of):
        side = 1 - xh if b % 2 else xh
        at = (side * 8 + x_order(y)[b // 2] * 2 + c_of) * 48
        return pl.ds(pl.multiple_of(at, 16), 48)

    c_of = 1 - core if last else core
    lows = [
        jnp.where(keep[spot(b, c_of), :] == owner, low[b * 48 : (b + 1) * 48], 0.0)
        for b in range(8)
    ]
    out = (out + split_dot(jnp.concatenate(lows, 0), up[...])).astype(jnp.bfloat16)
    if not last:
        refs[0][...] = out
        return
    first, outs, res = refs[0], refs[1:5], refs[5]
    for b in range(8):
        res[spot(b, core), :] = first[b * 48 : (b + 1) * 48]
        res[spot(b, 1 - core), :] = out[b * 48 : (b + 1) * 48]
    for n in range(4):
        outs[n][...] = res[pl.ds(pl.multiple_of(((z + n) & 3) * 192, 64), 192), :]


def project(info, keep, down, up, weight, rows, first=None):
    last, bf = first is not None, jnp.bfloat16
    count, width = rows.shape[0], weight.shape[1]
    shares = [jax.ShapeDtypeStruct((count // 2, width), bf)] * 4
    return pl.pallas_call(
        functools.partial(project_kernel, last),
        in_specs=[SMEM] + [VMEM] * (6 if last else 5),
        out_specs=[VMEM] * 4 if last else VMEM,
        out_shape=shares if last else jax.ShapeDtypeStruct((count, width), bf),
        scratch_shapes=[pltpu.VMEM((2 * count, width), bf)] if last else [],
        compiler_params=params(),
        name="project",
    )(info, keep, down, up, weight, rows, *([first] if last else []))


def ring(value, shift):
    return [value, shift(value, 1), shift(value, 2), shift(value, -1)]


def body(
    prompt,
    key_value_weight,
    adapter_down_weight,
    adapter_up_weight,
    request_adapter_index,
    destination,
    rotated_query,
    key_value_cache,
    current_key_value,
    cached_length,
    row_adapter_index,
    output_weight,
    output_down_weight,
    output_up_weight,
):
    barrier = lax.optimization_barrier
    axes = ("pool", "xh", "y", "core", "head")
    place_of = jnp.stack([lax.axis_index(a) for a in axes]).astype(jnp.int32)
    info = jnp.concatenate([place_of, destination, request_adapter_index])
    tokens = prompt.reshape(-1, prompt.shape[2])
    tokens = pltpu.with_memory_space_constraint(tokens, pltpu.VMEM)
    rows, heads = rotated_query.shape[0], rotated_query.shape[1] // HEAD_DIM
    query = rotated_query.reshape(rows, heads, HEAD_DIM)

    cache = pltpu.with_memory_space_constraint(key_value_cache, pltpu.HBM)
    keys, values = pack(
        info,
        pltpu.with_memory_space_constraint(key_value_weight, pltpu.HBM),
        pltpu.with_memory_space_constraint(adapter_down_weight, pltpu.HBM),
    )
    keys_across = x_mirror(keys)
    ring_values = ring(values, y_shift)
    keys, keys_across, ring_values, cached_length = barrier(
        (keys, keys_across, ring_values, cached_length)
    )
    key0 = jnp.concatenate([keys, keys_across], 0)
    value0 = jnp.concatenate([v[:256] for v in ring_values], 0)
    down0 = jnp.concatenate([v[256:] for v in ring_values], 0)
    key1, key3 = y_shift(key0, 1), y_shift(key0, -1)
    value1, value3 = x_shift(value0, 1), x_shift(value0, -1)
    down_own = jnp.concatenate([down0, xh_swap(down0)], 0)
    attended = attend(query, cache, current_key_value, cached_length, 0, 1)
    attended = attended.reshape(rows, heads * HEAD_DIM)
    key0, value0, key1, key3, value1, value3, down_own, attended = barrier(
        (key0, value0, key1, key3, value1, value3, down_own, attended)
    )
    key2, value2 = y_shift(key0, 2), x_shift(value0, 2)
    blocks = [key0, value0, key1, key3, value1, value3]
    order = ((0, 0), (1, 0), (0, 1), (0, 3), (1, 1), (1, 3))
    theirs = core_swap(jnp.concatenate(blocks, 0))
    across = xh_swap(attended)
    low = low_rank(info, tokens, down_own, core_swap(down_own))
    pair = jnp.concatenate([low, z_flip(low, 1)], 0)
    lows = jnp.concatenate([pair, z_flip(pair, 2)], 0)
    pieces = tuple((kv, 0, n, 0, j) for n, (kv, j) in enumerate(order))
    first = main_product(info, tokens, pieces, blocks)
    pieces = tuple((kv, 1, 0, 1024 * n, j) for n, (kv, j) in enumerate(order))
    second = main_product(info, tokens, pieces, [theirs])
    key2, value2, first, second, across, lows, attended = barrier(
        (key2, value2, first, second, across, lows, attended)
    )
    mine = ring(jnp.concatenate([attended, across], 0), y_shift)
    last = [key2, value2, core_swap(key2), core_swap(value2)]
    pieces = ((0, 0, 0, 0, 2), (1, 0, 1, 0, 2), (0, 1, 2, 0, 2), (1, 1, 3, 0, 2))
    same, other = finish(info, tokens, pieces, last, [first, second], lows, adapter_up_weight)

    b0 = lax.ppermute(same, "pool", [(0, 1), (1, 0)])
    a0 = x_mirror(other)
    b0, a0, mine = barrier((b0, a0, mine))
    mine = jnp.concatenate(mine, 0)
    partner = core_swap(mine)
    both0 = jnp.stack([b0, a0])
    both1, both3 = y_shift(both0, 1), y_shift(both0, -1)
    ranks = ADAPTERS * RANK
    down = jnp.transpose(output_down_weight, (1, 2, 0)).reshape(ranks, -1)
    up = output_up_weight.reshape(ranks, -1)
    keep = row_adapter_index[:, None]
    shares = project(info, keep, down, up, output_weight, mine)
    shares = project(info, keep, down, up, output_weight, partner, shares)
    decoded = shares[0].astype(jnp.float32)
    for k, share in ((1, shares[1]), (2, shares[2]), (-1, shares[3])):
        decoded = decoded + z_shift(share, k).astype(jnp.float32)
    decoded = decoded.astype(jnp.bfloat16)
    both1, both3 = barrier((both1, both3))
    b2, a2 = y_shift(both1[0], 1), y_shift(both3[1], -1)
    middle, decoded = barrier(([both0, both1, both3], decoded))
    theirs = [core_swap(v) for v in middle]
    b2, a2, theirs = barrier((b2, a2, theirs))
    theirs2 = [core_swap(b2), core_swap(a2)]
    kinds = ((0, 0), (1, 0), (0, 1), (1, 1), (0, 3), (1, 3))
    rest = ((0, 2), (1, 2))
    handed = place(info, kinds, rest, middle, theirs)
    handed = place(info, rest, (), [b2[None], a2[None]], [v[None] for v in theirs2], handed)
    return handed, decoded


def solution(mesh):
    fine = Mesh(mesh.devices.reshape(2, 2, 4, 2, 4), ("pool", "xh", "y", "core", "head"))
    seq = ("xh", "y", "core")
    every = ("pool",) + seq
    in_specs = (
        P("pool", seq, None),
        P(seq, None, "head"),
        P(seq, None),
        P(None, None, None, "head"),
        P("pool"),
        P(),
        P(every, "head"),
        P(every, None, None, "head"),
        P(every, None, "head"),
        P(every),
        P("pool"),
        P("head", seq),
        P("head", None, None),
        P(None, None, seq),
    )
    out_specs = (P(every, None, None, None, "head"), P(("pool", "head"), seq))
    return jax.shard_map(body, mesh=fine, in_specs=in_specs, out_specs=out_specs, check_vma=False)
```

```python
import functools

import jax
import jax.numpy as jnp
from jax import lax
from jax.experimental import pallas as pl
from jax.experimental.pallas import tpu as pltpu
from jax.sharding import Mesh
from jax.sharding import PartitionSpec as P

HEAD_DIM = 128
RANK = 16
ADAPTERS = 8
CAP = 2
REQ_POOL = 4
X_SLOTS = 3
MIB = 2**20


POOL, XH, Y, CORE, HEAD, DEST, ADAPTER = 0, 1, 2, 3, 4, 5, 13
VMEM = pl.BlockSpec(memory_space=pltpu.VMEM)
SMEM = pl.BlockSpec(memory_space=pltpu.SMEM)
ANY = pl.BlockSpec(memory_space=pl.ANY)
HBM = pl.BlockSpec(memory_space=pltpu.HBM)


def params(limit=8):
    return pltpu.CompilerParams(vmem_limit_bytes=limit * MIB)


def x_mirror(value):
    return lax.ppermute(value, ("pool", "xh"), [(i, 3 - i) for i in range(4)])


def x_shift(value, k):
    pairs = []
    for x in range(4):
        t = (x + k) % 4
        pairs.append(((x % 2) * 2 + x // 2, (t % 2) * 2 + t // 2))
    return lax.ppermute(value, ("pool", "xh"), pairs)


def y_shift(value, k):
    return lax.ppermute(value, "y", [(i, (i + k) % 4) for i in range(4)])


def xh_swap(value):
    return lax.ppermute(value, "xh", [(0, 1), (1, 0)])


def z_shift(value, k):
    return lax.ppermute(value, "head", [(i, (i + k) % 4) for i in range(4)])


def z_flip(value, mask):
    return lax.ppermute(value, "head", [(i, i ^ mask) for i in range(4)])


def core_swap(value):
    return lax.ppermute(value, "core", [(0, 1), (1, 0)])


def pack_kernel(info, w_hbm, d_hbm, k_ref, v_ref, w_ref, d_ref, sems):
    weight = pltpu.make_async_copy(w_hbm, w_ref, sems.at[0])
    down = pltpu.make_async_copy(d_hbm, d_ref, sems.at[1])
    weight.start()
    down.start()
    weight.wait()
    k_ref[...] = w_ref[:, 0, :]
    v_ref[0:256] = w_ref[pl.ds(pl.multiple_of(info[POOL] * 256, 256), 256), 1, :]
    column = lax.broadcasted_iota(jnp.int32, (256, 128), 0)
    lane = lax.broadcasted_iota(jnp.int32, (256, 128), 1)
    pick = (column == info[ADAPTER + info[HEAD]] * 32 + lane) & (lane < 32)
    down.wait()
    low = lax.dot_general(
        pick.astype(jnp.bfloat16),
        d_ref[...],
        (((0,), (1,)), ((), ())),
        preferred_element_type=jnp.float32,
    ).astype(jnp.bfloat16)
    v_ref[256:288] = low[0:32, 0:256]
    v_ref[288:320] = low[0:32, 256:512]


def pack(info, weight, down):
    return pl.pallas_call(
        pack_kernel,
        in_specs=[SMEM, HBM, HBM],
        out_specs=[VMEM, VMEM],
        out_shape=[
            jax.ShapeDtypeStruct((512, 256), jnp.bfloat16),
            jax.ShapeDtypeStruct((320, 256), jnp.bfloat16),
        ],
        scratch_shapes=[
            pltpu.VMEM(weight.shape, weight.dtype),
            pltpu.VMEM(down.shape, down.dtype),
            pltpu.SemaphoreType.DMA((2,)),
        ],
        compiler_params=params(),
        name="pack",
    )(info, weight, down)


ROWS_STEP = 12


def attend_kernel(offset, len_ref, q_ref, kv_ref, cur_ref, o_ref):
    first = pl.program_id(0) * ROWS_STEP + offset
    factor = HEAD_DIM**-0.5
    lane = lax.broadcasted_iota(jnp.int32, (8, 256), 1)
    is_key = (lane & 1) == 0
    scores, own = [], []
    for i in range(ROWS_STEP):
        n = len_ref[first + i]
        valid = is_key & (lane < 2 * n)
        for h in range(2):
            both = kv_ref[i, :, :, h * 128 : (h + 1) * 128].reshape(256, 128)
            q = q_ref[i, h * 8 : (h + 1) * 8, :]
            s = lax.dot_general(
                q, both, (((1,), (1,)), ((), ())), preferred_element_type=jnp.float32
            )
            scores.append(jnp.where(valid, s * factor, -1e30))
            k = cur_ref[i, 0:1, h * 128 : (h + 1) * 128].astype(jnp.float32)
            own.append(jnp.sum(q.astype(jnp.float32) * k, axis=-1, keepdims=True) * factor)
    s = jnp.concatenate(scores, 0)
    o = jnp.concatenate(own, 0)
    highest = jnp.maximum(jnp.max(s, axis=-1, keepdims=True), o)
    raw = jnp.exp(s - highest)
    own_raw = jnp.exp(o - highest)
    norm = jnp.sum(raw, axis=-1, keepdims=True) + own_raw
    weights = pltpu.roll(raw / norm, 1, 1).astype(jnp.bfloat16)
    own_weight = (own_raw / norm).astype(jnp.bfloat16).astype(jnp.float32)
    for i in range(ROWS_STEP):
        for h in range(2):
            both = kv_ref[i, :, :, h * 128 : (h + 1) * 128].reshape(256, 128)
            j = (i * 2 + h) * 8
            v = cur_ref[i, 1:2, h * 128 : (h + 1) * 128].astype(jnp.float32)
            mixed = jnp.dot(weights[j : j + 8], both, preferred_element_type=jnp.float32)
            mixed = mixed + own_weight[j : j + 8] * v
            o_ref[i, h * 8 : (h + 1) * 8, :] = mixed.astype(jnp.bfloat16)


def attend(query, cache, current, lengths, part, parts):
    rows, heads = query.shape[0] // parts, query.shape[1]
    first = part * (rows // ROWS_STEP)
    return pl.pallas_call(
        functools.partial(attend_kernel, first * ROWS_STEP),
        grid_spec=pltpu.PrefetchScalarGridSpec(
            num_scalar_prefetch=1,
            grid=(rows // ROWS_STEP,),
            in_specs=[
                pl.BlockSpec((ROWS_STEP, heads, 128), lambda g, n: (g + first, 0, 0)),
                pl.BlockSpec((ROWS_STEP, 128, 2, 256), lambda g, n: (g + first, 0, 0, 0)),
                pl.BlockSpec((ROWS_STEP, 2, 256), lambda g, n: (g + first, 0, 0)),
            ],
            out_specs=pl.BlockSpec((ROWS_STEP, heads, 128), lambda g, n: (g, 0, 0)),
        ),
        out_shape=jax.ShapeDtypeStruct((rows, heads, 128), jnp.bfloat16),
        compiler_params=params(),
        name="attend",
    )(lengths, query, cache, current)


def split_dot(low, up, dims=(((1,), (0,)), ((), ()))):
    high = low.astype(jnp.bfloat16)
    rest = (low - high.astype(jnp.float32)).astype(jnp.bfloat16)
    return lax.dot_general(high, up, dims, preferred_element_type=jnp.float32) + lax.dot_general(
        rest, up, dims, preferred_element_type=jnp.float32
    )


def x_order(x):
    return [x, (x + 3) & 3, (x + 2) & 3, (x + 1) & 3]


def low_kernel(info, prompt, own_ref, other_ref, out_ref):
    xh, y, core = info[XH], info[Y], info[CORE]
    rows = pl.ds(pl.multiple_of(info[HEAD] * 128, 128), 128)
    low = jnp.zeros((32, 128), jnp.float32)
    for n in range(2):
        ref, c_of = ((own_ref, core), (other_ref, 1 - core))[n]
        downs, tokens = [], []
        for i in range(16):
            side = xh if i < 8 else 1 - xh
            shard = side * 8 + x_order(y)[(i // 2) % 4] * 2 + c_of
            at = pl.multiple_of(shard * 512 + (i % 2) * 256, 256)
            tokens.append(prompt[rows, pl.ds(at, 256)])
            downs.append(ref[i * 32 : (i + 1) * 32])
        low = low + lax.dot_general(
            jnp.concatenate(downs, 1),
            jnp.concatenate(tokens, 1),
            (((1,), (1,)), ((), ())),
            preferred_element_type=jnp.float32,
        )
    out_ref[...] = low


def low_rank(info, tokens, own, other):
    return pl.pallas_call(
        low_kernel,
        in_specs=[SMEM, VMEM, VMEM, VMEM],
        out_specs=VMEM,
        out_shape=jax.ShapeDtypeStruct((32, 128), jnp.float32),
        compiler_params=params(),
        name="low_rank",
    )(info, tokens, own, other)


def add_products(pieces, fresh, info, prompt, blocks, outs):
    pool, xh, y, core = info[POOL], info[XH], info[Y], info[CORE]
    fresh = [fresh, fresh]
    for kv, partner, which, row, j in pieces:
        c_of = 1 - core if partner else core
        tokens = []
        if kv == 0:
            for side in (xh, 1 - xh):
                at = pl.multiple_of((side * 8 + x_order(y)[j] * 2 + c_of) * 512, 512)
                tokens.append(prompt[:, pl.ds(at, 512)])
        else:
            xi = x_order(2 * xh + pool)[j]
            for yi in x_order(y):
                at = ((xi >> 1) * 8 + yi * 2 + c_of) * 512 + (xi & 1) * 256
                tokens.append(prompt[:, pl.ds(pl.multiple_of(at, 256), 256)])
        part = jnp.dot(
            jnp.concatenate(tokens, 1),
            blocks[which][row : row + 1024],
            preferred_element_type=jnp.float32,
        )
        if fresh[kv]:
            outs[kv][...] = part
        else:
            outs[kv][...] += part
        fresh[kv] = False


def main_kernel(pieces, info, prompt, *refs):
    add_products(pieces, True, info, prompt, refs[:-2], refs[-2:])


def main_product(info, tokens, pieces, blocks):
    shape = jax.ShapeDtypeStruct((tokens.shape[0], 256), jnp.float32)
    return pl.pallas_call(
        functools.partial(main_kernel, pieces),
        in_specs=[SMEM] + [VMEM] * (1 + len(blocks)),
        out_specs=[VMEM, VMEM],
        out_shape=[shape, shape],
        compiler_params=params(),
        name="main_product",
    )(info, tokens, *blocks)


def finish_kernel(pieces, n_sums, info, prompt, *refs):
    n = len(refs) - 6 - 2 * n_sums
    blocks, sums = refs[:n], refs[n : n + 2 * n_sums]
    lows, up_ref, near_ref, far_ref, k_ref, v_ref = refs[n + 2 * n_sums :]
    pool, xh, z = info[POOL], info[XH], info[HEAD]
    for kv, ref in enumerate((k_ref, v_ref)):
        total = sums[kv][...]
        for m in range(1, n_sums):
            total = total + sums[2 * m + kv][...]
        ref[...] = total
    add_products(pieces, False, info, prompt, blocks, (k_ref, v_ref))
    owners = [info[DEST + pool * REQ_POOL + r] for r in range(REQ_POOL)]
    dims = (((0,), (0,)), ((), ()))
    for n in range(REQ_POOL):
        r = z ^ n
        a = info[ADAPTER + r]
        rows = pl.ds(pl.multiple_of(r * 128, 128), 128)
        low = lows[n * 32 : (n + 1) * 32]
        both = []
        for kv, ref in enumerate((k_ref, v_ref)):
            value = ref[rows, :] + split_dot(low[kv * 16 : (kv + 1) * 16], up_ref[a, kv], dims)
            both.append(value.astype(jnp.bfloat16))
        result = jnp.stack(both, axis=1)
        owner = info[DEST + pool * REQ_POOL + r]
        slot = jnp.int32(0)
        for q in range(REQ_POOL):
            slot = slot + (((owners[q] >> 3) == (owner >> 3)) & (q < r)).astype(jnp.int32)

        @pl.when((owner >> 3) == xh)
        def _():
            near_ref[slot] = result

        @pl.when((owner >> 3) != xh)
        def _():
            far_ref[slot] = result


def finish(info, tokens, pieces, blocks, sums, lows, up):
    shape = jax.ShapeDtypeStruct((X_SLOTS, 128, 2, 256), jnp.bfloat16)
    total = pltpu.VMEM((tokens.shape[0], 256), jnp.float32)
    flat = [v for pair in sums for v in pair]
    return pl.pallas_call(
        functools.partial(finish_kernel, pieces, len(sums)),
        in_specs=[SMEM] + [VMEM] * (3 + len(blocks) + len(flat)),
        out_specs=[VMEM, VMEM],
        out_shape=[shape, shape],
        scratch_shapes=[total, total],
        compiler_params=params(),
        name="finish",
    )(info, tokens, *blocks, *flat, lows, up)


def slots_of(info, pool, xh, owner):
    owners = [info[DEST + pool * REQ_POOL + r] for r in range(REQ_POOL)]
    index = [jnp.int32(0)] * CAP
    used = [jnp.int32(0)] * CAP
    place, mine = jnp.int32(0), jnp.int32(0)
    for r in range(REQ_POOL):
        hit = (owners[r] == owner).astype(jnp.int32)
        for j in range(CAP):
            here = hit * (mine == j).astype(jnp.int32)
            index[j] = index[j] + here * place
            used[j] = used[j] + here
        mine = mine + hit
        place = place + ((owners[r] >> 3) == xh).astype(jnp.int32)
    return index, used


def place_kernel(kinds, rest, sizes, info, *refs):
    n = len(sizes)
    at = [(i, b) for i, size in enumerate(sizes) for b in range(size)]
    ins, others = refs[:n], refs[n : 2 * n]
    out, zero, sems = refs[-3], refs[-2], refs[-1]
    xh, y, core = info[XH], info[Y], info[CORE]
    index, used = slots_of(info, 1 - info[POOL], xh, xh * 8 + y * 2 + core)
    if rest:
        zero[...] = jnp.zeros_like(zero)

    def spot(j, kind, c_of):
        side = xh if kind[0] == 0 else 1 - xh
        token = (side * 8 + x_order(y)[kind[1]] * 2 + c_of) * 128
        return out.at[0, j, pl.ds(pl.multiple_of(token, 128), 128)]

    def transfers(j):
        full = []
        for b, kind in enumerate(kinds):
            i, k = at[b]
            full.append((ins[i].at[k, index[j]], spot(j, kind, core)))
            full.append((others[i].at[k, index[j]], spot(j, kind, 1 - core)))
        return [
            pltpu.make_async_copy(src, dst, sems.at[j, i]) for i, (src, dst) in enumerate(full)
        ]

    def clears(j):
        spots = [spot(j, kind, c) for kind in kinds + rest for c in (core, 1 - core)]
        return [pltpu.make_async_copy(zero, dst, sems.at[j, i]) for i, dst in enumerate(spots)]

    for step in ("start", "wait"):
        for j in range(CAP):

            @pl.when(used[j] == 1)
            def _():
                for c in transfers(j):
                    getattr(c, step)()

            if rest:

                @pl.when(used[j] == 0)
                def _():
                    for c in clears(j):
                        getattr(c, step)()


def place(info, kinds, rest, parts, others, out=None):
    shape = jax.ShapeDtypeStruct((1, CAP, 2048, 2, 256), jnp.bfloat16)
    ins = [info, *parts, *others] + ([] if out is None else [out])
    return pl.pallas_call(
        functools.partial(place_kernel, kinds, rest, tuple(p.shape[0] for p in parts)),
        in_specs=[SMEM] + [VMEM] * (len(parts) + len(others)) + ([] if out is None else [ANY]),
        out_specs=ANY,
        out_shape=shape,
        scratch_shapes=[
            pltpu.VMEM((128, 2, 256), jnp.bfloat16),
            pltpu.SemaphoreType.DMA((CAP, 16)),
        ],
        input_output_aliases={} if out is None else {len(ins) - 1: 0},
        compiler_params=params(),
        name="place",
    )(*ins)


def project_kernel(info, keep, down, up, w_ref, *refs):
    ins, outs, res = refs[:2], refs[2:6], refs[6]
    xh, y, core, z = info[XH], info[Y], info[CORE], info[HEAD]
    value = jnp.concatenate([ref[...] for ref in ins], 0)
    out = jnp.dot(value, w_ref[...], preferred_element_type=jnp.float32)
    low = lax.dot_general(
        value, down[...], (((1,), (1,)), ((), ())), preferred_element_type=jnp.float32
    )
    owner = lax.broadcasted_iota(jnp.int32, (48, ADAPTERS * RANK), 1) >> 4
    spots, lows = [], []
    for b in range(8):
        row, c_of = x_order(y)[b % 4], core if b < 4 else 1 - core
        for i in range(2):
            side = xh if i == 0 else 1 - xh
            at = pl.ds(pl.multiple_of((side * 8 + row * 2 + c_of) * 48, 16), 48)
            n = b * 96 + i * 48
            spots.append(at)
            lows.append(jnp.where(keep[at, :] == owner, low[n : n + 48], 0.0))
    out = (out + split_dot(jnp.concatenate(lows, 0), up[...])).astype(jnp.bfloat16)
    for n in range(16):
        res[spots[n], :] = out[n * 48 : (n + 1) * 48]
    for n in range(4):
        outs[n][...] = res[pl.ds(pl.multiple_of(((z + n) & 3) * 192, 64), 192), :]


def project(info, keep, down, up, weight, parts):
    rows, width = 768, weight.shape[1]
    return pl.pallas_call(
        project_kernel,
        in_specs=[SMEM] + [VMEM] * 6,
        out_specs=[VMEM] * 4,
        out_shape=[jax.ShapeDtypeStruct((rows // 4, width), jnp.bfloat16)] * 4,
        scratch_shapes=[pltpu.VMEM((rows, width), jnp.bfloat16)],
        compiler_params=params(),
        name="project",
    )(info, keep, down, up, weight, *parts)


def ring(value, shift):
    return [value, shift(value, 1), shift(value, 2), shift(value, -1)]


def body(
    prompt,
    key_value_weight,
    adapter_down_weight,
    adapter_up_weight,
    request_adapter_index,
    destination,
    rotated_query,
    key_value_cache,
    current_key_value,
    cached_length,
    row_adapter_index,
    output_weight,
    output_down_weight,
    output_up_weight,
):
    barrier = lax.optimization_barrier
    axes = ("pool", "xh", "y", "core", "head")
    place_of = jnp.stack([lax.axis_index(a) for a in axes]).astype(jnp.int32)
    info = jnp.concatenate([place_of, destination, request_adapter_index])
    tokens = prompt.reshape(-1, prompt.shape[2])
    tokens = pltpu.with_memory_space_constraint(tokens, pltpu.VMEM)
    rows, heads = rotated_query.shape[0], rotated_query.shape[1] // HEAD_DIM
    query = rotated_query.reshape(rows, heads, HEAD_DIM)

    cache = pltpu.with_memory_space_constraint(key_value_cache, pltpu.HBM)
    keys, values = pack(
        info,
        pltpu.with_memory_space_constraint(key_value_weight, pltpu.HBM),
        pltpu.with_memory_space_constraint(adapter_down_weight, pltpu.HBM),
    )
    keys_across = x_mirror(keys)
    ring_values = ring(values, y_shift)
    keys, keys_across, ring_values, cached_length = barrier(
        (keys, keys_across, ring_values, cached_length)
    )
    key0 = jnp.concatenate([keys, keys_across], 0)
    value0 = jnp.concatenate([v[:256] for v in ring_values], 0)
    down0 = jnp.concatenate([v[256:] for v in ring_values], 0)
    key1, key3 = y_shift(key0, 1), y_shift(key0, -1)
    value1, value3 = x_shift(value0, 1), x_shift(value0, -1)
    down_own = jnp.concatenate([down0, xh_swap(down0)], 0)
    attended = attend(query, cache, current_key_value, cached_length, 0, 1)
    attended = attended.reshape(rows, heads * HEAD_DIM)
    key0, value0, key1, key3, value1, value3, down_own, attended = barrier(
        (key0, value0, key1, key3, value1, value3, down_own, attended)
    )
    key2, value2 = y_shift(key0, 2), x_shift(value0, 2)
    blocks = [key0, value0, key1, key3, value1, value3]
    order = ((0, 0), (1, 0), (0, 1), (0, 3), (1, 1), (1, 3))
    theirs = core_swap(jnp.concatenate(blocks, 0))
    across = xh_swap(attended)
    low = low_rank(info, tokens, down_own, core_swap(down_own))
    pair = jnp.concatenate([low, z_flip(low, 1)], 0)
    lows = jnp.concatenate([pair, z_flip(pair, 2)], 0)
    pieces = tuple((kv, 0, n, 0, j) for n, (kv, j) in enumerate(order))
    first = main_product(info, tokens, pieces, blocks)
    pieces = tuple((kv, 1, 0, 1024 * n, j) for n, (kv, j) in enumerate(order))
    second = main_product(info, tokens, pieces, [theirs])
    key2, value2, first, second, across, lows, attended = barrier(
        (key2, value2, first, second, across, lows, attended)
    )
    mine = ring(jnp.concatenate([attended, across], 0), y_shift)
    last = [key2, value2, core_swap(key2), core_swap(value2)]
    pieces = ((0, 0, 0, 0, 2), (1, 0, 1, 0, 2), (0, 1, 2, 0, 2), (1, 1, 3, 0, 2))
    same, other = finish(info, tokens, pieces, last, [first, second], lows, adapter_up_weight)

    b0 = lax.ppermute(same, "pool", [(0, 1), (1, 0)])
    a0 = x_mirror(other)
    b0, a0, mine = barrier((b0, a0, mine))
    mine = jnp.concatenate(mine, 0)
    partner = core_swap(mine)
    both0 = jnp.stack([b0, a0])
    both1, both3 = y_shift(both0, 1), y_shift(both0, -1)
    ranks = ADAPTERS * RANK
    down = jnp.transpose(output_down_weight, (1, 2, 0)).reshape(ranks, -1)
    up = output_up_weight.reshape(ranks, -1)
    keep = row_adapter_index[:, None]
    shares = list(project(info, keep, down, up, output_weight, [mine, partner]))
    shares[1:] = [z_shift(v, k) for v, k in zip(shares[1:], (1, 2, -1))]
    both0, both1, both3, shares[:3] = barrier((both0, both1, both3, shares[:3]))
    decoded = sum(v.astype(jnp.float32) for v in shares).astype(jnp.bfloat16)
    b2, a2 = y_shift(both1[0], 1), y_shift(both3[1], -1)
    middle = [both0, both1, both3]
    theirs = [core_swap(v) for v in middle]
    b2, a2, theirs, decoded = barrier((b2, a2, theirs, decoded))
    theirs2 = [core_swap(b2), core_swap(a2)]
    kinds = ((0, 0), (1, 0), (0, 1), (1, 1), (0, 3), (1, 3))
    rest = ((0, 2), (1, 2))
    handed = place(info, kinds, rest, middle, theirs)
    handed = place(info, rest, (), [b2[None], a2[None]], [v[None] for v in theirs2], handed)
    return handed, decoded


def solution(mesh):
    fine = Mesh(mesh.devices.reshape(2, 2, 4, 2, 4), ("pool", "xh", "y", "core", "head"))
    seq = ("xh", "y", "core")
    every = ("pool",) + seq
    in_specs = (
        P("pool", seq, None),
        P(seq, None, "head"),
        P(seq, None),
        P(None, None, None, "head"),
        P("pool"),
        P(),
        P(every, "head"),
        P(every, None, None, "head"),
        P(every, None, "head"),
        P(every),
        P("pool"),
        P("head", seq),
        P("head", None, None),
        P(None, None, seq),
    )
    out_specs = (P(every, None, None, None, "head"), P(("pool", "head"), seq))
    return jax.shard_map(body, mesh=fine, in_specs=in_specs, out_specs=out_specs, check_vma=False)
```

```python
import functools

import jax
import jax.numpy as jnp
from jax import lax
from jax.experimental import pallas as pl
from jax.experimental.pallas import tpu as pltpu
from jax.sharding import Mesh
from jax.sharding import PartitionSpec as P

HEAD_DIM = 128
RANK = 16
ADAPTERS = 8
CAP = 2
REQ_POOL = 4
X_SLOTS = 3
MIB = 2**20


POOL, XH, Y, CORE, HEAD, DEST, ADAPTER = 0, 1, 2, 3, 4, 5, 13
VMEM = pl.BlockSpec(memory_space=pltpu.VMEM)
SMEM = pl.BlockSpec(memory_space=pltpu.SMEM)
ANY = pl.BlockSpec(memory_space=pl.ANY)
HBM = pl.BlockSpec(memory_space=pltpu.HBM)


def params(limit=8):
    return pltpu.CompilerParams(vmem_limit_bytes=limit * MIB)


def x_mirror(value):
    return lax.ppermute(value, ("pool", "xh"), [(i, 3 - i) for i in range(4)])


def x_shift(value, k):
    pairs = []
    for x in range(4):
        t = (x + k) % 4
        pairs.append(((x % 2) * 2 + x // 2, (t % 2) * 2 + t // 2))
    return lax.ppermute(value, ("pool", "xh"), pairs)


def y_shift(value, k):
    return lax.ppermute(value, "y", [(i, (i + k) % 4) for i in range(4)])


def xh_swap(value):
    return lax.ppermute(value, "xh", [(0, 1), (1, 0)])


def z_shift(value, k):
    return lax.ppermute(value, "head", [(i, (i + k) % 4) for i in range(4)])


def z_flip(value, mask):
    return lax.ppermute(value, "head", [(i, i ^ mask) for i in range(4)])


def core_swap(value):
    return lax.ppermute(value, "core", [(0, 1), (1, 0)])


def pack_kernel(info, w_hbm, d_hbm, k_ref, v_ref, w_ref, d_ref, sems):
    weight = pltpu.make_async_copy(w_hbm, w_ref, sems.at[0])
    down = pltpu.make_async_copy(d_hbm, d_ref, sems.at[1])
    weight.start()
    down.start()
    weight.wait()
    k_ref[...] = w_ref[:, 0, :]
    v_ref[0:256] = w_ref[pl.ds(pl.multiple_of(info[POOL] * 256, 256), 256), 1, :]
    column = lax.broadcasted_iota(jnp.int32, (256, 128), 0)
    lane = lax.broadcasted_iota(jnp.int32, (256, 128), 1)
    pick = (column == info[ADAPTER + info[HEAD]] * 32 + lane) & (lane < 32)
    down.wait()
    low = lax.dot_general(
        pick.astype(jnp.bfloat16),
        d_ref[...],
        (((0,), (1,)), ((), ())),
        preferred_element_type=jnp.float32,
    ).astype(jnp.bfloat16)
    v_ref[256:288] = low[0:32, 0:256]
    v_ref[288:320] = low[0:32, 256:512]


def pack(info, weight, down):
    return pl.pallas_call(
        pack_kernel,
        in_specs=[SMEM, HBM, HBM],
        out_specs=[VMEM, VMEM],
        out_shape=[
            jax.ShapeDtypeStruct((512, 256), jnp.bfloat16),
            jax.ShapeDtypeStruct((320, 256), jnp.bfloat16),
        ],
        scratch_shapes=[
            pltpu.VMEM(weight.shape, weight.dtype),
            pltpu.VMEM(down.shape, down.dtype),
            pltpu.SemaphoreType.DMA((2,)),
        ],
        compiler_params=params(),
        name="pack",
    )(info, weight, down)


ROWS_STEP = 12


def attend_kernel(offset, len_ref, q_ref, kv_ref, cur_ref, o_ref):
    first = pl.program_id(0) * ROWS_STEP + offset
    factor = HEAD_DIM**-0.5
    lane = lax.broadcasted_iota(jnp.int32, (8, 256), 1)
    is_key = (lane & 1) == 0
    scores, own = [], []
    for i in range(ROWS_STEP):
        n = len_ref[first + i]
        valid = is_key & (lane < 2 * n)
        for h in range(2):
            both = kv_ref[i, :, :, h * 128 : (h + 1) * 128].reshape(256, 128)
            q = q_ref[i, h * 8 : (h + 1) * 8, :]
            s = lax.dot_general(
                q, both, (((1,), (1,)), ((), ())), preferred_element_type=jnp.float32
            )
            scores.append(jnp.where(valid, s * factor, -1e30))
            k = cur_ref[i, 0:1, h * 128 : (h + 1) * 128].astype(jnp.float32)
            own.append(jnp.sum(q.astype(jnp.float32) * k, axis=-1, keepdims=True) * factor)
    s = jnp.concatenate(scores, 0)
    o = jnp.concatenate(own, 0)
    highest = jnp.maximum(jnp.max(s, axis=-1, keepdims=True), o)
    raw = jnp.exp(s - highest)
    own_raw = jnp.exp(o - highest)
    norm = jnp.sum(raw, axis=-1, keepdims=True) + own_raw
    weights = pltpu.roll(raw / norm, 1, 1).astype(jnp.bfloat16)
    own_weight = (own_raw / norm).astype(jnp.bfloat16).astype(jnp.float32)
    for i in range(ROWS_STEP):
        for h in range(2):
            both = kv_ref[i, :, :, h * 128 : (h + 1) * 128].reshape(256, 128)
            j = (i * 2 + h) * 8
            v = cur_ref[i, 1:2, h * 128 : (h + 1) * 128].astype(jnp.float32)
            mixed = jnp.dot(weights[j : j + 8], both, preferred_element_type=jnp.float32)
            mixed = mixed + own_weight[j : j + 8] * v
            o_ref[i, h * 8 : (h + 1) * 8, :] = mixed.astype(jnp.bfloat16)


def attend(query, cache, current, lengths, part, parts):
    rows, heads = query.shape[0] // parts, query.shape[1]
    first = part * (rows // ROWS_STEP)
    return pl.pallas_call(
        functools.partial(attend_kernel, first * ROWS_STEP),
        grid_spec=pltpu.PrefetchScalarGridSpec(
            num_scalar_prefetch=1,
            grid=(rows // ROWS_STEP,),
            in_specs=[
                pl.BlockSpec((ROWS_STEP, heads, 128), lambda g, n: (g + first, 0, 0)),
                pl.BlockSpec((ROWS_STEP, 128, 2, 256), lambda g, n: (g + first, 0, 0, 0)),
                pl.BlockSpec((ROWS_STEP, 2, 256), lambda g, n: (g + first, 0, 0)),
            ],
            out_specs=pl.BlockSpec((ROWS_STEP, heads, 128), lambda g, n: (g, 0, 0)),
        ),
        out_shape=jax.ShapeDtypeStruct((rows, heads, 128), jnp.bfloat16),
        compiler_params=params(),
        name="attend",
    )(lengths, query, cache, current)


def split_dot(low, up, dims=(((1,), (0,)), ((), ()))):
    high = low.astype(jnp.bfloat16)
    rest = (low - high.astype(jnp.float32)).astype(jnp.bfloat16)
    return lax.dot_general(high, up, dims, preferred_element_type=jnp.float32) + lax.dot_general(
        rest, up, dims, preferred_element_type=jnp.float32
    )


def x_order(x):
    return [x, (x + 3) & 3, (x + 2) & 3, (x + 1) & 3]


def low_kernel(info, prompt, own_ref, other_ref, out_ref):
    xh, y, core = info[XH], info[Y], info[CORE]
    rows = pl.ds(pl.multiple_of(info[HEAD] * 128, 128), 128)
    low = jnp.zeros((32, 128), jnp.float32)
    for n in range(2):
        ref, c_of = ((own_ref, core), (other_ref, 1 - core))[n]
        downs, tokens = [], []
        for i in range(16):
            side = xh if i < 8 else 1 - xh
            shard = side * 8 + x_order(y)[(i // 2) % 4] * 2 + c_of
            at = pl.multiple_of(shard * 512 + (i % 2) * 256, 256)
            tokens.append(prompt[rows, pl.ds(at, 256)])
            downs.append(ref[i * 32 : (i + 1) * 32])
        low = low + lax.dot_general(
            jnp.concatenate(downs, 1),
            jnp.concatenate(tokens, 1),
            (((1,), (1,)), ((), ())),
            preferred_element_type=jnp.float32,
        )
    out_ref[...] = low


def low_rank(info, tokens, own, other):
    return pl.pallas_call(
        low_kernel,
        in_specs=[SMEM, VMEM, VMEM, VMEM],
        out_specs=VMEM,
        out_shape=jax.ShapeDtypeStruct((32, 128), jnp.float32),
        compiler_params=params(),
        name="low_rank",
    )(info, tokens, own, other)


def add_products(pieces, fresh, info, prompt, blocks, outs):
    pool, xh, y, core = info[POOL], info[XH], info[Y], info[CORE]
    fresh = [fresh, fresh]
    for kv, partner, which, row, j in pieces:
        c_of = 1 - core if partner else core
        tokens = []
        if kv == 0:
            for side in (xh, 1 - xh):
                at = pl.multiple_of((side * 8 + x_order(y)[j] * 2 + c_of) * 512, 512)
                tokens.append(prompt[:, pl.ds(at, 512)])
        else:
            xi = x_order(2 * xh + pool)[j]
            for yi in x_order(y):
                at = ((xi >> 1) * 8 + yi * 2 + c_of) * 512 + (xi & 1) * 256
                tokens.append(prompt[:, pl.ds(pl.multiple_of(at, 256), 256)])
        part = jnp.dot(
            jnp.concatenate(tokens, 1),
            blocks[which][row : row + 1024],
            preferred_element_type=jnp.float32,
        )
        if fresh[kv]:
            outs[kv][...] = part
        else:
            outs[kv][...] += part
        fresh[kv] = False


def main_kernel(pieces, info, prompt, *refs):
    add_products(pieces, True, info, prompt, refs[:-2], refs[-2:])


def main_product(info, tokens, pieces, blocks):
    shape = jax.ShapeDtypeStruct((tokens.shape[0], 256), jnp.float32)
    return pl.pallas_call(
        functools.partial(main_kernel, pieces),
        in_specs=[SMEM] + [VMEM] * (1 + len(blocks)),
        out_specs=[VMEM, VMEM],
        out_shape=[shape, shape],
        compiler_params=params(),
        name="main_product",
    )(info, tokens, *blocks)


def finish_kernel(pieces, n_sums, info, prompt, *refs):
    n = len(refs) - 6 - 2 * n_sums
    blocks, sums = refs[:n], refs[n : n + 2 * n_sums]
    lows, up_ref, near_ref, far_ref, k_ref, v_ref = refs[n + 2 * n_sums :]
    pool, xh, z = info[POOL], info[XH], info[HEAD]
    for kv, ref in enumerate((k_ref, v_ref)):
        total = sums[kv][...]
        for m in range(1, n_sums):
            total = total + sums[2 * m + kv][...]
        ref[...] = total
    add_products(pieces, False, info, prompt, blocks, (k_ref, v_ref))
    owners = [info[DEST + pool * REQ_POOL + r] for r in range(REQ_POOL)]
    dims = (((0,), (0,)), ((), ()))
    for n in range(REQ_POOL):
        r = z ^ n
        a = info[ADAPTER + r]
        rows = pl.ds(pl.multiple_of(r * 128, 128), 128)
        low = lows[n * 32 : (n + 1) * 32]
        both = []
        for kv, ref in enumerate((k_ref, v_ref)):
            value = ref[rows, :] + split_dot(low[kv * 16 : (kv + 1) * 16], up_ref[a, kv], dims)
            both.append(value.astype(jnp.bfloat16))
        result = jnp.stack(both, axis=1)
        owner = info[DEST + pool * REQ_POOL + r]
        slot = jnp.int32(0)
        for q in range(REQ_POOL):
            slot = slot + (((owners[q] >> 3) == (owner >> 3)) & (q < r)).astype(jnp.int32)

        @pl.when((owner >> 3) == xh)
        def _():
            near_ref[slot] = result

        @pl.when((owner >> 3) != xh)
        def _():
            far_ref[slot] = result


def finish(info, tokens, pieces, blocks, sums, lows, up):
    shape = jax.ShapeDtypeStruct((X_SLOTS, 128, 2, 256), jnp.bfloat16)
    total = pltpu.VMEM((tokens.shape[0], 256), jnp.float32)
    flat = [v for pair in sums for v in pair]
    return pl.pallas_call(
        functools.partial(finish_kernel, pieces, len(sums)),
        in_specs=[SMEM] + [VMEM] * (3 + len(blocks) + len(flat)),
        out_specs=[VMEM, VMEM],
        out_shape=[shape, shape],
        scratch_shapes=[total, total],
        compiler_params=params(),
        name="finish",
    )(info, tokens, *blocks, *flat, lows, up)


def slots_of(info, pool, xh, owner):
    owners = [info[DEST + pool * REQ_POOL + r] for r in range(REQ_POOL)]
    index = [jnp.int32(0)] * CAP
    used = [jnp.int32(0)] * CAP
    place, mine = jnp.int32(0), jnp.int32(0)
    for r in range(REQ_POOL):
        hit = (owners[r] == owner).astype(jnp.int32)
        for j in range(CAP):
            here = hit * (mine == j).astype(jnp.int32)
            index[j] = index[j] + here * place
            used[j] = used[j] + here
        mine = mine + hit
        place = place + ((owners[r] >> 3) == xh).astype(jnp.int32)
    return index, used


def place_kernel(kinds, rest, sizes, info, *refs):
    n = len(sizes)
    at = [(i, b) for i, size in enumerate(sizes) for b in range(size)]
    ins, others = refs[:n], refs[n : 2 * n]
    out, zero, sems = refs[-3], refs[-2], refs[-1]
    xh, y, core = info[XH], info[Y], info[CORE]
    index, used = slots_of(info, 1 - info[POOL], xh, xh * 8 + y * 2 + core)
    if rest:
        zero[...] = jnp.zeros_like(zero)

    def spot(j, kind, c_of):
        side = xh if kind[0] == 0 else 1 - xh
        token = (side * 8 + x_order(y)[kind[1]] * 2 + c_of) * 128
        return out.at[0, j, pl.ds(pl.multiple_of(token, 128), 128)]

    def transfers(j):
        full = []
        for b, kind in enumerate(kinds):
            i, k = at[b]
            full.append((ins[i].at[k, index[j]], spot(j, kind, core)))
            full.append((others[i].at[k, index[j]], spot(j, kind, 1 - core)))
        return [
            pltpu.make_async_copy(src, dst, sems.at[j, i]) for i, (src, dst) in enumerate(full)
        ]

    def clears(j):
        spots = [spot(j, kind, c) for kind in kinds + rest for c in (core, 1 - core)]
        return [pltpu.make_async_copy(zero, dst, sems.at[j, i]) for i, dst in enumerate(spots)]

    for step in ("start", "wait"):
        for j in range(CAP):

            @pl.when(used[j] == 1)
            def _():
                for c in transfers(j):
                    getattr(c, step)()

            if rest:

                @pl.when(used[j] == 0)
                def _():
                    for c in clears(j):
                        getattr(c, step)()


def place(info, kinds, rest, parts, others, out=None):
    shape = jax.ShapeDtypeStruct((1, CAP, 2048, 2, 256), jnp.bfloat16)
    ins = [info, *parts, *others] + ([] if out is None else [out])
    return pl.pallas_call(
        functools.partial(place_kernel, kinds, rest, tuple(p.shape[0] for p in parts)),
        in_specs=[SMEM] + [VMEM] * (len(parts) + len(others)) + ([] if out is None else [ANY]),
        out_specs=ANY,
        out_shape=shape,
        scratch_shapes=[
            pltpu.VMEM((128, 2, 256), jnp.bfloat16),
            pltpu.SemaphoreType.DMA((CAP, 16)),
        ],
        input_output_aliases={} if out is None else {len(ins) - 1: 0},
        compiler_params=params(),
        name="place",
    )(*ins)


def project_kernel(info, keep, down, up, w_ref, *refs):
    ins, outs, res = refs[:2], refs[2:6], refs[6]
    xh, y, core, z = info[XH], info[Y], info[CORE], info[HEAD]
    value = jnp.concatenate([ref[...] for ref in ins], 0)
    out = jnp.dot(value, w_ref[...], preferred_element_type=jnp.float32)
    low = lax.dot_general(
        value, down[...], (((1,), (1,)), ((), ())), preferred_element_type=jnp.float32
    )
    owner = lax.broadcasted_iota(jnp.int32, (48, ADAPTERS * RANK), 1) >> 4
    spots, lows = [], []
    for b in range(8):
        row, c_of = x_order(y)[b % 4], core if b < 4 else 1 - core
        for i in range(2):
            side = xh if i == 0 else 1 - xh
            at = pl.ds(pl.multiple_of((side * 8 + row * 2 + c_of) * 48, 16), 48)
            n = b * 96 + i * 48
            spots.append(at)
            lows.append(jnp.where(keep[at, :] == owner, low[n : n + 48], 0.0))
    out = (out + split_dot(jnp.concatenate(lows, 0), up[...])).astype(jnp.bfloat16)
    for n in range(16):
        res[spots[n], :] = out[n * 48 : (n + 1) * 48]
    for n in range(4):
        outs[n][...] = res[pl.ds(pl.multiple_of(((z + n) & 3) * 192, 64), 192), :]


def project(info, keep, down, up, weight, parts):
    rows, width = 768, weight.shape[1]
    return pl.pallas_call(
        project_kernel,
        in_specs=[SMEM] + [VMEM] * 6,
        out_specs=[VMEM] * 4,
        out_shape=[jax.ShapeDtypeStruct((rows // 4, width), jnp.bfloat16)] * 4,
        scratch_shapes=[pltpu.VMEM((rows, width), jnp.bfloat16)],
        compiler_params=params(),
        name="project",
    )(info, keep, down, up, weight, *parts)


def ring(value, shift):
    return [value, shift(value, 1), shift(value, 2), shift(value, -1)]


def body(
    prompt,
    key_value_weight,
    adapter_down_weight,
    adapter_up_weight,
    request_adapter_index,
    destination,
    rotated_query,
    key_value_cache,
    current_key_value,
    cached_length,
    row_adapter_index,
    output_weight,
    output_down_weight,
    output_up_weight,
):
    barrier = lax.optimization_barrier
    axes = ("pool", "xh", "y", "core", "head")
    place_of = jnp.stack([lax.axis_index(a) for a in axes]).astype(jnp.int32)
    info = jnp.concatenate([place_of, destination, request_adapter_index])
    tokens = prompt.reshape(-1, prompt.shape[2])
    tokens = pltpu.with_memory_space_constraint(tokens, pltpu.VMEM)
    rows, heads = rotated_query.shape[0], rotated_query.shape[1] // HEAD_DIM
    query = rotated_query.reshape(rows, heads, HEAD_DIM)

    cache = pltpu.with_memory_space_constraint(key_value_cache, pltpu.HBM)
    keys, values = pack(
        info,
        pltpu.with_memory_space_constraint(key_value_weight, pltpu.HBM),
        pltpu.with_memory_space_constraint(adapter_down_weight, pltpu.HBM),
    )
    keys_across = x_mirror(keys)
    ring_values = ring(values, y_shift)
    keys, keys_across, ring_values, cached_length = barrier(
        (keys, keys_across, ring_values, cached_length)
    )
    key0 = jnp.concatenate([keys, keys_across], 0)
    value0 = jnp.concatenate([v[:256] for v in ring_values], 0)
    down0 = jnp.concatenate([v[256:] for v in ring_values], 0)
    key1, key3 = y_shift(key0, 1), y_shift(key0, -1)
    value1, value3 = x_shift(value0, 1), x_shift(value0, -1)
    down_own = jnp.concatenate([down0, xh_swap(down0)], 0)
    attended = attend(query, cache, current_key_value, cached_length, 0, 1)
    attended = attended.reshape(rows, heads * HEAD_DIM)
    key0, value0, key1, key3, value1, value3, down_own, attended = barrier(
        (key0, value0, key1, key3, value1, value3, down_own, attended)
    )
    key2, value2 = y_shift(key0, 2), x_shift(value0, 2)
    blocks = [key0, value0, key1, key3, value1, value3]
    order = ((0, 0), (1, 0), (0, 1), (0, 3), (1, 1), (1, 3))
    theirs = core_swap(jnp.concatenate(blocks, 0))
    across = xh_swap(attended)
    low = low_rank(info, tokens, down_own, core_swap(down_own))
    pair = jnp.concatenate([low, z_flip(low, 1)], 0)
    lows = jnp.concatenate([pair, z_flip(pair, 2)], 0)
    pieces = tuple((kv, 0, n, 0, j) for n, (kv, j) in enumerate(order))
    first = main_product(info, tokens, pieces, blocks)
    pieces = tuple((kv, 1, 0, 1024 * n, j) for n, (kv, j) in enumerate(order))
    second = main_product(info, tokens, pieces, [theirs])
    key2, value2, first, second, across, lows, attended = barrier(
        (key2, value2, first, second, across, lows, attended)
    )
    mine = ring(jnp.concatenate([attended, across], 0), y_shift)
    last = [key2, value2, core_swap(key2), core_swap(value2)]
    pieces = ((0, 0, 0, 0, 2), (1, 0, 1, 0, 2), (0, 1, 2, 0, 2), (1, 1, 3, 0, 2))
    same, other = finish(info, tokens, pieces, last, [first, second], lows, adapter_up_weight)

    b0 = lax.ppermute(same, "pool", [(0, 1), (1, 0)])
    a0 = x_mirror(other)
    b0, a0, mine = barrier((b0, a0, mine))
    mine = jnp.concatenate(mine, 0)
    partner = core_swap(mine)
    both0 = jnp.stack([b0, a0])
    both1, both3 = y_shift(both0, 1), y_shift(both0, -1)
    ranks = ADAPTERS * RANK
    down = jnp.transpose(output_down_weight, (1, 2, 0)).reshape(ranks, -1)
    up = output_up_weight.reshape(ranks, -1)
    keep = row_adapter_index[:, None]
    shares = list(project(info, keep, down, up, output_weight, [mine, partner]))
    theirs0 = core_swap(both0)
    shares, theirs0 = barrier((shares, theirs0))
    shares[1:] = [z_shift(v, k) for v, k in zip(shares[1:], (1, 2, -1))]
    both0, both1, both3, shares[1], shares[3] = barrier(
        (both0, both1, both3, shares[1], shares[3])
    )
    decoded = sum(v.astype(jnp.float32) for v in shares).astype(jnp.bfloat16)
    b2, a2 = y_shift(both1[0], 1), y_shift(both3[1], -1)
    middle = [both0, both1, both3]
    theirs = [theirs0, core_swap(both1), core_swap(both3)]
    b2, a2, theirs, decoded = barrier((b2, a2, theirs, decoded))
    theirs2 = [core_swap(b2), core_swap(a2)]
    kinds = ((0, 0), (1, 0), (0, 1), (1, 1), (0, 3), (1, 3))
    rest = ((0, 2), (1, 2))
    handed = place(info, kinds, rest, middle, theirs)
    handed = place(info, rest, (), [b2[None], a2[None]], [v[None] for v in theirs2], handed)
    return handed, decoded


def solution(mesh):
    fine = Mesh(mesh.devices.reshape(2, 2, 4, 2, 4), ("pool", "xh", "y", "core", "head"))
    seq = ("xh", "y", "core")
    every = ("pool",) + seq
    in_specs = (
        P("pool", seq, None),
        P(seq, None, "head"),
        P(seq, None),
        P(None, None, None, "head"),
        P("pool"),
        P(),
        P(every, "head"),
        P(every, None, None, "head"),
        P(every, None, "head"),
        P(every),
        P("pool"),
        P("head", seq),
        P("head", None, None),
        P(None, None, seq),
    )
    out_specs = (P(every, None, None, None, "head"), P(("pool", "head"), seq))
    return jax.shard_map(body, mesh=fine, in_specs=in_specs, out_specs=out_specs, check_vma=False)
```

```python
import functools

import jax
import jax.numpy as jnp
from jax import lax
from jax.experimental import pallas as pl
from jax.experimental.pallas import tpu as pltpu
from jax.sharding import Mesh
from jax.sharding import PartitionSpec as P

HEAD_DIM = 128
RANK = 16
ADAPTERS = 8
CAP = 2
REQ_POOL = 4
X_SLOTS = 3
MIB = 2**20


POOL, XH, Y, CORE, HEAD, DEST, ADAPTER = 0, 1, 2, 3, 4, 5, 13
VMEM = pl.BlockSpec(memory_space=pltpu.VMEM)
SMEM = pl.BlockSpec(memory_space=pltpu.SMEM)
ANY = pl.BlockSpec(memory_space=pl.ANY)
HBM = pl.BlockSpec(memory_space=pltpu.HBM)


def params(limit=8):
    return pltpu.CompilerParams(vmem_limit_bytes=limit * MIB)


def x_mirror(value):
    return lax.ppermute(value, ("pool", "xh"), [(i, 3 - i) for i in range(4)])


def x_shift(value, k):
    pairs = []
    for x in range(4):
        t = (x + k) % 4
        pairs.append(((x % 2) * 2 + x // 2, (t % 2) * 2 + t // 2))
    return lax.ppermute(value, ("pool", "xh"), pairs)


def y_shift(value, k):
    return lax.ppermute(value, "y", [(i, (i + k) % 4) for i in range(4)])


def xh_swap(value):
    return lax.ppermute(value, "xh", [(0, 1), (1, 0)])


def z_shift(value, k):
    return lax.ppermute(value, "head", [(i, (i + k) % 4) for i in range(4)])


def z_flip(value, mask):
    return lax.ppermute(value, "head", [(i, i ^ mask) for i in range(4)])


def core_swap(value):
    return lax.ppermute(value, "core", [(0, 1), (1, 0)])


def pack_kernel(info, w_hbm, d_hbm, k_ref, v_ref, w_ref, d_ref, sems):
    weight = pltpu.make_async_copy(w_hbm, w_ref, sems.at[0])
    down = pltpu.make_async_copy(d_hbm, d_ref, sems.at[1])
    weight.start()
    down.start()
    weight.wait()
    k_ref[...] = w_ref[:, 0, :]
    v_ref[0:256] = w_ref[pl.ds(pl.multiple_of(info[POOL] * 256, 256), 256), 1, :]
    column = lax.broadcasted_iota(jnp.int32, (256, 128), 0)
    lane = lax.broadcasted_iota(jnp.int32, (256, 128), 1)
    pick = (column == info[ADAPTER + info[HEAD]] * 32 + lane) & (lane < 32)
    down.wait()
    low = lax.dot_general(
        pick.astype(jnp.bfloat16),
        d_ref[...],
        (((0,), (1,)), ((), ())),
        preferred_element_type=jnp.float32,
    ).astype(jnp.bfloat16)
    v_ref[256:288] = low[0:32, 0:256]
    v_ref[288:320] = low[0:32, 256:512]


def pack(info, weight, down):
    return pl.pallas_call(
        pack_kernel,
        in_specs=[SMEM, HBM, HBM],
        out_specs=[VMEM, VMEM],
        out_shape=[
            jax.ShapeDtypeStruct((512, 256), jnp.bfloat16),
            jax.ShapeDtypeStruct((320, 256), jnp.bfloat16),
        ],
        scratch_shapes=[
            pltpu.VMEM(weight.shape, weight.dtype),
            pltpu.VMEM(down.shape, down.dtype),
            pltpu.SemaphoreType.DMA((2,)),
        ],
        compiler_params=params(),
        name="pack",
    )(info, weight, down)


ROWS_STEP = 12


def attend_kernel(offset, len_ref, q_ref, kv_ref, cur_ref, o_ref):
    first = pl.program_id(0) * ROWS_STEP + offset
    factor = HEAD_DIM**-0.5
    lane = lax.broadcasted_iota(jnp.int32, (8, 256), 1)
    is_key = (lane & 1) == 0
    scores, own = [], []
    for i in range(ROWS_STEP):
        n = len_ref[first + i]
        valid = is_key & (lane < 2 * n)
        for h in range(2):
            both = kv_ref[i, :, :, h * 128 : (h + 1) * 128].reshape(256, 128)
            q = q_ref[i, h * 8 : (h + 1) * 8, :]
            s = lax.dot_general(
                q, both, (((1,), (1,)), ((), ())), preferred_element_type=jnp.float32
            )
            scores.append(jnp.where(valid, s * factor, -1e30))
            k = cur_ref[i, 0:1, h * 128 : (h + 1) * 128].astype(jnp.float32)
            own.append(jnp.sum(q.astype(jnp.float32) * k, axis=-1, keepdims=True) * factor)
    s = jnp.concatenate(scores, 0)
    o = jnp.concatenate(own, 0)
    highest = jnp.maximum(jnp.max(s, axis=-1, keepdims=True), o)
    raw = jnp.exp(s - highest)
    own_raw = jnp.exp(o - highest)
    norm = jnp.sum(raw, axis=-1, keepdims=True) + own_raw
    weights = pltpu.roll(raw / norm, 1, 1).astype(jnp.bfloat16)
    own_weight = (own_raw / norm).astype(jnp.bfloat16).astype(jnp.float32)
    for i in range(ROWS_STEP):
        for h in range(2):
            both = kv_ref[i, :, :, h * 128 : (h + 1) * 128].reshape(256, 128)
            j = (i * 2 + h) * 8
            v = cur_ref[i, 1:2, h * 128 : (h + 1) * 128].astype(jnp.float32)
            mixed = jnp.dot(weights[j : j + 8], both, preferred_element_type=jnp.float32)
            mixed = mixed + own_weight[j : j + 8] * v
            o_ref[i, h * 8 : (h + 1) * 8, :] = mixed.astype(jnp.bfloat16)


def attend(query, cache, current, lengths, part, parts):
    rows, heads = query.shape[0] // parts, query.shape[1]
    first = part * (rows // ROWS_STEP)
    return pl.pallas_call(
        functools.partial(attend_kernel, first * ROWS_STEP),
        grid_spec=pltpu.PrefetchScalarGridSpec(
            num_scalar_prefetch=1,
            grid=(rows // ROWS_STEP,),
            in_specs=[
                pl.BlockSpec((ROWS_STEP, heads, 128), lambda g, n: (g + first, 0, 0)),
                pl.BlockSpec((ROWS_STEP, 128, 2, 256), lambda g, n: (g + first, 0, 0, 0)),
                pl.BlockSpec((ROWS_STEP, 2, 256), lambda g, n: (g + first, 0, 0)),
            ],
            out_specs=pl.BlockSpec((ROWS_STEP, heads, 128), lambda g, n: (g, 0, 0)),
        ),
        out_shape=jax.ShapeDtypeStruct((rows, heads, 128), jnp.bfloat16),
        compiler_params=params(),
        name="attend",
    )(lengths, query, cache, current)


def split_dot(low, up, dims=(((1,), (0,)), ((), ()))):
    high = low.astype(jnp.bfloat16)
    rest = (low - high.astype(jnp.float32)).astype(jnp.bfloat16)
    return lax.dot_general(high, up, dims, preferred_element_type=jnp.float32) + lax.dot_general(
        rest, up, dims, preferred_element_type=jnp.float32
    )


def x_order(x):
    return [x, (x + 3) & 3, (x + 2) & 3, (x + 1) & 3]


def low_kernel(info, prompt, own_ref, other_ref, out_ref):
    xh, y, core = info[XH], info[Y], info[CORE]
    rows = pl.ds(pl.multiple_of(info[HEAD] * 128, 128), 128)
    low = jnp.zeros((32, 128), jnp.float32)
    for n in range(2):
        ref, c_of = ((own_ref, core), (other_ref, 1 - core))[n]
        downs, tokens = [], []
        for i in range(16):
            side = xh if i < 8 else 1 - xh
            shard = side * 8 + x_order(y)[(i // 2) % 4] * 2 + c_of
            at = pl.multiple_of(shard * 512 + (i % 2) * 256, 256)
            tokens.append(prompt[rows, pl.ds(at, 256)])
            downs.append(ref[i * 32 : (i + 1) * 32])
        low = low + lax.dot_general(
            jnp.concatenate(downs, 1),
            jnp.concatenate(tokens, 1),
            (((1,), (1,)), ((), ())),
            preferred_element_type=jnp.float32,
        )
    out_ref[...] = low


def low_rank(info, tokens, own, other):
    return pl.pallas_call(
        low_kernel,
        in_specs=[SMEM, VMEM, VMEM, VMEM],
        out_specs=VMEM,
        out_shape=jax.ShapeDtypeStruct((32, 128), jnp.float32),
        compiler_params=params(),
        name="low_rank",
    )(info, tokens, own, other)


def add_products(pieces, fresh, info, prompt, blocks, outs):
    pool, xh, y, core = info[POOL], info[XH], info[Y], info[CORE]
    fresh = [fresh, fresh]
    for kv, partner, which, row, j in pieces:
        c_of = 1 - core if partner else core
        tokens = []
        if kv == 0:
            for side in (xh, 1 - xh):
                at = pl.multiple_of((side * 8 + x_order(y)[j] * 2 + c_of) * 512, 512)
                tokens.append(prompt[:, pl.ds(at, 512)])
        else:
            xi = x_order(2 * xh + pool)[j]
            for yi in x_order(y):
                at = ((xi >> 1) * 8 + yi * 2 + c_of) * 512 + (xi & 1) * 256
                tokens.append(prompt[:, pl.ds(pl.multiple_of(at, 256), 256)])
        part = jnp.dot(
            jnp.concatenate(tokens, 1),
            blocks[which][row : row + 1024],
            preferred_element_type=jnp.float32,
        )
        if fresh[kv]:
            outs[kv][...] = part
        else:
            outs[kv][...] += part
        fresh[kv] = False


def main_kernel(pieces, info, prompt, *refs):
    add_products(pieces, True, info, prompt, refs[:-2], refs[-2:])


def main_product(info, tokens, pieces, blocks):
    shape = jax.ShapeDtypeStruct((tokens.shape[0], 256), jnp.float32)
    return pl.pallas_call(
        functools.partial(main_kernel, pieces),
        in_specs=[SMEM] + [VMEM] * (1 + len(blocks)),
        out_specs=[VMEM, VMEM],
        out_shape=[shape, shape],
        compiler_params=params(),
        name="main_product",
    )(info, tokens, *blocks)


def finish_kernel(pieces, n_sums, info, prompt, *refs):
    n = len(refs) - 6 - 2 * n_sums
    blocks, sums = refs[:n], refs[n : n + 2 * n_sums]
    lows, up_ref, near_ref, far_ref, k_ref, v_ref = refs[n + 2 * n_sums :]
    pool, xh, z = info[POOL], info[XH], info[HEAD]
    for kv, ref in enumerate((k_ref, v_ref)):
        total = sums[kv][...]
        for m in range(1, n_sums):
            total = total + sums[2 * m + kv][...]
        ref[...] = total
    add_products(pieces, False, info, prompt, blocks, (k_ref, v_ref))
    owners = [info[DEST + pool * REQ_POOL + r] for r in range(REQ_POOL)]
    dims = (((0,), (0,)), ((), ()))
    for n in range(REQ_POOL):
        r = z ^ n
        a = info[ADAPTER + r]
        rows = pl.ds(pl.multiple_of(r * 128, 128), 128)
        low = lows[n * 32 : (n + 1) * 32]
        both = []
        for kv, ref in enumerate((k_ref, v_ref)):
            value = ref[rows, :] + split_dot(low[kv * 16 : (kv + 1) * 16], up_ref[a, kv], dims)
            both.append(value.astype(jnp.bfloat16))
        result = jnp.stack(both, axis=1)
        owner = info[DEST + pool * REQ_POOL + r]
        slot = jnp.int32(0)
        for q in range(REQ_POOL):
            slot = slot + (((owners[q] >> 3) == (owner >> 3)) & (q < r)).astype(jnp.int32)

        @pl.when((owner >> 3) == xh)
        def _():
            near_ref[slot] = result

        @pl.when((owner >> 3) != xh)
        def _():
            far_ref[slot] = result


def finish(info, tokens, pieces, blocks, sums, lows, up):
    shape = jax.ShapeDtypeStruct((X_SLOTS, 128, 2, 256), jnp.bfloat16)
    total = pltpu.VMEM((tokens.shape[0], 256), jnp.float32)
    flat = [v for pair in sums for v in pair]
    return pl.pallas_call(
        functools.partial(finish_kernel, pieces, len(sums)),
        in_specs=[SMEM] + [VMEM] * (3 + len(blocks) + len(flat)),
        out_specs=[VMEM, VMEM],
        out_shape=[shape, shape],
        scratch_shapes=[total, total],
        compiler_params=params(),
        name="finish",
    )(info, tokens, *blocks, *flat, lows, up)


def slots_of(info, pool, xh, owner):
    owners = [info[DEST + pool * REQ_POOL + r] for r in range(REQ_POOL)]
    index = [jnp.int32(0)] * CAP
    used = [jnp.int32(0)] * CAP
    place, mine = jnp.int32(0), jnp.int32(0)
    for r in range(REQ_POOL):
        hit = (owners[r] == owner).astype(jnp.int32)
        for j in range(CAP):
            here = hit * (mine == j).astype(jnp.int32)
            index[j] = index[j] + here * place
            used[j] = used[j] + here
        mine = mine + hit
        place = place + ((owners[r] >> 3) == xh).astype(jnp.int32)
    return index, used


def place_kernel(kinds, rest, sizes, info, *refs):
    n = len(sizes)
    at = [(i, b) for i, size in enumerate(sizes) for b in range(size)]
    ins, others = refs[:n], refs[n : 2 * n]
    out, zero, sems = refs[-3], refs[-2], refs[-1]
    xh, y, core = info[XH], info[Y], info[CORE]
    index, used = slots_of(info, 1 - info[POOL], xh, xh * 8 + y * 2 + core)
    if rest:
        zero[...] = jnp.zeros_like(zero)

    def spot(j, kind, c_of):
        side = xh if kind[0] == 0 else 1 - xh
        token = (side * 8 + x_order(y)[kind[1]] * 2 + c_of) * 128
        return out.at[0, j, pl.ds(pl.multiple_of(token, 128), 128)]

    def transfers(j):
        full = []
        for b, kind in enumerate(kinds):
            i, k = at[b]
            full.append((ins[i].at[k, index[j]], spot(j, kind, core)))
            full.append((others[i].at[k, index[j]], spot(j, kind, 1 - core)))
        return [
            pltpu.make_async_copy(src, dst, sems.at[j, i]) for i, (src, dst) in enumerate(full)
        ]

    def clears(j):
        spots = [spot(j, kind, c) for kind in kinds + rest for c in (core, 1 - core)]
        return [pltpu.make_async_copy(zero, dst, sems.at[j, i]) for i, dst in enumerate(spots)]

    for step in ("start", "wait"):
        for j in range(CAP):

            @pl.when(used[j] == 1)
            def _():
                for c in transfers(j):
                    getattr(c, step)()

            if rest:

                @pl.when(used[j] == 0)
                def _():
                    for c in clears(j):
                        getattr(c, step)()


def place(info, kinds, rest, parts, others, out=None):
    shape = jax.ShapeDtypeStruct((1, CAP, 2048, 2, 256), jnp.bfloat16)
    ins = [info, *parts, *others] + ([] if out is None else [out])
    return pl.pallas_call(
        functools.partial(place_kernel, kinds, rest, tuple(p.shape[0] for p in parts)),
        in_specs=[SMEM] + [VMEM] * (len(parts) + len(others)) + ([] if out is None else [ANY]),
        out_specs=ANY,
        out_shape=shape,
        scratch_shapes=[
            pltpu.VMEM((128, 2, 256), jnp.bfloat16),
            pltpu.SemaphoreType.DMA((CAP, 16)),
        ],
        input_output_aliases={} if out is None else {len(ins) - 1: 0},
        compiler_params=params(),
        name="place",
    )(*ins)


def project_kernel(info, keep, down, up, w_ref, *refs):
    ins, outs, res = refs[:2], refs[2:6], refs[6]
    xh, y, core, z = info[XH], info[Y], info[CORE], info[HEAD]
    value = jnp.concatenate([ref[...] for ref in ins], 0)
    out = jnp.dot(value, w_ref[...], preferred_element_type=jnp.float32)
    low = lax.dot_general(
        value, down[...], (((1,), (1,)), ((), ())), preferred_element_type=jnp.float32
    )
    owner = lax.broadcasted_iota(jnp.int32, (48, ADAPTERS * RANK), 1) >> 4
    spots, lows = [], []
    for b in range(8):
        row, c_of = x_order(y)[b % 4], core if b < 4 else 1 - core
        for i in range(2):
            side = xh if i == 0 else 1 - xh
            at = pl.ds(pl.multiple_of((side * 8 + row * 2 + c_of) * 48, 16), 48)
            n = b * 96 + i * 48
            spots.append(at)
            lows.append(jnp.where(keep[at, :] == owner, low[n : n + 48], 0.0))
    out = (out + split_dot(jnp.concatenate(lows, 0), up[...])).astype(jnp.bfloat16)
    for n in range(16):
        res[spots[n], :] = out[n * 48 : (n + 1) * 48]
    for n in range(4):
        outs[n][...] = res[pl.ds(pl.multiple_of(((z + n) & 3) * 192, 64), 192), :]


def project(info, keep, down, up, weight, parts):
    rows, width = 768, weight.shape[1]
    return pl.pallas_call(
        project_kernel,
        in_specs=[SMEM] + [VMEM] * 6,
        out_specs=[VMEM] * 4,
        out_shape=[jax.ShapeDtypeStruct((rows // 4, width), jnp.bfloat16)] * 4,
        scratch_shapes=[pltpu.VMEM((rows, width), jnp.bfloat16)],
        compiler_params=params(),
        name="project",
    )(info, keep, down, up, weight, *parts)


def ring(value, shift):
    return [value, shift(value, 1), shift(value, 2), shift(value, -1)]


def body(
    prompt,
    key_value_weight,
    adapter_down_weight,
    adapter_up_weight,
    request_adapter_index,
    destination,
    rotated_query,
    key_value_cache,
    current_key_value,
    cached_length,
    row_adapter_index,
    output_weight,
    output_down_weight,
    output_up_weight,
):
    barrier = lax.optimization_barrier
    axes = ("pool", "xh", "y", "core", "head")
    place_of = jnp.stack([lax.axis_index(a) for a in axes]).astype(jnp.int32)
    info = jnp.concatenate([place_of, destination, request_adapter_index])
    tokens = prompt.reshape(-1, prompt.shape[2])
    tokens = pltpu.with_memory_space_constraint(tokens, pltpu.VMEM)
    rows, heads = rotated_query.shape[0], rotated_query.shape[1] // HEAD_DIM
    query = rotated_query.reshape(rows, heads, HEAD_DIM)

    cache = pltpu.with_memory_space_constraint(key_value_cache, pltpu.HBM)
    keys, values = pack(
        info,
        pltpu.with_memory_space_constraint(key_value_weight, pltpu.HBM),
        pltpu.with_memory_space_constraint(adapter_down_weight, pltpu.HBM),
    )
    keys_across = x_mirror(keys)
    ring_values = ring(values, y_shift)
    keys, keys_across, cached_length = barrier((keys, keys_across, cached_length))
    key0 = jnp.concatenate([keys, keys_across], 0)
    value0 = jnp.concatenate([v[:256] for v in ring_values], 0)
    down0 = jnp.concatenate([v[256:] for v in ring_values], 0)
    key1, key3 = y_shift(key0, 1), y_shift(key0, -1)
    value1, value3 = x_shift(value0, 1), x_shift(value0, -1)
    down_own = jnp.concatenate([down0, xh_swap(down0)], 0)
    attended = attend(query, cache, current_key_value, cached_length, 0, 1)
    attended = attended.reshape(rows, heads * HEAD_DIM)
    key0, value0, key1, key3, value1, value3, down_own, attended = barrier(
        (key0, value0, key1, key3, value1, value3, down_own, attended)
    )
    key2, value2 = y_shift(key0, 2), x_shift(value0, 2)
    blocks = [key0, value0, key1, key3, value1, value3]
    order = ((0, 0), (1, 0), (0, 1), (0, 3), (1, 1), (1, 3))
    theirs = core_swap(jnp.concatenate(blocks, 0))
    across = xh_swap(attended)
    low = low_rank(info, tokens, down_own, core_swap(down_own))
    pair = jnp.concatenate([low, z_flip(low, 1)], 0)
    lows = jnp.concatenate([pair, z_flip(pair, 2)], 0)
    pieces = tuple((kv, 0, n, 0, j) for n, (kv, j) in enumerate(order))
    first = main_product(info, tokens, pieces, blocks)
    pieces = tuple((kv, 1, 0, 1024 * n, j) for n, (kv, j) in enumerate(order))
    second = main_product(info, tokens, pieces, [theirs])
    key2, value2, first, second, across, lows, attended = barrier(
        (key2, value2, first, second, across, lows, attended)
    )
    mine = ring(jnp.concatenate([attended, across], 0), y_shift)
    last = [key2, value2, core_swap(key2), core_swap(value2)]
    pieces = ((0, 0, 0, 0, 2), (1, 0, 1, 0, 2), (0, 1, 2, 0, 2), (1, 1, 3, 0, 2))
    same, other = finish(info, tokens, pieces, last, [first, second], lows, adapter_up_weight)

    b0 = lax.ppermute(same, "pool", [(0, 1), (1, 0)])
    a0 = x_mirror(other)
    b0, a0, mine = barrier((b0, a0, mine))
    mine = jnp.concatenate(mine, 0)
    partner = core_swap(mine)
    both0 = jnp.stack([b0, a0])
    both1, both3 = y_shift(both0, 1), y_shift(both0, -1)
    ranks = ADAPTERS * RANK
    down = jnp.transpose(output_down_weight, (1, 2, 0)).reshape(ranks, -1)
    up = output_up_weight.reshape(ranks, -1)
    keep = row_adapter_index[:, None]
    shares = list(project(info, keep, down, up, output_weight, [mine, partner]))
    theirs0 = core_swap(both0)
    shares, theirs0 = barrier((shares, theirs0))
    shares[1:] = [z_shift(v, k) for v, k in zip(shares[1:], (1, 2, -1))]
    both0, both1, both3, shares[1], shares[3] = barrier(
        (both0, both1, both3, shares[1], shares[3])
    )
    decoded = sum(v.astype(jnp.float32) for v in shares).astype(jnp.bfloat16)
    b2, a2 = y_shift(both1[0], 1), y_shift(both3[1], -1)
    middle = [both0, both1, both3]
    theirs = [theirs0, core_swap(both1), core_swap(both3)]
    b2, a2, theirs, decoded = barrier((b2, a2, theirs, decoded))
    theirs2 = [core_swap(b2), core_swap(a2)]
    kinds = ((0, 0), (1, 0), (0, 1), (1, 1), (0, 3), (1, 3))
    rest = ((0, 2), (1, 2))
    handed = place(info, kinds, rest, middle, theirs)
    handed = place(info, rest, (), [b2[None], a2[None]], [v[None] for v in theirs2], handed)
    return handed, decoded


def solution(mesh):
    fine = Mesh(mesh.devices.reshape(2, 2, 4, 2, 4), ("pool", "xh", "y", "core", "head"))
    seq = ("xh", "y", "core")
    every = ("pool",) + seq
    in_specs = (
        P("pool", seq, None),
        P(seq, None, "head"),
        P(seq, None),
        P(None, None, None, "head"),
        P("pool"),
        P(),
        P(every, "head"),
        P(every, None, None, "head"),
        P(every, None, "head"),
        P(every),
        P("pool"),
        P("head", seq),
        P("head", None, None),
        P(None, None, seq),
    )
    out_specs = (P(every, None, None, None, "head"), P(("pool", "head"), seq))
    return jax.shard_map(body, mesh=fine, in_specs=in_specs, out_specs=out_specs, check_vma=False)
```

```python
import functools

import jax
import jax.numpy as jnp
from jax import lax
from jax.experimental import pallas as pl
from jax.experimental.pallas import tpu as pltpu
from jax.sharding import Mesh
from jax.sharding import PartitionSpec as P

HEAD_DIM = 128
RANK = 16
ADAPTERS = 8
CAP = 2
REQ_POOL = 4
X_SLOTS = 3
MIB = 2**20


POOL, XH, Y, CORE, HEAD, DEST, ADAPTER = 0, 1, 2, 3, 4, 5, 13
VMEM = pl.BlockSpec(memory_space=pltpu.VMEM)
SMEM = pl.BlockSpec(memory_space=pltpu.SMEM)
ANY = pl.BlockSpec(memory_space=pl.ANY)
HBM = pl.BlockSpec(memory_space=pltpu.HBM)


def params(limit=8):
    return pltpu.CompilerParams(vmem_limit_bytes=limit * MIB)


def x_mirror(value):
    return lax.ppermute(value, ("pool", "xh"), [(i, 3 - i) for i in range(4)])


def x_shift(value, k):
    pairs = []
    for x in range(4):
        t = (x + k) % 4
        pairs.append(((x % 2) * 2 + x // 2, (t % 2) * 2 + t // 2))
    return lax.ppermute(value, ("pool", "xh"), pairs)


def y_shift(value, k):
    return lax.ppermute(value, "y", [(i, (i + k) % 4) for i in range(4)])


def xh_swap(value):
    return lax.ppermute(value, "xh", [(0, 1), (1, 0)])


def z_shift(value, k):
    return lax.ppermute(value, "head", [(i, (i + k) % 4) for i in range(4)])


def z_flip(value, mask):
    return lax.ppermute(value, "head", [(i, i ^ mask) for i in range(4)])


def core_swap(value):
    return lax.ppermute(value, "core", [(0, 1), (1, 0)])


def pack_kernel(info, adapter, w_hbm, d_hbm, k_ref, v_ref, w_ref, d_ref, sems):
    weight = pltpu.make_async_copy(w_hbm, w_ref, sems.at[0])
    down = pltpu.make_async_copy(d_hbm, d_ref, sems.at[1])
    weight.start()
    down.start()
    weight.wait()
    k_ref[...] = w_ref[:, 0, :]
    v_ref[0:256] = w_ref[pl.ds(pl.multiple_of(info[POOL] * 256, 256), 256), 1, :]
    column = lax.broadcasted_iota(jnp.int32, (256, 128), 0)
    lane = lax.broadcasted_iota(jnp.int32, (256, 128), 1)
    pick = (column == adapter[info[HEAD]] * 32 + lane) & (lane < 32)
    down.wait()
    low = lax.dot_general(
        pick.astype(jnp.bfloat16),
        d_ref[...],
        (((0,), (1,)), ((), ())),
        preferred_element_type=jnp.float32,
    ).astype(jnp.bfloat16)
    v_ref[256:288] = low[0:32, 0:256]
    v_ref[288:320] = low[0:32, 256:512]


def pack(info, adapter, weight, down):
    return pl.pallas_call(
        pack_kernel,
        in_specs=[SMEM, SMEM, HBM, HBM],
        out_specs=[VMEM, VMEM],
        out_shape=[
            jax.ShapeDtypeStruct((512, 256), jnp.bfloat16),
            jax.ShapeDtypeStruct((320, 256), jnp.bfloat16),
        ],
        scratch_shapes=[
            pltpu.VMEM(weight.shape, weight.dtype),
            pltpu.VMEM(down.shape, down.dtype),
            pltpu.SemaphoreType.DMA((2,)),
        ],
        compiler_params=params(),
        name="pack",
    )(info, adapter, weight, down)


ROWS_STEP = 12


def attend_kernel(offset, len_ref, q_ref, kv_ref, cur_ref, o_ref):
    first = pl.program_id(0) * ROWS_STEP + offset
    factor = HEAD_DIM**-0.5
    lane = lax.broadcasted_iota(jnp.int32, (8, 256), 1)
    is_key = (lane & 1) == 0
    scores, own = [], []
    for i in range(ROWS_STEP):
        n = len_ref[first + i]
        valid = is_key & (lane < 2 * n)
        for h in range(2):
            both = kv_ref[i, :, :, h * 128 : (h + 1) * 128].reshape(256, 128)
            q = q_ref[i, h * 8 : (h + 1) * 8, :]
            s = lax.dot_general(
                q, both, (((1,), (1,)), ((), ())), preferred_element_type=jnp.float32
            )
            scores.append(jnp.where(valid, s * factor, -1e30))
            k = cur_ref[i, 0:1, h * 128 : (h + 1) * 128].astype(jnp.float32)
            own.append(jnp.sum(q.astype(jnp.float32) * k, axis=-1, keepdims=True) * factor)
    s = jnp.concatenate(scores, 0)
    o = jnp.concatenate(own, 0)
    highest = jnp.maximum(jnp.max(s, axis=-1, keepdims=True), o)
    raw = jnp.exp(s - highest)
    own_raw = jnp.exp(o - highest)
    norm = jnp.sum(raw, axis=-1, keepdims=True) + own_raw
    weights = pltpu.roll(raw / norm, 1, 1).astype(jnp.bfloat16)
    own_weight = (own_raw / norm).astype(jnp.bfloat16).astype(jnp.float32)
    for i in range(ROWS_STEP):
        for h in range(2):
            both = kv_ref[i, :, :, h * 128 : (h + 1) * 128].reshape(256, 128)
            j = (i * 2 + h) * 8
            v = cur_ref[i, 1:2, h * 128 : (h + 1) * 128].astype(jnp.float32)
            mixed = jnp.dot(weights[j : j + 8], both, preferred_element_type=jnp.float32)
            mixed = mixed + own_weight[j : j + 8] * v
            o_ref[i, h * 8 : (h + 1) * 8, :] = mixed.astype(jnp.bfloat16)


def attend(query, cache, current, lengths, part, parts):
    rows, heads = query.shape[0] // parts, query.shape[1]
    first = part * (rows // ROWS_STEP)
    return pl.pallas_call(
        functools.partial(attend_kernel, first * ROWS_STEP),
        grid_spec=pltpu.PrefetchScalarGridSpec(
            num_scalar_prefetch=1,
            grid=(rows // ROWS_STEP,),
            in_specs=[
                pl.BlockSpec((ROWS_STEP, heads, 128), lambda g, n: (g + first, 0, 0)),
                pl.BlockSpec((ROWS_STEP, 128, 2, 256), lambda g, n: (g + first, 0, 0, 0)),
                pl.BlockSpec((ROWS_STEP, 2, 256), lambda g, n: (g + first, 0, 0)),
            ],
            out_specs=pl.BlockSpec((ROWS_STEP, heads, 128), lambda g, n: (g, 0, 0)),
        ),
        out_shape=jax.ShapeDtypeStruct((rows, heads, 128), jnp.bfloat16),
        compiler_params=params(),
        name="attend",
    )(lengths, query, cache, current)


def split_dot(low, up, dims=(((1,), (0,)), ((), ()))):
    high = low.astype(jnp.bfloat16)
    rest = (low - high.astype(jnp.float32)).astype(jnp.bfloat16)
    return lax.dot_general(high, up, dims, preferred_element_type=jnp.float32) + lax.dot_general(
        rest, up, dims, preferred_element_type=jnp.float32
    )


def x_order(x):
    return [x, (x + 3) & 3, (x + 2) & 3, (x + 1) & 3]


def low_kernel(info, prompt, own_ref, other_ref, out_ref):
    xh, y, core = info[XH], info[Y], info[CORE]
    rows = pl.ds(pl.multiple_of(info[HEAD] * 128, 128), 128)
    low = jnp.zeros((32, 128), jnp.float32)
    for n in range(2):
        ref, c_of = ((own_ref, core), (other_ref, 1 - core))[n]
        downs, tokens = [], []
        for i in range(16):
            side = xh if i < 8 else 1 - xh
            shard = side * 8 + x_order(y)[(i // 2) % 4] * 2 + c_of
            at = pl.multiple_of(shard * 512 + (i % 2) * 256, 256)
            tokens.append(prompt[rows, pl.ds(at, 256)])
            downs.append(ref[i * 32 : (i + 1) * 32])
        low = low + lax.dot_general(
            jnp.concatenate(downs, 1),
            jnp.concatenate(tokens, 1),
            (((1,), (1,)), ((), ())),
            preferred_element_type=jnp.float32,
        )
    out_ref[...] = low


def low_rank(info, tokens, own, other):
    return pl.pallas_call(
        low_kernel,
        in_specs=[SMEM, VMEM, VMEM, VMEM],
        out_specs=VMEM,
        out_shape=jax.ShapeDtypeStruct((32, 128), jnp.float32),
        compiler_params=params(),
        name="low_rank",
    )(info, tokens, own, other)


def add_products(pieces, fresh, info, prompt, blocks, outs):
    pool, xh, y, core = info[POOL], info[XH], info[Y], info[CORE]
    fresh = [fresh, fresh]
    for kv, partner, which, row, j in pieces:
        c_of = 1 - core if partner else core
        tokens = []
        if kv == 0:
            for side in (xh, 1 - xh):
                at = pl.multiple_of((side * 8 + x_order(y)[j] * 2 + c_of) * 512, 512)
                tokens.append(prompt[:, pl.ds(at, 512)])
        else:
            xi = x_order(2 * xh + pool)[j]
            for yi in x_order(y):
                at = ((xi >> 1) * 8 + yi * 2 + c_of) * 512 + (xi & 1) * 256
                tokens.append(prompt[:, pl.ds(pl.multiple_of(at, 256), 256)])
        part = jnp.dot(
            jnp.concatenate(tokens, 1),
            blocks[which][row : row + 1024],
            preferred_element_type=jnp.float32,
        )
        if fresh[kv]:
            outs[kv][...] = part
        else:
            outs[kv][...] += part
        fresh[kv] = False


def main_kernel(pieces, info, prompt, *refs):
    add_products(pieces, True, info, prompt, refs[:-2], refs[-2:])


def main_product(info, tokens, pieces, blocks):
    shape = jax.ShapeDtypeStruct((tokens.shape[0], 256), jnp.float32)
    return pl.pallas_call(
        functools.partial(main_kernel, pieces),
        in_specs=[SMEM] + [VMEM] * (1 + len(blocks)),
        out_specs=[VMEM, VMEM],
        out_shape=[shape, shape],
        compiler_params=params(),
        name="main_product",
    )(info, tokens, *blocks)


def finish_kernel(pieces, n_sums, info, prompt, *refs):
    n = len(refs) - 6 - 2 * n_sums
    blocks, sums = refs[:n], refs[n : n + 2 * n_sums]
    lows, up_ref, near_ref, far_ref, k_ref, v_ref = refs[n + 2 * n_sums :]
    pool, xh, z = info[POOL], info[XH], info[HEAD]
    for kv, ref in enumerate((k_ref, v_ref)):
        total = sums[kv][...]
        for m in range(1, n_sums):
            total = total + sums[2 * m + kv][...]
        ref[...] = total
    add_products(pieces, False, info, prompt, blocks, (k_ref, v_ref))
    owners = [info[DEST + pool * REQ_POOL + r] for r in range(REQ_POOL)]
    dims = (((0,), (0,)), ((), ()))
    for n in range(REQ_POOL):
        r = z ^ n
        a = info[ADAPTER + r]
        rows = pl.ds(pl.multiple_of(r * 128, 128), 128)
        low = lows[n * 32 : (n + 1) * 32]
        both = []
        for kv, ref in enumerate((k_ref, v_ref)):
            value = ref[rows, :] + split_dot(low[kv * 16 : (kv + 1) * 16], up_ref[a, kv], dims)
            both.append(value.astype(jnp.bfloat16))
        result = jnp.stack(both, axis=1)
        owner = info[DEST + pool * REQ_POOL + r]
        slot = jnp.int32(0)
        for q in range(REQ_POOL):
            slot = slot + (((owners[q] >> 3) == (owner >> 3)) & (q < r)).astype(jnp.int32)

        @pl.when((owner >> 3) == xh)
        def _():
            near_ref[slot] = result

        @pl.when((owner >> 3) != xh)
        def _():
            far_ref[slot] = result


def finish(info, tokens, pieces, blocks, sums, lows, up):
    shape = jax.ShapeDtypeStruct((X_SLOTS, 128, 2, 256), jnp.bfloat16)
    total = pltpu.VMEM((tokens.shape[0], 256), jnp.float32)
    flat = [v for pair in sums for v in pair]
    return pl.pallas_call(
        functools.partial(finish_kernel, pieces, len(sums)),
        in_specs=[SMEM] + [VMEM] * (3 + len(blocks) + len(flat)),
        out_specs=[VMEM, VMEM],
        out_shape=[shape, shape],
        scratch_shapes=[total, total],
        compiler_params=params(),
        name="finish",
    )(info, tokens, *blocks, *flat, lows, up)


def slots_of(info, pool, xh, owner):
    owners = [info[DEST + pool * REQ_POOL + r] for r in range(REQ_POOL)]
    index = [jnp.int32(0)] * CAP
    used = [jnp.int32(0)] * CAP
    place, mine = jnp.int32(0), jnp.int32(0)
    for r in range(REQ_POOL):
        hit = (owners[r] == owner).astype(jnp.int32)
        for j in range(CAP):
            here = hit * (mine == j).astype(jnp.int32)
            index[j] = index[j] + here * place
            used[j] = used[j] + here
        mine = mine + hit
        place = place + ((owners[r] >> 3) == xh).astype(jnp.int32)
    return index, used


def place_kernel(kinds, rest, sizes, info, *refs):
    n = len(sizes)
    at = [(i, b) for i, size in enumerate(sizes) for b in range(size)]
    ins, others = refs[:n], refs[n : 2 * n]
    out, zero, sems = refs[-3], refs[-2], refs[-1]
    xh, y, core = info[XH], info[Y], info[CORE]
    index, used = slots_of(info, 1 - info[POOL], xh, xh * 8 + y * 2 + core)
    if rest:
        zero[...] = jnp.zeros_like(zero)

    def spot(j, kind, c_of):
        side = xh if kind[0] == 0 else 1 - xh
        token = (side * 8 + x_order(y)[kind[1]] * 2 + c_of) * 128
        return out.at[0, j, pl.ds(pl.multiple_of(token, 128), 128)]

    def transfers(j):
        full = []
        for b, kind in enumerate(kinds):
            i, k = at[b]
            full.append((ins[i].at[k, index[j]], spot(j, kind, core)))
            full.append((others[i].at[k, index[j]], spot(j, kind, 1 - core)))
        return [
            pltpu.make_async_copy(src, dst, sems.at[j, i]) for i, (src, dst) in enumerate(full)
        ]

    def clears(j):
        spots = [spot(j, kind, c) for kind in kinds + rest for c in (core, 1 - core)]
        return [pltpu.make_async_copy(zero, dst, sems.at[j, i]) for i, dst in enumerate(spots)]

    for step in ("start", "wait"):
        for j in range(CAP):

            @pl.when(used[j] == 1)
            def _():
                for c in transfers(j):
                    getattr(c, step)()

            if rest:

                @pl.when(used[j] == 0)
                def _():
                    for c in clears(j):
                        getattr(c, step)()


def place(info, kinds, rest, parts, others, out=None):
    shape = jax.ShapeDtypeStruct((1, CAP, 2048, 2, 256), jnp.bfloat16)
    ins = [info, *parts, *others] + ([] if out is None else [out])
    return pl.pallas_call(
        functools.partial(place_kernel, kinds, rest, tuple(p.shape[0] for p in parts)),
        in_specs=[SMEM] + [VMEM] * (len(parts) + len(others)) + ([] if out is None else [ANY]),
        out_specs=ANY,
        out_shape=shape,
        scratch_shapes=[
            pltpu.VMEM((128, 2, 256), jnp.bfloat16),
            pltpu.SemaphoreType.DMA((CAP, 16)),
        ],
        input_output_aliases={} if out is None else {len(ins) - 1: 0},
        compiler_params=params(),
        name="place",
    )(*ins)


def project_kernel(info, keep, down, up, w_ref, *refs):
    ins, outs, res = refs[:2], refs[2:6], refs[6]
    xh, y, core, z = info[XH], info[Y], info[CORE], info[HEAD]
    value = jnp.concatenate([ref[...] for ref in ins], 0)
    out = jnp.dot(value, w_ref[...], preferred_element_type=jnp.float32)
    low = lax.dot_general(
        value, down[...], (((1,), (1,)), ((), ())), preferred_element_type=jnp.float32
    )
    owner = lax.broadcasted_iota(jnp.int32, (48, ADAPTERS * RANK), 1) >> 4
    spots, lows = [], []
    for b in range(8):
        row, c_of = x_order(y)[b % 4], core if b < 4 else 1 - core
        for i in range(2):
            side = xh if i == 0 else 1 - xh
            at = pl.ds(pl.multiple_of((side * 8 + row * 2 + c_of) * 48, 16), 48)
            n = b * 96 + i * 48
            spots.append(at)
            lows.append(jnp.where(keep[at, :] == owner, low[n : n + 48], 0.0))
    out = (out + split_dot(jnp.concatenate(lows, 0), up[...])).astype(jnp.bfloat16)
    for n in range(16):
        res[spots[n], :] = out[n * 48 : (n + 1) * 48]
    for n in range(4):
        outs[n][...] = res[pl.ds(pl.multiple_of(((z + n) & 3) * 192, 64), 192), :]


def project(info, keep, down, up, weight, parts):
    rows, width = 768, weight.shape[1]
    return pl.pallas_call(
        project_kernel,
        in_specs=[SMEM] + [VMEM] * 6,
        out_specs=[VMEM] * 4,
        out_shape=[jax.ShapeDtypeStruct((rows // 4, width), jnp.bfloat16)] * 4,
        scratch_shapes=[pltpu.VMEM((rows, width), jnp.bfloat16)],
        compiler_params=params(),
        name="project",
    )(info, keep, down, up, weight, *parts)


def ring(value, shift):
    return [value, shift(value, 1), shift(value, 2), shift(value, -1)]


def body(
    prompt,
    key_value_weight,
    adapter_down_weight,
    adapter_up_weight,
    request_adapter_index,
    destination,
    rotated_query,
    key_value_cache,
    current_key_value,
    cached_length,
    row_adapter_index,
    output_weight,
    output_down_weight,
    output_up_weight,
):
    barrier = lax.optimization_barrier
    axes = ("pool", "xh", "y", "core", "head")
    place_of = jnp.stack([lax.axis_index(a) for a in axes]).astype(jnp.int32)
    info = jnp.concatenate([place_of, destination, request_adapter_index])
    tokens = prompt.reshape(-1, prompt.shape[2])
    tokens = pltpu.with_memory_space_constraint(tokens, pltpu.VMEM)
    rows, heads = rotated_query.shape[0], rotated_query.shape[1] // HEAD_DIM
    query = rotated_query.reshape(rows, heads, HEAD_DIM)

    cache = pltpu.with_memory_space_constraint(key_value_cache, pltpu.HBM)
    keys, values = pack(
        place_of,
        request_adapter_index,
        pltpu.with_memory_space_constraint(key_value_weight, pltpu.HBM),
        pltpu.with_memory_space_constraint(adapter_down_weight, pltpu.HBM),
    )
    keys_across = x_mirror(keys)
    ring_values = ring(values, y_shift)
    keys, keys_across, cached_length = barrier((keys, keys_across, cached_length))
    key0 = jnp.concatenate([keys, keys_across], 0)
    value0 = jnp.concatenate([v[:256] for v in ring_values], 0)
    down0 = jnp.concatenate([v[256:] for v in ring_values], 0)
    key1, key3 = y_shift(key0, 1), y_shift(key0, -1)
    value1, value3 = x_shift(value0, 1), x_shift(value0, -1)
    down_own = jnp.concatenate([down0, xh_swap(down0)], 0)
    attended = attend(query, cache, current_key_value, cached_length, 0, 1)
    attended = attended.reshape(rows, heads * HEAD_DIM)
    key0, value0, key1, key3, value1, value3, down_own, attended = barrier(
        (key0, value0, key1, key3, value1, value3, down_own, attended)
    )
    key2, value2 = y_shift(key0, 2), x_shift(value0, 2)
    blocks = [key0, value0, key1, key3, value1, value3]
    order = ((0, 0), (1, 0), (0, 1), (0, 3), (1, 1), (1, 3))
    theirs = core_swap(jnp.concatenate(blocks, 0))
    across = xh_swap(attended)
    low = low_rank(info, tokens, down_own, core_swap(down_own))
    pair = jnp.concatenate([low, z_flip(low, 1)], 0)
    lows = jnp.concatenate([pair, z_flip(pair, 2)], 0)
    pieces = tuple((kv, 0, n, 0, j) for n, (kv, j) in enumerate(order))
    first = main_product(info, tokens, pieces, blocks)
    pieces = tuple((kv, 1, 0, 1024 * n, j) for n, (kv, j) in enumerate(order))
    second = main_product(info, tokens, pieces, [theirs])
    key2, value2, first, second, across, lows, attended = barrier(
        (key2, value2, first, second, across, lows, attended)
    )
    mine = ring(jnp.concatenate([attended, across], 0), y_shift)
    last = [key2, value2, core_swap(key2), core_swap(value2)]
    pieces = ((0, 0, 0, 0, 2), (1, 0, 1, 0, 2), (0, 1, 2, 0, 2), (1, 1, 3, 0, 2))
    same, other = finish(info, tokens, pieces, last, [first, second], lows, adapter_up_weight)

    b0 = lax.ppermute(same, "pool", [(0, 1), (1, 0)])
    a0 = x_mirror(other)
    b0, a0, mine = barrier((b0, a0, mine))
    mine = jnp.concatenate(mine, 0)
    partner = core_swap(mine)
    both0 = jnp.stack([b0, a0])
    both1, both3 = y_shift(both0, 1), y_shift(both0, -1)
    ranks = ADAPTERS * RANK
    down = jnp.transpose(output_down_weight, (1, 2, 0)).reshape(ranks, -1)
    up = output_up_weight.reshape(ranks, -1)
    keep = row_adapter_index[:, None]
    shares = list(project(info, keep, down, up, output_weight, [mine, partner]))
    theirs0 = core_swap(both0)
    shares, theirs0 = barrier((shares, theirs0))
    shares[1:] = [z_shift(v, k) for v, k in zip(shares[1:], (1, 2, -1))]
    both0, both1, both3, shares[1], shares[3] = barrier(
        (both0, both1, both3, shares[1], shares[3])
    )
    decoded = sum(v.astype(jnp.float32) for v in shares).astype(jnp.bfloat16)
    b2, a2 = y_shift(both1[0], 1), y_shift(both3[1], -1)
    middle = [both0, both1, both3]
    theirs = [theirs0, core_swap(both1), core_swap(both3)]
    b2, a2, theirs, decoded = barrier((b2, a2, theirs, decoded))
    theirs2 = [core_swap(b2), core_swap(a2)]
    kinds = ((0, 0), (1, 0), (0, 1), (1, 1), (0, 3), (1, 3))
    rest = ((0, 2), (1, 2))
    handed = place(info, kinds, rest, middle, theirs)
    handed = place(info, rest, (), [b2[None], a2[None]], [v[None] for v in theirs2], handed)
    return handed, decoded


def solution(mesh):
    fine = Mesh(mesh.devices.reshape(2, 2, 4, 2, 4), ("pool", "xh", "y", "core", "head"))
    seq = ("xh", "y", "core")
    every = ("pool",) + seq
    in_specs = (
        P("pool", seq, None),
        P(seq, None, "head"),
        P(seq, None),
        P(None, None, None, "head"),
        P("pool"),
        P(),
        P(every, "head"),
        P(every, None, None, "head"),
        P(every, None, "head"),
        P(every),
        P("pool"),
        P("head", seq),
        P("head", None, None),
        P(None, None, seq),
    )
    out_specs = (P(every, None, None, None, "head"), P(("pool", "head"), seq))
    return jax.shard_map(body, mesh=fine, in_specs=in_specs, out_specs=out_specs, check_vma=False)
```
